128 devices in a mesh: tx: 32 (over y, x, core), ty: 4 (over z).
Axes of the slice: x: 4, y: 4, z: 4, core: 2. Of those that a mesh axis runs over, the one named last changes fastest.
Arguments:
- points: bfloat16 [524288, 128], P(('tx', 'ty')), may hold values from -6 to 6
- embed_weight: bfloat16 [128, 512], replicated, may hold values from -0.5 to 0.5
- inner_weights: bfloat16 [1, 512, 512], replicated, may hold values from -0.25 to 0.25
- output_weight: bfloat16 [512, 128], replicated, may hold values from -0.25 to 0.25
- counts: int32 [128, 512], replicated, may hold values from 1 to 16, as said below
- point_order: int32 [128, 4096], P(('tx', 'ty')), may hold values from 0 to 4095, each once within a row
- inducing: bfloat16 [128, 128], replicated, may hold values from -6 to 6
- first_proj: bfloat16 [4, 128, 128], replicated, may hold values from -0.5 to 0.5
- second_proj: bfloat16 [4, 128, 128], replicated, may hold values from -0.5 to 0.5
- mixing: bfloat16 [8, 128, 128], replicated, may hold values from -0.1875 to 0.1875
Outputs:
- encoded: bfloat16 [524288, 128], P(('tx', 'ty'))
The draws below stay inside these ranges and needn't reach their ends.
Inputs may be any that keep to these rules, and one draw needn't show every extreme that they name: Row s sums to 4096. For every source s and every device, the counts of s in the 4 tiles that device holds sum to exactly 32, and one of those 4 entries equals 16. Row s is a permutation of the local points of source s: the points of tile g are point_order[s, offsets[s, g] + c] for c below counts[s, g].
All inputs are finite; a program needn't handle non-finite values.
Results may differ from the reference program's by a relative error of at most 0.025.
Values may be sent and summed in bfloat16 or wider, within the bound.
A program may use at most 64 MiB of HBM per device.

```python
import jax
import jax.numpy as jnp
from jax import lax

PTS_DEV = 4096
IN = 128
HID = 512
MIDS = 1
C = 128
NI = 128
HEADS = 2
TLX = 2
TLY = 2
GX = 64
GY = 8
TILES = 512
CAP = 16
POINTS = 524288
N_TX = 32
N_TY = 4


def draw_counts(key, part):
    sources = N_TX * N_TY
    quota = PTS_DEV // sources
    spare = quota - CAP - 3
    key_a, key_b, key_c = jax.random.split(jax.random.fold_in(key, 17), 3)
    shape = (sources, N_TX, N_TY)
    cut_a = jax.random.randint(key_a, shape, 0, spare + 1, dtype=jnp.int32)
    cut_b = jax.random.randint(key_b, shape, 0, spare + 1, dtype=jnp.int32)
    lower = jnp.minimum(cut_a, cut_b)
    upper = jnp.maximum(cut_a, cut_b)
    pieces = jnp.stack([1 + lower, 1 + upper - lower, 1 + spare - upper], axis=-1)
    peak = jax.random.randint(key_c, shape, 0, TLX * TLY, dtype=jnp.int32)
    slots = jnp.arange(TLX * TLY, dtype=jnp.int32)
    rank = slots[None, None, None, :] - (slots[None, None, None, :] > peak[..., None]).astype(jnp.int32)
    rank = jnp.clip(rank, 0, 2).astype(jnp.int32)
    picked = jnp.take_along_axis(pieces, rank, axis=-1)
    values = jnp.where(slots[None, None, None, :] == peak[..., None], CAP, picked)
    values = values.reshape(sources, N_TX, N_TY, TLX, TLY).transpose(0, 1, 3, 2, 4)
    return values.reshape(sources, N_TX * TLX * N_TY * TLY).astype(jnp.int32)


def levels(rng, shape, shards, smallest, top_value):
    def one(position, blocks):
        steps = jax.random.uniform(jax.random.fold_in(jax.random.fold_in(rng, 6), position), (blocks,), jnp.float32, smallest / len(shards), top_value / len(shards))
        return jnp.repeat(jnp.exp(steps), shape[position] // blocks).reshape((-1,) + (1,) * (len(shape) - position - 1))

    loudness = one(*shards[0])
    for cut in shards[1:]:
        loudness = loudness * one(*cut)
    return loudness


def noise(stream_key, shape, width, reach, shards=(), held_as=jnp.bfloat16):
    drawn = width * jax.random.normal(stream_key, shape, jnp.float32)
    if shards:
        drawn = drawn * levels(stream_key, shape, shards, -0.22, 0.18)
    return jnp.clip(drawn, -reach, reach).astype(held_as)


def setup_inputs(seed: int = 0) -> dict:
    key_of = jax.random.split(jax.random.key(seed), 11)
    points = noise(key_of[0], (POINTS, IN), 1.0, 6.0, ((0, 128),))
    embed_weight = noise(key_of[1], (IN, HID), IN ** -0.5, 0.5)
    inner_weights = noise(key_of[2], (MIDS, HID, HID), HID ** -0.5, 0.25)
    output_weight = noise(key_of[3], (HID, C), HID ** -0.5, 0.25)
    counts = draw_counts(jax.random.fold_in(key_of[10], 71), 0)
    point_order = jax.vmap(lambda own: jax.random.permutation(own, PTS_DEV))(jax.random.split(key_of[5], (N_TX * N_TY))).reshape((N_TX * N_TY, PTS_DEV)).astype(jnp.int32)
    inducing = noise(key_of[6], (NI, C), 1.0, 6.0)
    first_proj = noise(key_of[7], (4, C, C), C ** -0.5, 0.5)
    second_proj = noise(key_of[8], (4, C, C), C ** -0.5, 0.5)
    mixing = noise(key_of[9], (8, C, C), (8 * C) ** -0.5, 0.1875)
    return dict(points=points, embed_weight=embed_weight, inner_weights=inner_weights, output_weight=output_weight, counts=counts, point_order=point_order, inducing=inducing, first_proj=first_proj, second_proj=second_proj, mixing=mixing)


sharpness = 32.0
epsilon = 1e-06
neighbour_steps = ((-1, -1), (-1, 0), (-1, 1), (0, -1), (0, 1), (1, -1), (1, 0), (1, 1))

def unit_heads(projected, head_count):
    pieces = projected.reshape(projected.shape[:-1] + (head_count, projected.shape[-1] // head_count))
    magnitude = jnp.sqrt(lax.optimization_barrier(jnp.sum(pieces * pieces, axis=-1, keepdims=True)) + epsilon)
    return (pieces / magnitude).reshape(projected.shape).astype(jnp.bfloat16)

def attend(query_rows, key_rows, value_rows, weight_mask, head_count):
    head_width = query_rows.shape[-1] // head_count
    outputs = []
    for head_id in range(head_count):
        lower = head_id * head_width
        upper = lower + head_width
        scores = jnp.dot(query_rows[:, lower:upper], key_rows[:, lower:upper].T, preferred_element_type=jnp.float32)
        weights = jnp.exp(sharpness * scores) * weight_mask[None, :]
        totals = lax.optimization_barrier(jnp.sum(weights, axis=1, keepdims=True))
        numer = jnp.dot(weights.astype(jnp.bfloat16), value_rows[:, lower:upper], preferred_element_type=jnp.float32)
        outputs.append(numer / totals)
    return jnp.concatenate(outputs, axis=1).astype(jnp.bfloat16)

def reference(points, embed_weight, inner_weights, output_weight, counts, point_order, inducing, first_proj, second_proj, mixing):
    devices = N_TX * N_TY
    hidden = jax.nn.silu(jnp.dot(points, embed_weight, preferred_element_type=jnp.float32)).astype(jnp.bfloat16)
    for layer_id in range(MIDS):
        hidden = jax.nn.silu(jnp.dot(hidden, inner_weights[layer_id], preferred_element_type=jnp.float32)).astype(jnp.bfloat16)
    features = jnp.dot(hidden, output_weight, preferred_element_type=jnp.float32).astype(jnp.bfloat16)
    offsets = (jnp.cumsum(counts, axis=1) - counts).astype(jnp.int32)
    slot_ids = jnp.arange(CAP, dtype=jnp.int32)
    sources = jnp.arange(devices, dtype=jnp.int32)

    def tile_input(tile_id):
        starts = lax.dynamic_index_in_dim(offsets, tile_id, 1, keepdims=False)
        tallies = lax.dynamic_index_in_dim(counts, tile_id, 1, keepdims=False)
        filled = slot_ids[None, :] < tallies[:, None]
        positions = jnp.where(filled, starts[:, None] + slot_ids[None, :], 0).astype(jnp.int32)
        local_index = jnp.take_along_axis(point_order, positions, axis=1)
        indices = (local_index + sources[:, None] * PTS_DEV).reshape(-1).astype(jnp.int32)
        filled = filled.reshape(-1)
        picked = jnp.where(filled[:, None], features[indices], jnp.zeros((), jnp.bfloat16))
        return (picked, filled, indices)
    inducing_queries = unit_heads(jnp.dot(inducing, first_proj[0], preferred_element_type=jnp.float32), HEADS)

    def summarize(tile_id):
        picked, filled, unused = tile_input(tile_id)
        key_rows = unit_heads(jnp.dot(picked, first_proj[1], preferred_element_type=jnp.float32), HEADS)
        value_rows = jnp.dot(picked, first_proj[2], preferred_element_type=jnp.float32).astype(jnp.bfloat16)
        attended = attend(inducing_queries, key_rows, value_rows, filled.astype(jnp.float32), HEADS)
        return (inducing.astype(jnp.float32) + jnp.dot(attended, first_proj[3], preferred_element_type=jnp.float32)).astype(jnp.bfloat16)
    summary = lax.map(summarize, jnp.arange(TILES, dtype=jnp.int32)).reshape(GX, GY, NI, C)
    padded = jnp.pad(summary, ((1, 1), (1, 1), (0, 0), (0, 0)))
    mixture = summary.astype(jnp.float32)
    for direction, steps in enumerate(neighbour_steps):
        shifted = padded[1 + steps[0]:1 + steps[0] + GX, 1 + steps[1]:1 + steps[1] + GY].astype(jnp.float32)
        mixture = mixture + jnp.einsum('xyic,ce->xyie', shifted, mixing[direction].astype(jnp.float32))
    mixture = mixture.astype(jnp.bfloat16).reshape(TILES, NI, C)

    def finish(tile_id, encoded):
        picked, filled, indices = tile_input(tile_id)
        mixed_tile = lax.dynamic_index_in_dim(mixture, tile_id, 0, keepdims=False)
        point_queries = unit_heads(jnp.dot(picked, second_proj[0], preferred_element_type=jnp.float32), HEADS)
        key_rows = unit_heads(jnp.dot(mixed_tile, second_proj[1], preferred_element_type=jnp.float32), HEADS)
        value_rows = jnp.dot(mixed_tile, second_proj[2], preferred_element_type=jnp.float32).astype(jnp.bfloat16)
        attended = attend(point_queries, key_rows, value_rows, jnp.ones((NI,), jnp.float32), HEADS)
        result = (picked.astype(jnp.float32) + jnp.dot(attended, second_proj[3], preferred_element_type=jnp.float32)).astype(jnp.bfloat16)
        targets = jnp.where(filled, indices, devices * PTS_DEV).astype(jnp.int32)
        return encoded.at[targets].set(result, mode='drop')
    return lax.fori_loop(0, TILES, finish, jnp.zeros((devices * PTS_DEV, C), jnp.bfloat16))
```

```python
import jax
import jax.numpy as jnp
from jax import lax
from jax.sharding import PartitionSpec as P

HEADS = 2
TLX = 2
TLY = 2


sharpness = 32.0
epsilon = 1e-06
neighbour_steps = ((-1, -1), (-1, 0), (-1, 1), (0, -1), (0, 1), (1, -1), (1, 0), (1, 1))


def padded_2(block, sides, width):
    for axis, dim in sides:
        count = lax.axis_size(axis)
        forward = [(i, i + 1) for i in range(count - 1)]
        backward = [(target, source) for source, target in forward]
        low = lax.ppermute(
            lax.slice_in_dim(block, block.shape[dim] - width, None, axis=dim), axis, forward
        )
        high = lax.ppermute(lax.slice_in_dim(block, 0, width, axis=dim), axis, backward)
        block = jnp.concatenate([low, block, high], axis=dim)
    return block


def unit_heads(projected, head_count):
    pieces = projected.reshape(
        projected.shape[:-1] + (head_count, projected.shape[-1] // head_count)
    )
    magnitude = jnp.sqrt(jnp.sum(pieces * pieces, axis=-1, keepdims=True) + epsilon)
    return (pieces / magnitude).reshape(projected.shape).astype(jnp.bfloat16)


def gather_rows(order, rows, block):
    column_ids = jnp.arange(rows.shape[0], dtype=jnp.int32)

    def pick_block(index_block):
        table = (index_block[:, None] == column_ids[None, :]).astype(jnp.bfloat16)
        return jnp.dot(table, rows, preferred_element_type=jnp.float32).astype(jnp.bfloat16)

    picked = lax.map(pick_block, order.reshape(-1, block))
    return picked.reshape(order.shape[0], rows.shape[1])


def scatter_rows(order, rows, block):
    target_ids = jnp.arange(rows.shape[0], dtype=jnp.int32).reshape(-1, block)

    def place_block(target_block):
        table = (target_block[:, None] == order[None, :]).astype(jnp.bfloat16)
        return jnp.dot(table, rows, preferred_element_type=jnp.float32).astype(jnp.bfloat16)

    placed = lax.map(place_block, target_ids)
    return placed.reshape(rows.shape[0], rows.shape[1])


def body(
    points,
    embed_weight,
    inner_weights,
    output_weight,
    counts,
    point_order,
    inducing,
    first_proj,
    second_proj,
    mixing,
):
    along_x = lax.axis_size("tx")
    along_y = lax.axis_size("ty")
    devices = along_x * along_y
    index_x = lax.axis_index("tx")
    index_y = lax.axis_index("ty")
    own_index = index_x * along_y + index_y
    point_count = points.shape[0]
    per_device = TLX * TLY
    width = output_weight.shape[1]
    quota = point_count // devices
    band = quota * along_y
    head_width = width // HEADS
    inducing_count = inducing.shape[0]

    hidden = jax.nn.silu(jnp.dot(points, embed_weight, preferred_element_type=jnp.float32)).astype(
        jnp.bfloat16
    )
    for layer_id in range(inner_weights.shape[0]):
        hidden = jax.nn.silu(
            jnp.dot(hidden, inner_weights[layer_id], preferred_element_type=jnp.float32)
        ).astype(jnp.bfloat16)
    features = jnp.dot(hidden, output_weight, preferred_element_type=jnp.float32).astype(
        jnp.bfloat16
    )

    own_counts = lax.dynamic_index_in_dim(counts, own_index, 0, keepdims=False)
    own_offsets = jnp.cumsum(own_counts) - own_counts
    grid_counts = own_counts.reshape(along_x, TLX, along_y, TLY)
    grid_offsets = own_offsets.reshape(along_x, TLX, along_y, TLY)
    band_start = grid_offsets[:, 0, 0, 0][:, None]
    first_len = grid_counts[:, 0, :, 0] + grid_counts[:, 0, :, 1]
    first_start = grid_offsets[:, 0, :, 0] - band_start
    second_start = grid_offsets[:, 1, :, 0] - band_start
    slot_ids = jnp.arange(quota, dtype=jnp.int32)
    local_pos = jnp.where(
        slot_ids[None, None, :] < first_len[:, :, None],
        first_start[:, :, None] + slot_ids[None, None, :],
        second_start[:, :, None] + slot_ids[None, None, :] - first_len[:, :, None],
    ).reshape(along_x, band)
    band_ids = jnp.arange(band, dtype=jnp.int32)
    band_table = (local_pos[:, :, None] == band_ids[None, None, :]).astype(jnp.bfloat16)

    order = point_order[0]
    ordered = gather_rows(order, features, 512).reshape(along_x, band, width)
    outgoing = jnp.einsum(
        "xrp,xpe->xre", band_table, ordered, preferred_element_type=jnp.float32
    ).astype(jnp.bfloat16)
    outgoing = outgoing.reshape(devices, quota, width)
    arrived = lax.all_to_all(outgoing, ("tx", "ty"), split_axis=0, concat_axis=0, tiled=True)
    all_rows = arrived.reshape(devices * quota, width)

    inbound = counts.reshape(devices, along_x, TLX, along_y, TLY)
    inbound = lax.dynamic_index_in_dim(inbound, index_x, 1, keepdims=False)
    inbound = lax.dynamic_index_in_dim(inbound, index_y, 2, keepdims=False)
    inbound = inbound.reshape(devices, per_device)
    through = jnp.cumsum(inbound, axis=1)
    row_tile = jnp.sum(
        (slot_ids[None, :, None] >= through[:, None, : per_device - 1]).astype(jnp.int32), axis=2
    ).reshape(-1)
    tile_ids = jnp.arange(per_device, dtype=jnp.int32)
    row_mask = (row_tile[:, None] == tile_ids[None, :]).astype(jnp.float32)

    first_keys = unit_heads(
        jnp.dot(all_rows, first_proj[1], preferred_element_type=jnp.float32), HEADS
    )
    first_values = jnp.dot(all_rows, first_proj[2], preferred_element_type=jnp.float32).astype(
        jnp.bfloat16
    )
    inducing_queries = unit_heads(
        jnp.dot(inducing, first_proj[0], preferred_element_type=jnp.float32), HEADS
    )
    masked_values = first_values[:, None, :] * row_mask.astype(jnp.bfloat16)[:, :, None]
    heads_out = []
    for head_id in range(HEADS):
        lower = head_id * head_width
        upper = lower + head_width
        scores = jnp.dot(
            inducing_queries[:, lower:upper],
            first_keys[:, lower:upper].T,
            preferred_element_type=jnp.float32,
        )
        weights = jnp.exp(sharpness * scores)
        totals = jnp.dot(weights, row_mask, precision=lax.Precision.HIGHEST)
        numer = jnp.dot(
            weights.astype(jnp.bfloat16),
            masked_values[:, :, lower:upper].reshape(-1, per_device * head_width),
            preferred_element_type=jnp.float32,
        ).reshape(inducing_count, per_device, head_width)
        heads_out.append(numer / totals[:, :, None])
    first_attended = (
        jnp.concatenate(heads_out, axis=2).astype(jnp.bfloat16).transpose(1, 0, 2)
    )
    summary = (
        inducing.astype(jnp.float32)[None]
        + jnp.einsum(
            "tic,ce->tie", first_attended, first_proj[3], preferred_element_type=jnp.float32
        )
    ).astype(jnp.bfloat16)
    tile_grid = summary.reshape(TLX, TLY, inducing_count, width)
    padded = padded_2(tile_grid, (("tx", 0), ("ty", 1)), 1)
    stacked = jnp.stack(
        [
            padded[1 + steps[0] : 1 + steps[0] + TLX, 1 + steps[1] : 1 + steps[1] + TLY]
            for steps in neighbour_steps
        ]
    )
    mixture = tile_grid.astype(jnp.float32) + jnp.einsum(
        "dxyic,dce->xyie", stacked, mixing, preferred_element_type=jnp.float32
    )
    mixture = mixture.astype(jnp.bfloat16).reshape(per_device * inducing_count, width)

    point_queries = unit_heads(
        jnp.dot(all_rows, second_proj[0], preferred_element_type=jnp.float32), HEADS
    )
    second_keys = unit_heads(
        jnp.dot(mixture, second_proj[1], preferred_element_type=jnp.float32), HEADS
    )
    second_values = jnp.dot(mixture, second_proj[2], preferred_element_type=jnp.float32).astype(
        jnp.bfloat16
    )
    key_mask = jnp.repeat(row_mask, inducing_count, axis=1)
    heads_out = []
    for head_id in range(HEADS):
        lower = head_id * head_width
        upper = lower + head_width
        scores = jnp.dot(
            point_queries[:, lower:upper],
            second_keys[:, lower:upper].T,
            preferred_element_type=jnp.float32,
        )
        weights = jnp.exp(sharpness * scores) * key_mask
        totals = jnp.sum(weights, axis=1, keepdims=True)
        numer = jnp.dot(
            weights.astype(jnp.bfloat16),
            second_values[:, lower:upper],
            preferred_element_type=jnp.float32,
        )
        heads_out.append(numer / totals)
    second_attended = jnp.concatenate(heads_out, axis=1).astype(jnp.bfloat16)
    result = (
        all_rows.astype(jnp.float32)
        + jnp.dot(second_attended, second_proj[3], preferred_element_type=jnp.float32)
    ).astype(jnp.bfloat16)

    coming = lax.all_to_all(
        result.reshape(devices, quota, width), ("tx", "ty"), split_axis=0, concat_axis=0, tiled=True
    )
    returned = jnp.einsum(
        "xrp,xre->xpe",
        band_table,
        coming.reshape(along_x, band, width),
        preferred_element_type=jnp.float32,
    ).astype(jnp.bfloat16)
    return scatter_rows(order, returned.reshape(point_count, width), 512)


def solution(mesh):
    placed = (P(("tx", "ty"), None), P(), P(), P(), P(), P(("tx", "ty"), None), P(), P(), P(), P())
    return jax.shard_map(
        body, mesh=mesh, in_specs=placed, out_specs=P(("tx", "ty"), None), check_vma=False
    )
```

```python
import functools

import jax
import jax.numpy as jnp
from jax import lax
from jax.experimental import pallas as pl
from jax.experimental.pallas import tpu as pltpu
from jax.sharding import PartitionSpec as P

HEADS = 2
TLX = 2
TLY = 2


sharpness = 32.0
epsilon = 1e-06
neighbour_steps = ((-1, -1), (-1, 0), (-1, 1), (0, -1), (0, 1), (1, -1), (1, 0), (1, 1))


def exchange_kernel(n, ny, x_ref, o_ref, send_sem, recv_sem, local_sem):
    me = lax.axis_index("tx") * ny + lax.axis_index("ty")

    def copy_to(d):
        return pltpu.make_async_remote_copy(
            src_ref=x_ref.at[d], dst_ref=o_ref.at[me], send_sem=send_sem.at[d],
            recv_sem=recv_sem.at[me], device_id=(d // ny, d % ny),
            device_id_type=pl.DeviceIdType.MESH)

    def copy_from(s):
        return pltpu.make_async_remote_copy(
            src_ref=x_ref.at[s], dst_ref=o_ref.at[s], send_sem=send_sem.at[s],
            recv_sem=recv_sem.at[s], device_id=(s // ny, s % ny),
            device_id_type=pl.DeviceIdType.MESH)

    local = pltpu.make_async_copy(x_ref.at[me], o_ref.at[me], local_sem)
    local.start()

    def start(k, carry):
        copy_to(lax.rem(me + k, n)).start()
        return carry
    lax.fori_loop(1, n, start, 0)

    def finish(k, carry):
        copy_to(lax.rem(me + k, n)).wait_send()
        copy_from(lax.rem(me + n - k, n)).wait_recv()
        return carry
    lax.fori_loop(1, n, finish, 0)
    local.wait()

def exchange(x, nx, ny):
    n = nx * ny
    return pl.pallas_call(
        functools.partial(exchange_kernel, n, ny),
        out_shape=jax.ShapeDtypeStruct(x.shape, x.dtype),
        in_specs=[pl.BlockSpec(memory_space=pltpu.VMEM)],
        out_specs=pl.BlockSpec(memory_space=pltpu.VMEM),
        scratch_shapes=[pltpu.SemaphoreType.DMA((n,)), pltpu.SemaphoreType.DMA((n,)), pltpu.SemaphoreType.DMA],
        compiler_params=pltpu.CompilerParams(has_side_effects=True),
    )(x)


def padded_2(block, sides, width):
    for axis, dim in sides:
        count = lax.axis_size(axis)
        forward = [(i, i + 1) for i in range(count - 1)]
        backward = [(target, source) for source, target in forward]
        low = lax.ppermute(
            lax.slice_in_dim(block, block.shape[dim] - width, None, axis=dim), axis, forward
        )
        high = lax.ppermute(lax.slice_in_dim(block, 0, width, axis=dim), axis, backward)
        block = jnp.concatenate([low, block, high], axis=dim)
    return block


def unit_heads(projected, head_count):
    pieces = projected.reshape(
        projected.shape[:-1] + (head_count, projected.shape[-1] // head_count)
    )
    magnitude = jnp.sqrt(jnp.sum(pieces * pieces, axis=-1, keepdims=True) + epsilon)
    return (pieces / magnitude).reshape(projected.shape).astype(jnp.bfloat16)


def gather_rows(order, rows, block):
    column_ids = jnp.arange(rows.shape[0], dtype=jnp.int32)

    def pick_block(index_block):
        table = (index_block[:, None] == column_ids[None, :]).astype(jnp.bfloat16)
        return jnp.dot(table, rows, preferred_element_type=jnp.float32).astype(jnp.bfloat16)

    picked = lax.map(pick_block, order.reshape(-1, block))
    return picked.reshape(order.shape[0], rows.shape[1])


def scatter_rows(order, rows, block):
    target_ids = jnp.arange(rows.shape[0], dtype=jnp.int32).reshape(-1, block)

    def place_block(target_block):
        table = (target_block[:, None] == order[None, :]).astype(jnp.bfloat16)
        return jnp.dot(table, rows, preferred_element_type=jnp.float32).astype(jnp.bfloat16)

    placed = lax.map(place_block, target_ids)
    return placed.reshape(rows.shape[0], rows.shape[1])


def body(
    points,
    embed_weight,
    inner_weights,
    output_weight,
    counts,
    point_order,
    inducing,
    first_proj,
    second_proj,
    mixing,
):
    along_x = lax.axis_size("tx")
    along_y = lax.axis_size("ty")
    devices = along_x * along_y
    index_x = lax.axis_index("tx")
    index_y = lax.axis_index("ty")
    own_index = index_x * along_y + index_y
    point_count = points.shape[0]
    per_device = TLX * TLY
    width = output_weight.shape[1]
    quota = point_count // devices
    band = quota * along_y
    head_width = width // HEADS
    inducing_count = inducing.shape[0]

    hidden = jax.nn.silu(jnp.dot(points, embed_weight, preferred_element_type=jnp.float32)).astype(
        jnp.bfloat16
    )
    for layer_id in range(inner_weights.shape[0]):
        hidden = jax.nn.silu(
            jnp.dot(hidden, inner_weights[layer_id], preferred_element_type=jnp.float32)
        ).astype(jnp.bfloat16)
    features = jnp.dot(hidden, output_weight, preferred_element_type=jnp.float32).astype(
        jnp.bfloat16
    )

    own_counts = lax.dynamic_index_in_dim(counts, own_index, 0, keepdims=False)
    own_offsets = jnp.cumsum(own_counts) - own_counts
    grid_counts = own_counts.reshape(along_x, TLX, along_y, TLY)
    grid_offsets = own_offsets.reshape(along_x, TLX, along_y, TLY)
    band_start = grid_offsets[:, 0, 0, 0][:, None]
    first_len = grid_counts[:, 0, :, 0] + grid_counts[:, 0, :, 1]
    first_start = grid_offsets[:, 0, :, 0] - band_start
    second_start = grid_offsets[:, 1, :, 0] - band_start
    slot_ids = jnp.arange(quota, dtype=jnp.int32)
    local_pos = jnp.where(
        slot_ids[None, None, :] < first_len[:, :, None],
        first_start[:, :, None] + slot_ids[None, None, :],
        second_start[:, :, None] + slot_ids[None, None, :] - first_len[:, :, None],
    ).reshape(along_x, band)
    band_ids = jnp.arange(band, dtype=jnp.int32)
    band_table = (local_pos[:, :, None] == band_ids[None, None, :]).astype(jnp.bfloat16)

    order = point_order[0]
    ordered = gather_rows(order, features, 512).reshape(along_x, band, width)
    outgoing = jnp.einsum(
        "xrp,xpe->xre", band_table, ordered, preferred_element_type=jnp.float32
    ).astype(jnp.bfloat16)
    outgoing = outgoing.reshape(devices, quota, width)
    arrived = exchange(outgoing, along_x, along_y)
    all_rows = arrived.reshape(devices * quota, width)

    inbound = counts.reshape(devices, along_x, TLX, along_y, TLY)
    inbound = lax.dynamic_index_in_dim(inbound, index_x, 1, keepdims=False)
    inbound = lax.dynamic_index_in_dim(inbound, index_y, 2, keepdims=False)
    inbound = inbound.reshape(devices, per_device)
    through = jnp.cumsum(inbound, axis=1)
    row_tile = jnp.sum(
        (slot_ids[None, :, None] >= through[:, None, : per_device - 1]).astype(jnp.int32), axis=2
    ).reshape(-1)
    tile_ids = jnp.arange(per_device, dtype=jnp.int32)
    row_mask = (row_tile[:, None] == tile_ids[None, :]).astype(jnp.float32)

    first_keys = unit_heads(
        jnp.dot(all_rows, first_proj[1], preferred_element_type=jnp.float32), HEADS
    )
    first_values = jnp.dot(all_rows, first_proj[2], preferred_element_type=jnp.float32).astype(
        jnp.bfloat16
    )
    inducing_queries = unit_heads(
        jnp.dot(inducing, first_proj[0], preferred_element_type=jnp.float32), HEADS
    )
    masked_values = first_values[:, None, :] * row_mask.astype(jnp.bfloat16)[:, :, None]
    heads_out = []
    for head_id in range(HEADS):
        lower = head_id * head_width
        upper = lower + head_width
        scores = jnp.dot(
            inducing_queries[:, lower:upper],
            first_keys[:, lower:upper].T,
            preferred_element_type=jnp.float32,
        )
        weights = jnp.exp(sharpness * scores)
        totals = jnp.dot(weights, row_mask, precision=lax.Precision.HIGHEST)
        numer = jnp.dot(
            weights.astype(jnp.bfloat16),
            masked_values[:, :, lower:upper].reshape(-1, per_device * head_width),
            preferred_element_type=jnp.float32,
        ).reshape(inducing_count, per_device, head_width)
        heads_out.append(numer / totals[:, :, None])
    first_attended = (
        jnp.concatenate(heads_out, axis=2).astype(jnp.bfloat16).transpose(1, 0, 2)
    )
    summary = (
        inducing.astype(jnp.float32)[None]
        + jnp.einsum(
            "tic,ce->tie", first_attended, first_proj[3], preferred_element_type=jnp.float32
        )
    ).astype(jnp.bfloat16)
    tile_grid = summary.reshape(TLX, TLY, inducing_count, width)
    padded = padded_2(tile_grid, (("tx", 0), ("ty", 1)), 1)
    stacked = jnp.stack(
        [
            padded[1 + steps[0] : 1 + steps[0] + TLX, 1 + steps[1] : 1 + steps[1] + TLY]
            for steps in neighbour_steps
        ]
    )
    mixture = tile_grid.astype(jnp.float32) + jnp.einsum(
        "dxyic,dce->xyie", stacked, mixing, preferred_element_type=jnp.float32
    )
    mixture = mixture.astype(jnp.bfloat16).reshape(per_device * inducing_count, width)

    point_queries = unit_heads(
        jnp.dot(all_rows, second_proj[0], preferred_element_type=jnp.float32), HEADS
    )
    second_keys = unit_heads(
        jnp.dot(mixture, second_proj[1], preferred_element_type=jnp.float32), HEADS
    )
    second_values = jnp.dot(mixture, second_proj[2], preferred_element_type=jnp.float32).astype(
        jnp.bfloat16
    )
    key_mask = jnp.repeat(row_mask, inducing_count, axis=1)
    heads_out = []
    for head_id in range(HEADS):
        lower = head_id * head_width
        upper = lower + head_width
        scores = jnp.dot(
            point_queries[:, lower:upper],
            second_keys[:, lower:upper].T,
            preferred_element_type=jnp.float32,
        )
        weights = jnp.exp(sharpness * scores) * key_mask
        totals = jnp.sum(weights, axis=1, keepdims=True)
        numer = jnp.dot(
            weights.astype(jnp.bfloat16),
            second_values[:, lower:upper],
            preferred_element_type=jnp.float32,
        )
        heads_out.append(numer / totals)
    second_attended = jnp.concatenate(heads_out, axis=1).astype(jnp.bfloat16)
    result = (
        all_rows.astype(jnp.float32)
        + jnp.dot(second_attended, second_proj[3], preferred_element_type=jnp.float32)
    ).astype(jnp.bfloat16)

    coming = exchange(result.reshape(devices, quota, width), along_x, along_y)
    returned = jnp.einsum(
        "xrp,xre->xpe",
        band_table,
        coming.reshape(along_x, band, width),
        preferred_element_type=jnp.float32,
    ).astype(jnp.bfloat16)
    return scatter_rows(order, returned.reshape(point_count, width), 512)


def solution(mesh):
    placed = (P(("tx", "ty"), None), P(), P(), P(), P(), P(("tx", "ty"), None), P(), P(), P(), P())
    return jax.shard_map(
        body, mesh=mesh, in_specs=placed, out_specs=P(("tx", "ty"), None), check_vma=False
    )
```

```python
import functools

import jax
import jax.numpy as jnp
from jax import lax
from jax.experimental import pallas as pl
from jax.experimental.pallas import tpu as pltpu
from jax.sharding import PartitionSpec as P

HEADS = 2
TLX = 2
TLY = 2


sharpness = 32.0
epsilon = 1e-06
neighbour_steps = ((-1, -1), (-1, 0), (-1, 1), (0, -1), (0, 1), (1, -1), (1, 0), (1, 1))


def exchange_kernel(n, ny, x_ref, o_ref, send_sem, recv_sem, local_sem):
    me = lax.axis_index("tx") * ny + lax.axis_index("ty")

    def copy_to(d):
        return pltpu.make_async_remote_copy(
            src_ref=x_ref.at[d], dst_ref=o_ref.at[me], send_sem=send_sem.at[d],
            recv_sem=recv_sem.at[me], device_id=(d // ny, d % ny),
            device_id_type=pl.DeviceIdType.MESH)

    def copy_from(s):
        return pltpu.make_async_remote_copy(
            src_ref=x_ref.at[s], dst_ref=o_ref.at[s], send_sem=send_sem.at[s],
            recv_sem=recv_sem.at[s], device_id=(s // ny, s % ny),
            device_id_type=pl.DeviceIdType.MESH)

    local = pltpu.make_async_copy(x_ref.at[me], o_ref.at[me], local_sem)
    local.start()

    def start(k, carry):
        copy_to(lax.rem(me + k, n)).start()
        return carry
    lax.fori_loop(1, n, start, 0)

    def finish(k, carry):
        copy_to(lax.rem(me + k, n)).wait_send()
        copy_from(lax.rem(me + n - k, n)).wait_recv()
        return carry
    lax.fori_loop(1, n, finish, 0)
    local.wait()

def exchange(x, nx, ny):
    n = nx * ny
    return pl.pallas_call(
        functools.partial(exchange_kernel, n, ny),
        out_shape=jax.ShapeDtypeStruct(x.shape, x.dtype),
        in_specs=[pl.BlockSpec(memory_space=pltpu.VMEM)],
        out_specs=pl.BlockSpec(memory_space=pltpu.VMEM),
        scratch_shapes=[pltpu.SemaphoreType.DMA((n,)), pltpu.SemaphoreType.DMA((n,)), pltpu.SemaphoreType.DMA],
        compiler_params=pltpu.CompilerParams(has_side_effects=True),
    )(x)


def mlp_kernel(x_ref, w1_ref, w2_ref, w3_ref, o_ref):
    def silu(v):
        return v / (1.0 + jnp.exp(-v))

    h = silu(jnp.dot(x_ref[...], w1_ref[...], preferred_element_type=jnp.float32))
    h = h.astype(jnp.bfloat16)
    for layer_id in range(w2_ref.shape[0]):
        h = silu(jnp.dot(h, w2_ref[layer_id], preferred_element_type=jnp.float32))
        h = h.astype(jnp.bfloat16)
    o_ref[...] = jnp.dot(h, w3_ref[...], preferred_element_type=jnp.float32).astype(o_ref.dtype)


def point_mlp(x, w1, w2, w3, block):
    rows = x.shape[0]
    full = lambda shape: pl.BlockSpec(shape, lambda i: (0,) * len(shape))
    return pl.pallas_call(
        mlp_kernel,
        out_shape=jax.ShapeDtypeStruct((rows, w3.shape[1]), jnp.bfloat16),
        grid=(rows // block,),
        in_specs=[
            pl.BlockSpec((block, x.shape[1]), lambda i: (i, 0)),
            full(w1.shape),
            full(w2.shape),
            full(w3.shape),
        ],
        out_specs=pl.BlockSpec((block, w3.shape[1]), lambda i: (i, 0)),
    )(x, w1, w2, w3)


def permute_kernel(chunk, a_ref, b_ref, x_ref, o_ref):
    total = jnp.zeros(o_ref.shape, jnp.float32)
    keys = a_ref[...]
    for start in range(0, x_ref.shape[0], chunk):
        hits = (keys == b_ref[:, start : start + chunk]).astype(jnp.bfloat16)
        total += jnp.dot(hits, x_ref[start : start + chunk, :], preferred_element_type=jnp.float32)
    o_ref[...] = total.astype(o_ref.dtype)


def permute_rows(a, b, x, block, chunk):
    rows = a.shape[0]
    a = a.reshape(rows, 1)
    b = b.reshape(1, -1)
    return pl.pallas_call(
        functools.partial(permute_kernel, chunk),
        out_shape=jax.ShapeDtypeStruct((rows, x.shape[1]), x.dtype),
        grid=(rows // block,),
        in_specs=[
            pl.BlockSpec((block, 1), lambda i: (i, 0)),
            pl.BlockSpec(b.shape, lambda i: (0, 0)),
            pl.BlockSpec(x.shape, lambda i: (0, 0)),
        ],
        out_specs=pl.BlockSpec((block, x.shape[1]), lambda i: (i, 0)),
    )(a, b, x)


def padded_2(block, sides, width):
    for axis, dim in sides:
        count = lax.axis_size(axis)
        forward = [(i, i + 1) for i in range(count - 1)]
        backward = [(target, source) for source, target in forward]
        low = lax.ppermute(
            lax.slice_in_dim(block, block.shape[dim] - width, None, axis=dim), axis, forward
        )
        high = lax.ppermute(lax.slice_in_dim(block, 0, width, axis=dim), axis, backward)
        block = jnp.concatenate([low, block, high], axis=dim)
    return block


def unit_heads(projected, head_count):
    pieces = projected.reshape(
        projected.shape[:-1] + (head_count, projected.shape[-1] // head_count)
    )
    magnitude = jnp.sqrt(jnp.sum(pieces * pieces, axis=-1, keepdims=True) + epsilon)
    return (pieces / magnitude).reshape(projected.shape).astype(jnp.bfloat16)


def gather_rows(order, rows, block):
    column_ids = jnp.arange(rows.shape[0], dtype=jnp.int32)

    def pick_block(index_block):
        table = (index_block[:, None] == column_ids[None, :]).astype(jnp.bfloat16)
        return jnp.dot(table, rows, preferred_element_type=jnp.float32).astype(jnp.bfloat16)

    picked = lax.map(pick_block, order.reshape(-1, block))
    return picked.reshape(order.shape[0], rows.shape[1])


def scatter_rows(order, rows, block):
    target_ids = jnp.arange(rows.shape[0], dtype=jnp.int32).reshape(-1, block)

    def place_block(target_block):
        table = (target_block[:, None] == order[None, :]).astype(jnp.bfloat16)
        return jnp.dot(table, rows, preferred_element_type=jnp.float32).astype(jnp.bfloat16)

    placed = lax.map(place_block, target_ids)
    return placed.reshape(rows.shape[0], rows.shape[1])


def body(
    points,
    embed_weight,
    inner_weights,
    output_weight,
    counts,
    point_order,
    inducing,
    first_proj,
    second_proj,
    mixing,
):
    along_x = lax.axis_size("tx")
    along_y = lax.axis_size("ty")
    devices = along_x * along_y
    index_x = lax.axis_index("tx")
    index_y = lax.axis_index("ty")
    own_index = index_x * along_y + index_y
    point_count = points.shape[0]
    per_device = TLX * TLY
    width = output_weight.shape[1]
    quota = point_count // devices
    band = quota * along_y
    head_width = width // HEADS
    inducing_count = inducing.shape[0]

    features = point_mlp(points, embed_weight, inner_weights, output_weight, 512)

    own_counts = lax.dynamic_index_in_dim(counts, own_index, 0, keepdims=False)
    own_offsets = jnp.cumsum(own_counts) - own_counts
    grid_counts = own_counts.reshape(along_x, TLX, along_y, TLY)
    grid_offsets = own_offsets.reshape(along_x, TLX, along_y, TLY)
    band_start = grid_offsets[:, 0, 0, 0][:, None]
    first_len = grid_counts[:, 0, :, 0] + grid_counts[:, 0, :, 1]
    first_start = grid_offsets[:, 0, :, 0] - band_start
    second_start = grid_offsets[:, 1, :, 0] - band_start
    slot_ids = jnp.arange(quota, dtype=jnp.int32)
    local_pos = jnp.where(
        slot_ids[None, None, :] < first_len[:, :, None],
        first_start[:, :, None] + slot_ids[None, None, :],
        second_start[:, :, None] + slot_ids[None, None, :] - first_len[:, :, None],
    ).reshape(along_x, band)
    band_ids = jnp.arange(band, dtype=jnp.int32)
    band_table = (local_pos[:, :, None] == band_ids[None, None, :]).astype(jnp.bfloat16)

    order = point_order[0]
    ordered = permute_rows(order, jnp.arange(point_count, dtype=jnp.int32), features, 256, 512).reshape(along_x, band, width)
    outgoing = jnp.einsum(
        "xrp,xpe->xre", band_table, ordered, preferred_element_type=jnp.float32
    ).astype(jnp.bfloat16)
    outgoing = outgoing.reshape(devices, quota, width)
    arrived = lax.all_to_all(outgoing, ("tx", "ty"), split_axis=0, concat_axis=0, tiled=True)
    all_rows = arrived.reshape(devices * quota, width)

    inbound = counts.reshape(devices, along_x, TLX, along_y, TLY)
    inbound = lax.dynamic_index_in_dim(inbound, index_x, 1, keepdims=False)
    inbound = lax.dynamic_index_in_dim(inbound, index_y, 2, keepdims=False)
    inbound = inbound.reshape(devices, per_device)
    through = jnp.cumsum(inbound, axis=1)
    row_tile = jnp.sum(
        (slot_ids[None, :, None] >= through[:, None, : per_device - 1]).astype(jnp.int32), axis=2
    ).reshape(-1)
    tile_ids = jnp.arange(per_device, dtype=jnp.int32)
    row_mask = (row_tile[:, None] == tile_ids[None, :]).astype(jnp.float32)

    first_keys = unit_heads(
        jnp.dot(all_rows, first_proj[1], preferred_element_type=jnp.float32), HEADS
    )
    first_values = jnp.dot(all_rows, first_proj[2], preferred_element_type=jnp.float32).astype(
        jnp.bfloat16
    )
    inducing_queries = unit_heads(
        jnp.dot(inducing, first_proj[0], preferred_element_type=jnp.float32), HEADS
    )
    masked_values = first_values[:, None, :] * row_mask.astype(jnp.bfloat16)[:, :, None]
    heads_out = []
    for head_id in range(HEADS):
        lower = head_id * head_width
        upper = lower + head_width
        scores = jnp.dot(
            inducing_queries[:, lower:upper],
            first_keys[:, lower:upper].T,
            preferred_element_type=jnp.float32,
        )
        weights = jnp.exp(sharpness * scores)
        totals = jnp.dot(weights, row_mask, precision=lax.Precision.HIGHEST)
        numer = jnp.dot(
            weights.astype(jnp.bfloat16),
            masked_values[:, :, lower:upper].reshape(-1, per_device * head_width),
            preferred_element_type=jnp.float32,
        ).reshape(inducing_count, per_device, head_width)
        heads_out.append(numer / totals[:, :, None])
    first_attended = (
        jnp.concatenate(heads_out, axis=2).astype(jnp.bfloat16).transpose(1, 0, 2)
    )
    summary = (
        inducing.astype(jnp.float32)[None]
        + jnp.einsum(
            "tic,ce->tie", first_attended, first_proj[3], preferred_element_type=jnp.float32
        )
    ).astype(jnp.bfloat16)
    tile_grid = summary.reshape(TLX, TLY, inducing_count, width)
    padded = padded_2(tile_grid, (("tx", 0), ("ty", 1)), 1)
    stacked = jnp.stack(
        [
            padded[1 + steps[0] : 1 + steps[0] + TLX, 1 + steps[1] : 1 + steps[1] + TLY]
            for steps in neighbour_steps
        ]
    )
    mixture = tile_grid.astype(jnp.float32) + jnp.einsum(
        "dxyic,dce->xyie", stacked, mixing, preferred_element_type=jnp.float32
    )
    mixture = mixture.astype(jnp.bfloat16).reshape(per_device * inducing_count, width)

    point_queries = unit_heads(
        jnp.dot(all_rows, second_proj[0], preferred_element_type=jnp.float32), HEADS
    )
    second_keys = unit_heads(
        jnp.dot(mixture, second_proj[1], preferred_element_type=jnp.float32), HEADS
    )
    second_values = jnp.dot(mixture, second_proj[2], preferred_element_type=jnp.float32).astype(
        jnp.bfloat16
    )
    key_mask = jnp.repeat(row_mask, inducing_count, axis=1)
    heads_out = []
    for head_id in range(HEADS):
        lower = head_id * head_width
        upper = lower + head_width
        scores = jnp.dot(
            point_queries[:, lower:upper],
            second_keys[:, lower:upper].T,
            preferred_element_type=jnp.float32,
        )
        weights = jnp.exp(sharpness * scores) * key_mask
        totals = jnp.sum(weights, axis=1, keepdims=True)
        numer = jnp.dot(
            weights.astype(jnp.bfloat16),
            second_values[:, lower:upper],
            preferred_element_type=jnp.float32,
        )
        heads_out.append(numer / totals)
    second_attended = jnp.concatenate(heads_out, axis=1).astype(jnp.bfloat16)
    result = (
        all_rows.astype(jnp.float32)
        + jnp.dot(second_attended, second_proj[3], preferred_element_type=jnp.float32)
    ).astype(jnp.bfloat16)

    coming = lax.all_to_all(
        result.reshape(devices, quota, width), ("tx", "ty"), split_axis=0, concat_axis=0, tiled=True
    )
    returned = jnp.einsum(
        "xrp,xre->xpe",
        band_table,
        coming.reshape(along_x, band, width),
        preferred_element_type=jnp.float32,
    ).astype(jnp.bfloat16)
    return permute_rows(
        jnp.arange(point_count, dtype=jnp.int32), order, returned.reshape(point_count, width), 256, 512
    )


def solution(mesh):
    placed = (P(("tx", "ty"), None), P(), P(), P(), P(), P(("tx", "ty"), None), P(), P(), P(), P())
    return jax.shard_map(
        body, mesh=mesh, in_specs=placed, out_specs=P(("tx", "ty"), None), check_vma=False
    )
```

```python
import functools

import jax
import jax.numpy as jnp
from jax import lax
from jax.experimental import pallas as pl
from jax.experimental.pallas import tpu as pltpu
from jax.sharding import PartitionSpec as P

HEADS = 2
TLX = 2
TLY = 2


sharpness = 32.0
epsilon = 1e-06
neighbour_steps = ((-1, -1), (-1, 0), (-1, 1), (0, -1), (0, 1), (1, -1), (1, 0), (1, 1))


def exchange_kernel(n, ny, x_ref, o_ref, send_sem, recv_sem, local_sem):
    me = lax.axis_index("tx") * ny + lax.axis_index("ty")

    def copy_to(d):
        return pltpu.make_async_remote_copy(
            src_ref=x_ref.at[d], dst_ref=o_ref.at[me], send_sem=send_sem.at[d],
            recv_sem=recv_sem.at[me], device_id=(d // ny, d % ny),
            device_id_type=pl.DeviceIdType.MESH)

    def copy_from(s):
        return pltpu.make_async_remote_copy(
            src_ref=x_ref.at[s], dst_ref=o_ref.at[s], send_sem=send_sem.at[s],
            recv_sem=recv_sem.at[s], device_id=(s // ny, s % ny),
            device_id_type=pl.DeviceIdType.MESH)

    local = pltpu.make_async_copy(x_ref.at[me], o_ref.at[me], local_sem)
    local.start()

    def start(k, carry):
        copy_to(lax.rem(me + k, n)).start()
        return carry
    lax.fori_loop(1, n, start, 0)

    def finish(k, carry):
        copy_to(lax.rem(me + k, n)).wait_send()
        copy_from(lax.rem(me + n - k, n)).wait_recv()
        return carry
    lax.fori_loop(1, n, finish, 0)
    local.wait()

def exchange(x, nx, ny):
    n = nx * ny
    return pl.pallas_call(
        functools.partial(exchange_kernel, n, ny),
        out_shape=jax.ShapeDtypeStruct(x.shape, x.dtype),
        in_specs=[pl.BlockSpec(memory_space=pltpu.VMEM)],
        out_specs=pl.BlockSpec(memory_space=pltpu.VMEM),
        scratch_shapes=[pltpu.SemaphoreType.DMA((n,)), pltpu.SemaphoreType.DMA((n,)), pltpu.SemaphoreType.DMA],
        compiler_params=pltpu.CompilerParams(has_side_effects=True),
    )(x)


def mlp_kernel(x_ref, w1_ref, w2_ref, w3_ref, o_ref):
    def silu(v):
        return v / (1.0 + jnp.exp(-v))

    h = silu(jnp.dot(x_ref[...], w1_ref[...], preferred_element_type=jnp.float32))
    h = h.astype(jnp.bfloat16)
    for layer_id in range(w2_ref.shape[0]):
        h = silu(jnp.dot(h, w2_ref[layer_id], preferred_element_type=jnp.float32))
        h = h.astype(jnp.bfloat16)
    o_ref[...] = jnp.dot(h, w3_ref[...], preferred_element_type=jnp.float32).astype(o_ref.dtype)


def point_mlp(x, w1, w2, w3, block):
    rows = x.shape[0]
    full = lambda shape: pl.BlockSpec(shape, lambda i: (0,) * len(shape))
    return pl.pallas_call(
        mlp_kernel,
        out_shape=jax.ShapeDtypeStruct((rows, w3.shape[1]), jnp.bfloat16),
        grid=(rows // block,),
        in_specs=[
            pl.BlockSpec((block, x.shape[1]), lambda i: (i, 0)),
            full(w1.shape),
            full(w2.shape),
            full(w3.shape),
        ],
        out_specs=pl.BlockSpec((block, w3.shape[1]), lambda i: (i, 0)),
    )(x, w1, w2, w3)


def permute_kernel(chunk, a_ref, b_ref, x_ref, o_ref):
    total = jnp.zeros(o_ref.shape, jnp.float32)
    keys = a_ref[...]
    for start in range(0, x_ref.shape[0], chunk):
        hits = (keys == b_ref[:, start : start + chunk]).astype(jnp.bfloat16)
        total += jnp.dot(hits, x_ref[start : start + chunk, :], preferred_element_type=jnp.float32)
    o_ref[...] = total.astype(o_ref.dtype)


def permute_rows(a, b, x, block, chunk):
    rows = a.shape[0]
    a = a.reshape(rows, 1)
    b = b.reshape(1, -1)
    return pl.pallas_call(
        functools.partial(permute_kernel, chunk),
        out_shape=jax.ShapeDtypeStruct((rows, x.shape[1]), x.dtype),
        grid=(rows // block,),
        in_specs=[
            pl.BlockSpec((block, 1), lambda i: (i, 0)),
            pl.BlockSpec(b.shape, lambda i: (0, 0)),
            pl.BlockSpec(x.shape, lambda i: (0, 0)),
        ],
        out_specs=pl.BlockSpec((block, x.shape[1]), lambda i: (i, 0)),
    )(a, b, x)


def gather_kernel(unroll, pos_ref, order_ref, x_ref, o_ref):
    def body(step, carry):
        for lane in range(unroll):
            row = step * unroll + lane
            source = order_ref[pos_ref[row]]
            o_ref[pl.ds(row, 1), :] = x_ref[pl.ds(source, 1), :]
        return carry

    lax.fori_loop(0, o_ref.shape[0] // unroll, body, 0)


def scatter_kernel(unroll, pos_ref, order_ref, x_ref, o_ref):
    def body(step, carry):
        for lane in range(unroll):
            row = step * unroll + lane
            target = order_ref[pos_ref[row]]
            o_ref[pl.ds(target, 1), :] = x_ref[pl.ds(row, 1), :]
        return carry

    lax.fori_loop(0, x_ref.shape[0] // unroll, body, 0)


def move_rows(kernel, pos, order, x):
    return pl.pallas_call(
        functools.partial(kernel, 8),
        out_shape=jax.ShapeDtypeStruct(x.shape, x.dtype),
        in_specs=[
            pl.BlockSpec(memory_space=pltpu.SMEM),
            pl.BlockSpec(memory_space=pltpu.SMEM),
            pl.BlockSpec(memory_space=pltpu.VMEM),
        ],
        out_specs=pl.BlockSpec(memory_space=pltpu.VMEM),
    )(pos, order, x)


def halo(block):
    count_x = lax.axis_size("tx")
    count_y = lax.axis_size("ty")

    def shift(piece, step_x, step_y):
        pairs = []
        for source_x in range(count_x):
            for source_y in range(count_y):
                target_x = source_x + step_x
                target_y = source_y + step_y
                if 0 <= target_x < count_x and 0 <= target_y < count_y:
                    pairs.append((source_x * count_y + source_y, target_x * count_y + target_y))
        return lax.ppermute(piece, ("tx", "ty"), pairs)

    last_x, last_y = block.shape[0] - 1, block.shape[1] - 1
    low_x = shift(block[last_x:], 1, 0)
    high_x = shift(block[:1], -1, 0)
    low_y = shift(block[:, last_y:], 0, 1)
    high_y = shift(block[:, :1], 0, -1)
    low_low = shift(block[last_x:, last_y:], 1, 1)
    low_high = shift(block[last_x:, :1], 1, -1)
    high_low = shift(block[:1, last_y:], -1, 1)
    high_high = shift(block[:1, :1], -1, -1)
    top = jnp.concatenate([low_low, low_x, low_high], axis=1)
    middle = jnp.concatenate([low_y, block, high_y], axis=1)
    bottom = jnp.concatenate([high_low, high_x, high_high], axis=1)
    return jnp.concatenate([top, middle, bottom], axis=0)


def padded_2(block, sides, width):
    for axis, dim in sides:
        count = lax.axis_size(axis)
        forward = [(i, i + 1) for i in range(count - 1)]
        backward = [(target, source) for source, target in forward]
        low = lax.ppermute(
            lax.slice_in_dim(block, block.shape[dim] - width, None, axis=dim), axis, forward
        )
        high = lax.ppermute(lax.slice_in_dim(block, 0, width, axis=dim), axis, backward)
        block = jnp.concatenate([low, block, high], axis=dim)
    return block


def unit_heads(projected, head_count):
    pieces = projected.reshape(
        projected.shape[:-1] + (head_count, projected.shape[-1] // head_count)
    )
    magnitude = jnp.sqrt(jnp.sum(pieces * pieces, axis=-1, keepdims=True) + epsilon)
    return (pieces / magnitude).reshape(projected.shape).astype(jnp.bfloat16)


def gather_rows(order, rows, block):
    column_ids = jnp.arange(rows.shape[0], dtype=jnp.int32)

    def pick_block(index_block):
        table = (index_block[:, None] == column_ids[None, :]).astype(jnp.bfloat16)
        return jnp.dot(table, rows, preferred_element_type=jnp.float32).astype(jnp.bfloat16)

    picked = lax.map(pick_block, order.reshape(-1, block))
    return picked.reshape(order.shape[0], rows.shape[1])


def scatter_rows(order, rows, block):
    target_ids = jnp.arange(rows.shape[0], dtype=jnp.int32).reshape(-1, block)

    def place_block(target_block):
        table = (target_block[:, None] == order[None, :]).astype(jnp.bfloat16)
        return jnp.dot(table, rows, preferred_element_type=jnp.float32).astype(jnp.bfloat16)

    placed = lax.map(place_block, target_ids)
    return placed.reshape(rows.shape[0], rows.shape[1])


def body(
    points,
    embed_weight,
    inner_weights,
    output_weight,
    counts,
    point_order,
    inducing,
    first_proj,
    second_proj,
    mixing,
):
    along_x = lax.axis_size("tx")
    along_y = lax.axis_size("ty")
    devices = along_x * along_y
    index_x = lax.axis_index("tx")
    index_y = lax.axis_index("ty")
    own_index = index_x * along_y + index_y
    point_count = points.shape[0]
    per_device = TLX * TLY
    width = output_weight.shape[1]
    quota = point_count // devices
    band = quota * along_y
    head_width = width // HEADS
    inducing_count = inducing.shape[0]

    features = point_mlp(points, embed_weight, inner_weights, output_weight, 512)

    own_counts = lax.dynamic_index_in_dim(counts, own_index, 0, keepdims=False)
    own_offsets = jnp.cumsum(own_counts) - own_counts
    grid_counts = own_counts.reshape(along_x, TLX, along_y, TLY)
    grid_offsets = own_offsets.reshape(along_x, TLX, along_y, TLY)
    band_start = grid_offsets[:, 0, 0, 0][:, None]
    first_len = grid_counts[:, 0, :, 0] + grid_counts[:, 0, :, 1]
    first_start = grid_offsets[:, 0, :, 0] - band_start
    second_start = grid_offsets[:, 1, :, 0] - band_start
    slot_ids = jnp.arange(quota, dtype=jnp.int32)
    local_pos = jnp.where(
        slot_ids[None, None, :] < first_len[:, :, None],
        first_start[:, :, None] + slot_ids[None, None, :],
        second_start[:, :, None] + slot_ids[None, None, :] - first_len[:, :, None],
    ).reshape(along_x, band)
    send_pos = (local_pos + band_start).reshape(-1)
    order = point_order[0]
    outgoing = move_rows(gather_kernel, send_pos, order, features.astype(jnp.float32))
    outgoing = outgoing.astype(jnp.bfloat16)
    outgoing = outgoing.reshape(devices, quota, width)
    arrived = lax.all_to_all(outgoing, ("tx", "ty"), split_axis=0, concat_axis=0, tiled=True)
    all_rows = arrived.reshape(devices * quota, width)

    inbound = counts.reshape(devices, along_x, TLX, along_y, TLY)
    inbound = lax.dynamic_index_in_dim(inbound, index_x, 1, keepdims=False)
    inbound = lax.dynamic_index_in_dim(inbound, index_y, 2, keepdims=False)
    inbound = inbound.reshape(devices, per_device)
    through = jnp.cumsum(inbound, axis=1)
    row_tile = jnp.sum(
        (slot_ids[None, :, None] >= through[:, None, : per_device - 1]).astype(jnp.int32), axis=2
    ).reshape(-1)
    tile_ids = jnp.arange(per_device, dtype=jnp.int32)
    row_mask = (row_tile[:, None] == tile_ids[None, :]).astype(jnp.float32)

    first_keys = unit_heads(
        jnp.dot(all_rows, first_proj[1], preferred_element_type=jnp.float32), HEADS
    )
    first_values = jnp.dot(all_rows, first_proj[2], preferred_element_type=jnp.float32).astype(
        jnp.bfloat16
    )
    inducing_queries = unit_heads(
        jnp.dot(inducing, first_proj[0], preferred_element_type=jnp.float32), HEADS
    )
    masked_values = first_values[:, None, :] * row_mask.astype(jnp.bfloat16)[:, :, None]
    heads_out = []
    for head_id in range(HEADS):
        lower = head_id * head_width
        upper = lower + head_width
        scores = jnp.dot(
            inducing_queries[:, lower:upper],
            first_keys[:, lower:upper].T,
            preferred_element_type=jnp.float32,
        )
        weights = jnp.exp(sharpness * scores)
        totals = jnp.dot(weights, row_mask, precision=lax.Precision.HIGHEST)
        numer = jnp.dot(
            weights.astype(jnp.bfloat16),
            masked_values[:, :, lower:upper].reshape(-1, per_device * head_width),
            preferred_element_type=jnp.float32,
        ).reshape(inducing_count, per_device, head_width)
        heads_out.append(numer / totals[:, :, None])
    first_attended = (
        jnp.concatenate(heads_out, axis=2).astype(jnp.bfloat16).transpose(1, 0, 2)
    )
    summary = (
        inducing.astype(jnp.float32)[None]
        + jnp.einsum(
            "tic,ce->tie", first_attended, first_proj[3], preferred_element_type=jnp.float32
        )
    ).astype(jnp.bfloat16)
    tile_grid = summary.reshape(TLX, TLY, inducing_count, width)
    padded = halo(tile_grid)
    stacked = jnp.stack(
        [
            padded[1 + steps[0] : 1 + steps[0] + TLX, 1 + steps[1] : 1 + steps[1] + TLY]
            for steps in neighbour_steps
        ]
    )
    mixture = tile_grid.astype(jnp.float32) + jnp.einsum(
        "dxyic,dce->xyie", stacked, mixing, preferred_element_type=jnp.float32
    )
    mixture = mixture.astype(jnp.bfloat16).reshape(per_device * inducing_count, width)

    point_queries = unit_heads(
        jnp.dot(all_rows, second_proj[0], preferred_element_type=jnp.float32), HEADS
    )
    second_keys = unit_heads(
        jnp.dot(mixture, second_proj[1], preferred_element_type=jnp.float32), HEADS
    )
    second_values = jnp.dot(mixture, second_proj[2], preferred_element_type=jnp.float32).astype(
        jnp.bfloat16
    )
    key_mask = jnp.repeat(row_mask, inducing_count, axis=1)
    heads_out = []
    for head_id in range(HEADS):
        lower = head_id * head_width
        upper = lower + head_width
        scores = jnp.dot(
            point_queries[:, lower:upper],
            second_keys[:, lower:upper].T,
            preferred_element_type=jnp.float32,
        )
        weights = jnp.exp(sharpness * scores) * key_mask
        totals = jnp.sum(weights, axis=1, keepdims=True)
        numer = jnp.dot(
            weights.astype(jnp.bfloat16),
            second_values[:, lower:upper],
            preferred_element_type=jnp.float32,
        )
        heads_out.append(numer / totals)
    second_attended = jnp.concatenate(heads_out, axis=1).astype(jnp.bfloat16)
    result = (
        all_rows.astype(jnp.float32)
        + jnp.dot(second_attended, second_proj[3], preferred_element_type=jnp.float32)
    ).astype(jnp.bfloat16)

    coming = lax.all_to_all(
        result.reshape(devices, quota, width), ("tx", "ty"), split_axis=0, concat_axis=0, tiled=True
    )
    returned = move_rows(
        scatter_kernel, send_pos, order, coming.reshape(point_count, width).astype(jnp.float32)
    )
    return returned.astype(jnp.bfloat16)


def solution(mesh):
    placed = (P(("tx", "ty"), None), P(), P(), P(), P(), P(("tx", "ty"), None), P(), P(), P(), P())
    return jax.shard_map(
        body, mesh=mesh, in_specs=placed, out_specs=P(("tx", "ty"), None), check_vma=False
    )
```

```python
import functools

import jax
import jax.numpy as jnp
from jax import lax
from jax.experimental import pallas as pl
from jax.experimental.pallas import tpu as pltpu
from jax.sharding import PartitionSpec as P

HEADS = 2
TLX = 2
TLY = 2


sharpness = 32.0
epsilon = 1e-06
neighbour_steps = ((-1, -1), (-1, 0), (-1, 1), (0, -1), (0, 1), (1, -1), (1, 0), (1, 1))


def exchange_kernel(n, ny, x_ref, o_ref, send_sem, recv_sem, local_sem):
    me = lax.axis_index("tx") * ny + lax.axis_index("ty")

    def copy_to(d):
        return pltpu.make_async_remote_copy(
            src_ref=x_ref.at[d], dst_ref=o_ref.at[me], send_sem=send_sem.at[d],
            recv_sem=recv_sem.at[me], device_id=(d // ny, d % ny),
            device_id_type=pl.DeviceIdType.MESH)

    def copy_from(s):
        return pltpu.make_async_remote_copy(
            src_ref=x_ref.at[s], dst_ref=o_ref.at[s], send_sem=send_sem.at[s],
            recv_sem=recv_sem.at[s], device_id=(s // ny, s % ny),
            device_id_type=pl.DeviceIdType.MESH)

    local = pltpu.make_async_copy(x_ref.at[me], o_ref.at[me], local_sem)
    local.start()

    def start(k, carry):
        copy_to(lax.rem(me + k, n)).start()
        return carry
    lax.fori_loop(1, n, start, 0)

    def finish(k, carry):
        copy_to(lax.rem(me + k, n)).wait_send()
        copy_from(lax.rem(me + n - k, n)).wait_recv()
        return carry
    lax.fori_loop(1, n, finish, 0)
    local.wait()

def exchange(x, nx, ny):
    n = nx * ny
    return pl.pallas_call(
        functools.partial(exchange_kernel, n, ny),
        out_shape=jax.ShapeDtypeStruct(x.shape, x.dtype),
        in_specs=[pl.BlockSpec(memory_space=pltpu.VMEM)],
        out_specs=pl.BlockSpec(memory_space=pltpu.VMEM),
        scratch_shapes=[pltpu.SemaphoreType.DMA((n,)), pltpu.SemaphoreType.DMA((n,)), pltpu.SemaphoreType.DMA],
        compiler_params=pltpu.CompilerParams(has_side_effects=True),
    )(x)


def mlp_kernel(x_ref, w1_ref, w2_ref, w3_ref, o_ref):
    def silu(v):
        return v / (1.0 + jnp.exp(-v))

    h = silu(jnp.dot(x_ref[...], w1_ref[...], preferred_element_type=jnp.float32))
    h = h.astype(jnp.bfloat16)
    for layer_id in range(w2_ref.shape[0]):
        h = silu(jnp.dot(h, w2_ref[layer_id], preferred_element_type=jnp.float32))
        h = h.astype(jnp.bfloat16)
    o_ref[...] = jnp.dot(h, w3_ref[...], preferred_element_type=jnp.float32).astype(o_ref.dtype)


def point_mlp(x, w1, w2, w3, block):
    rows = x.shape[0]
    full = lambda shape: pl.BlockSpec(shape, lambda i: (0,) * len(shape))
    return pl.pallas_call(
        mlp_kernel,
        out_shape=jax.ShapeDtypeStruct((rows, w3.shape[1]), jnp.bfloat16),
        grid=(rows // block,),
        in_specs=[
            pl.BlockSpec((block, x.shape[1]), lambda i: (i, 0)),
            full(w1.shape),
            full(w2.shape),
            full(w3.shape),
        ],
        out_specs=pl.BlockSpec((block, w3.shape[1]), lambda i: (i, 0)),
    )(x, w1, w2, w3)


def permute_kernel(chunk, a_ref, b_ref, x_ref, o_ref):
    total = jnp.zeros(o_ref.shape, jnp.float32)
    keys = a_ref[...]
    for start in range(0, x_ref.shape[0], chunk):
        hits = (keys == b_ref[:, start : start + chunk]).astype(jnp.bfloat16)
        total += jnp.dot(hits, x_ref[start : start + chunk, :], preferred_element_type=jnp.float32)
    o_ref[...] = total.astype(o_ref.dtype)


def permute_rows(a, b, x, block, chunk):
    rows = a.shape[0]
    a = a.reshape(rows, 1)
    b = b.reshape(1, -1)
    return pl.pallas_call(
        functools.partial(permute_kernel, chunk),
        out_shape=jax.ShapeDtypeStruct((rows, x.shape[1]), x.dtype),
        grid=(rows // block,),
        in_specs=[
            pl.BlockSpec((block, 1), lambda i: (i, 0)),
            pl.BlockSpec(b.shape, lambda i: (0, 0)),
            pl.BlockSpec(x.shape, lambda i: (0, 0)),
        ],
        out_specs=pl.BlockSpec((block, x.shape[1]), lambda i: (i, 0)),
    )(a, b, x)


def gather_kernel(unroll, pos_ref, order_ref, x_ref, o_ref, rows_in, rows_out):
    rows_in[...] = x_ref[...].astype(jnp.float32)

    def body(step, carry):
        for lane in range(unroll):
            row = step * unroll + lane
            source = order_ref[pos_ref[row]]
            rows_out[pl.ds(row, 1), :] = rows_in[pl.ds(source, 1), :]
        return carry

    lax.fori_loop(0, o_ref.shape[0] // unroll, body, 0)
    o_ref[...] = rows_out[...].astype(o_ref.dtype)


def scatter_kernel(unroll, pos_ref, order_ref, x_ref, o_ref, rows_in, rows_out):
    rows_in[...] = x_ref[...].astype(jnp.float32)

    def body(step, carry):
        for lane in range(unroll):
            row = step * unroll + lane
            target = order_ref[pos_ref[row]]
            rows_out[pl.ds(target, 1), :] = rows_in[pl.ds(row, 1), :]
        return carry

    lax.fori_loop(0, x_ref.shape[0] // unroll, body, 0)
    o_ref[...] = rows_out[...].astype(o_ref.dtype)


def move_rows(kernel, pos, order, x):
    return pl.pallas_call(
        functools.partial(kernel, 8),
        out_shape=jax.ShapeDtypeStruct(x.shape, jnp.bfloat16),
        in_specs=[
            pl.BlockSpec(memory_space=pltpu.SMEM),
            pl.BlockSpec(memory_space=pltpu.SMEM),
            pl.BlockSpec(memory_space=pltpu.VMEM),
        ],
        out_specs=pl.BlockSpec(memory_space=pltpu.VMEM),
        scratch_shapes=[pltpu.VMEM(x.shape, jnp.float32), pltpu.VMEM(x.shape, jnp.float32)],
    )(pos, order, x)


def halo_kernel(count_x, count_y, x_ref, o_ref, send_sem, recv_sem, local_sem):
    index_x = lax.axis_index("tx")
    index_y = lax.axis_index("ty")
    size_x, size_y = x_ref.shape[0], x_ref.shape[1]
    mesh_ids = pl.DeviceIdType.MESH
    steps = [(a, b) for a in (-1, 0, 1) for b in (-1, 0, 1) if (a, b) != (0, 0)]

    def inside(px, py):
        return (px >= 0) & (px < count_x) & (py >= 0) & (py < count_y)

    def ranges(step, size):
        if step == 1:
            return pl.ds(size - 1, 1), pl.ds(0, 1)
        if step == -1:
            return pl.ds(0, 1), pl.ds(size + 1, 1)
        return pl.ds(0, size), pl.ds(1, size)

    barrier = pltpu.get_barrier_semaphore()
    for a, b in steps:
        @pl.when(inside(index_x + a, index_y + b))
        def _():
            pl.semaphore_signal(
                barrier, 1, device_id=(index_x + a, index_y + b), device_id_type=mesh_ids
            )
    peers = sum(inside(index_x + a, index_y + b).astype(jnp.int32) for a, b in steps)
    pl.semaphore_wait(barrier, peers)

    center = pltpu.make_async_copy(
        x_ref, o_ref.at[pl.ds(1, size_x), pl.ds(1, size_y)], local_sem
    )
    center.start()
    copies = []
    for k, (a, b) in enumerate(steps):
        source_x, target_x = ranges(a, size_x)
        source_y, target_y = ranges(b, size_y)
        copy = pltpu.make_async_remote_copy(
            src_ref=x_ref.at[source_x, source_y],
            dst_ref=o_ref.at[target_x, target_y],
            send_sem=send_sem.at[k],
            recv_sem=recv_sem.at[k],
            device_id=(index_x + a, index_y + b),
            device_id_type=mesh_ids,
        )
        copies.append(copy)
        pl.when(inside(index_x + a, index_y + b))(copy.start)
    for k, (a, b) in enumerate(steps):
        source_x, target_x = ranges(a, size_x)
        source_y, target_y = ranges(b, size_y)

        @pl.when(jnp.logical_not(inside(index_x - a, index_y - b)))
        def _():
            piece = o_ref.at[target_x, target_y]
            piece[...] = jnp.zeros(piece.shape, piece.dtype)
    for k, (a, b) in enumerate(steps):
        pl.when(inside(index_x + a, index_y + b))(copies[k].wait_send)
        pl.when(inside(index_x - a, index_y - b))(copies[k].wait_recv)
    center.wait()


def halo(block):
    count_x = lax.axis_size("tx")
    count_y = lax.axis_size("ty")
    shape = (block.shape[0] + 2, block.shape[1] + 2) + block.shape[2:]
    return pl.pallas_call(
        functools.partial(halo_kernel, count_x, count_y),
        out_shape=jax.ShapeDtypeStruct(shape, block.dtype),
        in_specs=[pl.BlockSpec(memory_space=pltpu.VMEM)],
        out_specs=pl.BlockSpec(memory_space=pltpu.VMEM),
        scratch_shapes=[
            pltpu.SemaphoreType.DMA((8,)),
            pltpu.SemaphoreType.DMA((8,)),
            pltpu.SemaphoreType.DMA,
        ],
        compiler_params=pltpu.CompilerParams(collective_id=0, has_side_effects=True),
    )(block)


def padded_2(block, sides, width):
    for axis, dim in sides:
        count = lax.axis_size(axis)
        forward = [(i, i + 1) for i in range(count - 1)]
        backward = [(target, source) for source, target in forward]
        low = lax.ppermute(
            lax.slice_in_dim(block, block.shape[dim] - width, None, axis=dim), axis, forward
        )
        high = lax.ppermute(lax.slice_in_dim(block, 0, width, axis=dim), axis, backward)
        block = jnp.concatenate([low, block, high], axis=dim)
    return block


def unit_heads(projected, head_count):
    pieces = projected.reshape(
        projected.shape[:-1] + (head_count, projected.shape[-1] // head_count)
    )
    magnitude = jnp.sqrt(jnp.sum(pieces * pieces, axis=-1, keepdims=True) + epsilon)
    return (pieces / magnitude).reshape(projected.shape).astype(jnp.bfloat16)


def gather_rows(order, rows, block):
    column_ids = jnp.arange(rows.shape[0], dtype=jnp.int32)

    def pick_block(index_block):
        table = (index_block[:, None] == column_ids[None, :]).astype(jnp.bfloat16)
        return jnp.dot(table, rows, preferred_element_type=jnp.float32).astype(jnp.bfloat16)

    picked = lax.map(pick_block, order.reshape(-1, block))
    return picked.reshape(order.shape[0], rows.shape[1])


def scatter_rows(order, rows, block):
    target_ids = jnp.arange(rows.shape[0], dtype=jnp.int32).reshape(-1, block)

    def place_block(target_block):
        table = (target_block[:, None] == order[None, :]).astype(jnp.bfloat16)
        return jnp.dot(table, rows, preferred_element_type=jnp.float32).astype(jnp.bfloat16)

    placed = lax.map(place_block, target_ids)
    return placed.reshape(rows.shape[0], rows.shape[1])


def body(
    points,
    embed_weight,
    inner_weights,
    output_weight,
    counts,
    point_order,
    inducing,
    first_proj,
    second_proj,
    mixing,
):
    along_x = lax.axis_size("tx")
    along_y = lax.axis_size("ty")
    devices = along_x * along_y
    index_x = lax.axis_index("tx")
    index_y = lax.axis_index("ty")
    own_index = index_x * along_y + index_y
    point_count = points.shape[0]
    per_device = TLX * TLY
    width = output_weight.shape[1]
    quota = point_count // devices
    band = quota * along_y
    head_width = width // HEADS
    inducing_count = inducing.shape[0]

    features = point_mlp(points, embed_weight, inner_weights, output_weight, 512)

    own_counts = lax.dynamic_index_in_dim(counts, own_index, 0, keepdims=False)
    own_offsets = jnp.cumsum(own_counts) - own_counts
    grid_counts = own_counts.reshape(along_x, TLX, along_y, TLY)
    grid_offsets = own_offsets.reshape(along_x, TLX, along_y, TLY)
    band_start = grid_offsets[:, 0, 0, 0][:, None]
    first_len = grid_counts[:, 0, :, 0] + grid_counts[:, 0, :, 1]
    first_start = grid_offsets[:, 0, :, 0] - band_start
    second_start = grid_offsets[:, 1, :, 0] - band_start
    slot_ids = jnp.arange(quota, dtype=jnp.int32)
    local_pos = jnp.where(
        slot_ids[None, None, :] < first_len[:, :, None],
        first_start[:, :, None] + slot_ids[None, None, :],
        second_start[:, :, None] + slot_ids[None, None, :] - first_len[:, :, None],
    ).reshape(along_x, band)
    send_pos = (local_pos + band_start).reshape(-1)
    order = point_order[0]
    outgoing = move_rows(gather_kernel, send_pos, order, features)
    outgoing = outgoing.reshape(devices, quota, width)
    arrived = lax.all_to_all(outgoing, ("tx", "ty"), split_axis=0, concat_axis=0, tiled=True)
    all_rows = arrived.reshape(devices * quota, width)

    inbound = counts.reshape(devices, along_x, TLX, along_y, TLY)
    inbound = lax.dynamic_index_in_dim(inbound, index_x, 1, keepdims=False)
    inbound = lax.dynamic_index_in_dim(inbound, index_y, 2, keepdims=False)
    inbound = inbound.reshape(devices, per_device)
    through = jnp.cumsum(inbound, axis=1)
    row_tile = jnp.sum(
        (slot_ids[None, :, None] >= through[:, None, : per_device - 1]).astype(jnp.int32), axis=2
    ).reshape(-1)
    tile_ids = jnp.arange(per_device, dtype=jnp.int32)
    row_mask = (row_tile[:, None] == tile_ids[None, :]).astype(jnp.float32)

    first_keys = unit_heads(
        jnp.dot(all_rows, first_proj[1], preferred_element_type=jnp.float32), HEADS
    )
    first_values = jnp.dot(all_rows, first_proj[2], preferred_element_type=jnp.float32).astype(
        jnp.bfloat16
    )
    inducing_queries = unit_heads(
        jnp.dot(inducing, first_proj[0], preferred_element_type=jnp.float32), HEADS
    )
    masked_values = first_values[:, None, :] * row_mask.astype(jnp.bfloat16)[:, :, None]
    heads_out = []
    for head_id in range(HEADS):
        lower = head_id * head_width
        upper = lower + head_width
        scores = jnp.dot(
            inducing_queries[:, lower:upper],
            first_keys[:, lower:upper].T,
            preferred_element_type=jnp.float32,
        )
        weights = jnp.exp(sharpness * scores)
        totals = jnp.dot(weights, row_mask, precision=lax.Precision.HIGHEST)
        numer = jnp.dot(
            weights.astype(jnp.bfloat16),
            masked_values[:, :, lower:upper].reshape(-1, per_device * head_width),
            preferred_element_type=jnp.float32,
        ).reshape(inducing_count, per_device, head_width)
        heads_out.append(numer / totals[:, :, None])
    first_attended = (
        jnp.concatenate(heads_out, axis=2).astype(jnp.bfloat16).transpose(1, 0, 2)
    )
    summary = (
        inducing.astype(jnp.float32)[None]
        + jnp.einsum(
            "tic,ce->tie", first_attended, first_proj[3], preferred_element_type=jnp.float32
        )
    ).astype(jnp.bfloat16)
    tile_grid = summary.reshape(TLX, TLY, inducing_count, width)
    padded = halo(tile_grid)
    stacked = jnp.stack(
        [
            padded[1 + steps[0] : 1 + steps[0] + TLX, 1 + steps[1] : 1 + steps[1] + TLY]
            for steps in neighbour_steps
        ]
    )
    mixture = tile_grid.astype(jnp.float32) + jnp.einsum(
        "dxyic,dce->xyie", stacked, mixing, preferred_element_type=jnp.float32
    )
    mixture = mixture.astype(jnp.bfloat16).reshape(per_device * inducing_count, width)

    point_queries = unit_heads(
        jnp.dot(all_rows, second_proj[0], preferred_element_type=jnp.float32), HEADS
    )
    second_keys = unit_heads(
        jnp.dot(mixture, second_proj[1], preferred_element_type=jnp.float32), HEADS
    )
    second_values = jnp.dot(mixture, second_proj[2], preferred_element_type=jnp.float32).astype(
        jnp.bfloat16
    )
    key_mask = jnp.repeat(row_mask, inducing_count, axis=1)
    heads_out = []
    for head_id in range(HEADS):
        lower = head_id * head_width
        upper = lower + head_width
        scores = jnp.dot(
            point_queries[:, lower:upper],
            second_keys[:, lower:upper].T,
            preferred_element_type=jnp.float32,
        )
        weights = jnp.exp(sharpness * scores) * key_mask
        totals = jnp.sum(weights, axis=1, keepdims=True)
        numer = jnp.dot(
            weights.astype(jnp.bfloat16),
            second_values[:, lower:upper],
            preferred_element_type=jnp.float32,
        )
        heads_out.append(numer / totals)
    second_attended = jnp.concatenate(heads_out, axis=1).astype(jnp.bfloat16)
    result = (
        all_rows.astype(jnp.float32)
        + jnp.dot(second_attended, second_proj[3], preferred_element_type=jnp.float32)
    ).astype(jnp.bfloat16)

    coming = lax.all_to_all(
        result.reshape(devices, quota, width), ("tx", "ty"), split_axis=0, concat_axis=0, tiled=True
    )
    returned = move_rows(
        scatter_kernel, send_pos, order, coming.reshape(point_count, width)
    )
    return returned


def solution(mesh):
    placed = (P(("tx", "ty"), None), P(), P(), P(), P(), P(("tx", "ty"), None), P(), P(), P(), P())
    return jax.shard_map(
        body, mesh=mesh, in_specs=placed, out_specs=P(("tx", "ty"), None), check_vma=False
    )
```

```python
import functools

import jax
import jax.numpy as jnp
from jax import lax
from jax.experimental import pallas as pl
from jax.experimental.pallas import tpu as pltpu
from jax.sharding import PartitionSpec as P

HEADS = 2
TLX = 2
TLY = 2


sharpness = 32.0
epsilon = 1e-06
neighbour_steps = ((-1, -1), (-1, 0), (-1, 1), (0, -1), (0, 1), (1, -1), (1, 0), (1, 1))


def mlp_kernel(x_ref, w1_ref, w2_ref, w3_ref, o_ref):
    def silu(v):
        return v / (1.0 + jnp.exp(-v))

    h = silu(jnp.dot(x_ref[...], w1_ref[...], preferred_element_type=jnp.float32))
    h = h.astype(jnp.bfloat16)
    for layer_id in range(w2_ref.shape[0]):
        h = silu(jnp.dot(h, w2_ref[layer_id], preferred_element_type=jnp.float32))
        h = h.astype(jnp.bfloat16)
    o_ref[...] = jnp.dot(h, w3_ref[...], preferred_element_type=jnp.float32).astype(o_ref.dtype)


def point_mlp(x, w1, w2, w3, block):
    rows = x.shape[0]
    full = lambda shape: pl.BlockSpec(shape, lambda i: (0,) * len(shape))
    return pl.pallas_call(
        mlp_kernel,
        out_shape=jax.ShapeDtypeStruct((rows, w3.shape[1]), jnp.bfloat16),
        grid=(rows // block,),
        in_specs=[
            pl.BlockSpec((block, x.shape[1]), lambda i: (i, 0)),
            full(w1.shape),
            full(w2.shape),
            full(w3.shape),
        ],
        out_specs=pl.BlockSpec((block, w3.shape[1]), lambda i: (i, 0)),
    )(x, w1, w2, w3)


def gather_kernel(unroll, pos_ref, order_ref, x_ref, o_ref, rows_in, rows_out):
    rows_in[...] = x_ref[...].astype(jnp.float32)

    def body(step, carry):
        for lane in range(unroll):
            row = step * unroll + lane
            source = order_ref[pos_ref[row]]
            rows_out[pl.ds(row, 1), :] = rows_in[pl.ds(source, 1), :]
        return carry

    lax.fori_loop(0, o_ref.shape[0] // unroll, body, 0)
    o_ref[...] = rows_out[...].astype(o_ref.dtype)


def scatter_kernel(unroll, pos_ref, order_ref, x_ref, o_ref, rows_in, rows_out):
    rows_in[...] = x_ref[...].astype(jnp.float32)

    def body(step, carry):
        for lane in range(unroll):
            row = step * unroll + lane
            target = order_ref[pos_ref[row]]
            rows_out[pl.ds(target, 1), :] = rows_in[pl.ds(row, 1), :]
        return carry

    lax.fori_loop(0, x_ref.shape[0] // unroll, body, 0)
    o_ref[...] = rows_out[...].astype(o_ref.dtype)


def move_rows(kernel, pos, order, x):
    return pl.pallas_call(
        functools.partial(kernel, 8),
        out_shape=jax.ShapeDtypeStruct(x.shape, jnp.bfloat16),
        in_specs=[
            pl.BlockSpec(memory_space=pltpu.SMEM),
            pl.BlockSpec(memory_space=pltpu.SMEM),
            pl.BlockSpec(memory_space=pltpu.VMEM),
        ],
        out_specs=pl.BlockSpec(memory_space=pltpu.VMEM),
        scratch_shapes=[pltpu.VMEM(x.shape, jnp.float32), pltpu.VMEM(x.shape, jnp.float32)],
    )(pos, order, x)


def mix_kernel(count_x, count_y, x_ref, mixing_ref, o_ref, padded, send_sem, recv_sem, local_sem):
    index_x = lax.axis_index("tx")
    index_y = lax.axis_index("ty")
    size_x, size_y = x_ref.shape[0], x_ref.shape[1]
    mesh_ids = pl.DeviceIdType.MESH
    steps = [(a, b) for a in (-1, 0, 1) for b in (-1, 0, 1) if (a, b) != (0, 0)]

    def inside(px, py):
        return (px >= 0) & (px < count_x) & (py >= 0) & (py < count_y)

    def ranges(step, size):
        if step == 1:
            return pl.ds(size - 1, 1), pl.ds(0, 1)
        if step == -1:
            return pl.ds(0, 1), pl.ds(size + 1, 1)
        return pl.ds(0, size), pl.ds(1, size)

    barrier = pltpu.get_barrier_semaphore()
    for a, b in steps:
        @pl.when(inside(index_x + a, index_y + b))
        def _():
            pl.semaphore_signal(
                barrier, 1, device_id=(index_x + a, index_y + b), device_id_type=mesh_ids
            )
    peers = sum(inside(index_x + a, index_y + b).astype(jnp.int32) for a, b in steps)
    pl.semaphore_wait(barrier, peers)

    center = pltpu.make_async_copy(
        x_ref, padded.at[pl.ds(1, size_x), pl.ds(1, size_y)], local_sem
    )
    center.start()
    copies = []
    for k, (a, b) in enumerate(steps):
        source_x, target_x = ranges(a, size_x)
        source_y, target_y = ranges(b, size_y)
        copy = pltpu.make_async_remote_copy(
            src_ref=x_ref.at[source_x, source_y],
            dst_ref=padded.at[target_x, target_y],
            send_sem=send_sem.at[k],
            recv_sem=recv_sem.at[k],
            device_id=(index_x + a, index_y + b),
            device_id_type=mesh_ids,
        )
        copies.append(copy)
        pl.when(inside(index_x + a, index_y + b))(copy.start)
    for k, (a, b) in enumerate(steps):
        source_x, target_x = ranges(a, size_x)
        source_y, target_y = ranges(b, size_y)

        @pl.when(jnp.logical_not(inside(index_x - a, index_y - b)))
        def _():
            piece = padded.at[target_x, target_y]
            piece[...] = jnp.zeros(piece.shape, piece.dtype)
    for k, (a, b) in enumerate(steps):
        pl.when(inside(index_x + a, index_y + b))(copies[k].wait_send)
        pl.when(inside(index_x - a, index_y - b))(copies[k].wait_recv)
    center.wait()
    for tile_x in range(size_x):
        for tile_y in range(size_y):
            total = x_ref[tile_x, tile_y].astype(jnp.float32)
            for k, (a, b) in enumerate(steps):
                total += jnp.dot(
                    padded[1 + tile_x + a, 1 + tile_y + b],
                    mixing_ref[k],
                    preferred_element_type=jnp.float32,
                )
            o_ref[tile_x, tile_y] = total.astype(o_ref.dtype)


def mix_tiles(block, mixing):
    count_x = lax.axis_size("tx")
    count_y = lax.axis_size("ty")
    shape = (block.shape[0] + 2, block.shape[1] + 2) + block.shape[2:]
    return pl.pallas_call(
        functools.partial(mix_kernel, count_x, count_y),
        out_shape=jax.ShapeDtypeStruct(block.shape, block.dtype),
        in_specs=[pl.BlockSpec(memory_space=pltpu.VMEM)] * 2,
        out_specs=pl.BlockSpec(memory_space=pltpu.VMEM),
        scratch_shapes=[
            pltpu.VMEM(shape, block.dtype),
            pltpu.SemaphoreType.DMA((8,)),
            pltpu.SemaphoreType.DMA((8,)),
            pltpu.SemaphoreType.DMA,
        ],
        compiler_params=pltpu.CompilerParams(collective_id=0, has_side_effects=True),
    )(block, mixing)


def unit_heads(projected, head_count):
    pieces = projected.reshape(
        projected.shape[:-1] + (head_count, projected.shape[-1] // head_count)
    )
    magnitude = jnp.sqrt(jnp.sum(pieces * pieces, axis=-1, keepdims=True) + epsilon)
    return (pieces / magnitude).reshape(projected.shape).astype(jnp.bfloat16)


def body(
    points,
    embed_weight,
    inner_weights,
    output_weight,
    counts,
    point_order,
    inducing,
    first_proj,
    second_proj,
    mixing,
):
    along_x = lax.axis_size("tx")
    along_y = lax.axis_size("ty")
    devices = along_x * along_y
    index_x = lax.axis_index("tx")
    index_y = lax.axis_index("ty")
    own_index = index_x * along_y + index_y
    point_count = points.shape[0]
    per_device = TLX * TLY
    width = output_weight.shape[1]
    quota = point_count // devices
    band = quota * along_y
    head_width = width // HEADS
    inducing_count = inducing.shape[0]

    features = point_mlp(points, embed_weight, inner_weights, output_weight, 512)

    own_counts = lax.dynamic_index_in_dim(counts, own_index, 0, keepdims=False)
    own_offsets = jnp.cumsum(own_counts) - own_counts
    grid_counts = own_counts.reshape(along_x, TLX, along_y, TLY)
    grid_offsets = own_offsets.reshape(along_x, TLX, along_y, TLY)
    band_start = grid_offsets[:, 0, 0, 0][:, None]
    first_len = grid_counts[:, 0, :, 0] + grid_counts[:, 0, :, 1]
    first_start = grid_offsets[:, 0, :, 0] - band_start
    second_start = grid_offsets[:, 1, :, 0] - band_start
    slot_ids = jnp.arange(quota, dtype=jnp.int32)
    local_pos = jnp.where(
        slot_ids[None, None, :] < first_len[:, :, None],
        first_start[:, :, None] + slot_ids[None, None, :],
        second_start[:, :, None] + slot_ids[None, None, :] - first_len[:, :, None],
    ).reshape(along_x, band)
    send_pos = (local_pos + band_start).reshape(-1)
    order = point_order[0]
    outgoing = move_rows(gather_kernel, send_pos, order, features)
    outgoing = outgoing.reshape(devices, quota, width)
    arrived = lax.all_to_all(outgoing, ("tx", "ty"), split_axis=0, concat_axis=0, tiled=True)
    all_rows = arrived.reshape(devices * quota, width)

    inbound = counts.reshape(devices, along_x, TLX, along_y, TLY)
    inbound = lax.dynamic_index_in_dim(inbound, index_x, 1, keepdims=False)
    inbound = lax.dynamic_index_in_dim(inbound, index_y, 2, keepdims=False)
    inbound = inbound.reshape(devices, per_device)
    through = jnp.cumsum(inbound, axis=1)
    row_tile = jnp.sum(
        (slot_ids[None, :, None] >= through[:, None, : per_device - 1]).astype(jnp.int32), axis=2
    ).reshape(-1)
    tile_ids = jnp.arange(per_device, dtype=jnp.int32)
    row_mask = (row_tile[:, None] == tile_ids[None, :]).astype(jnp.float32)

    first_keys = unit_heads(
        jnp.dot(all_rows, first_proj[1], preferred_element_type=jnp.float32), HEADS
    )
    first_values = jnp.dot(all_rows, first_proj[2], preferred_element_type=jnp.float32).astype(
        jnp.bfloat16
    )
    inducing_queries = unit_heads(
        jnp.dot(inducing, first_proj[0], preferred_element_type=jnp.float32), HEADS
    )
    masked_values = first_values[:, None, :] * row_mask.astype(jnp.bfloat16)[:, :, None]
    heads_out = []
    for head_id in range(HEADS):
        lower = head_id * head_width
        upper = lower + head_width
        scores = jnp.dot(
            inducing_queries[:, lower:upper],
            first_keys[:, lower:upper].T,
            preferred_element_type=jnp.float32,
        )
        weights = jnp.exp(sharpness * scores)
        totals = jnp.dot(weights, row_mask, precision=lax.Precision.HIGHEST)
        numer = jnp.dot(
            weights.astype(jnp.bfloat16),
            masked_values[:, :, lower:upper].reshape(-1, per_device * head_width),
            preferred_element_type=jnp.float32,
        ).reshape(inducing_count, per_device, head_width)
        heads_out.append(numer / totals[:, :, None])
    first_attended = (
        jnp.concatenate(heads_out, axis=2).astype(jnp.bfloat16).transpose(1, 0, 2)
    )
    summary = (
        inducing.astype(jnp.float32)[None]
        + jnp.einsum(
            "tic,ce->tie", first_attended, first_proj[3], preferred_element_type=jnp.float32
        )
    ).astype(jnp.bfloat16)
    tile_grid = summary.reshape(TLX, TLY, inducing_count, width)
    mixture = mix_tiles(tile_grid, mixing)
    mixture = mixture.astype(jnp.bfloat16).reshape(per_device * inducing_count, width)

    point_queries = unit_heads(
        jnp.dot(all_rows, second_proj[0], preferred_element_type=jnp.float32), HEADS
    )
    second_keys = unit_heads(
        jnp.dot(mixture, second_proj[1], preferred_element_type=jnp.float32), HEADS
    )
    second_values = jnp.dot(mixture, second_proj[2], preferred_element_type=jnp.float32).astype(
        jnp.bfloat16
    )
    key_mask = jnp.repeat(row_mask, inducing_count, axis=1)
    heads_out = []
    for head_id in range(HEADS):
        lower = head_id * head_width
        upper = lower + head_width
        scores = jnp.dot(
            point_queries[:, lower:upper],
            second_keys[:, lower:upper].T,
            preferred_element_type=jnp.float32,
        )
        weights = jnp.exp(sharpness * scores) * key_mask
        totals = jnp.sum(weights, axis=1, keepdims=True)
        numer = jnp.dot(
            weights.astype(jnp.bfloat16),
            second_values[:, lower:upper],
            preferred_element_type=jnp.float32,
        )
        heads_out.append(numer / totals)
    second_attended = jnp.concatenate(heads_out, axis=1).astype(jnp.bfloat16)
    result = (
        all_rows.astype(jnp.float32)
        + jnp.dot(second_attended, second_proj[3], preferred_element_type=jnp.float32)
    ).astype(jnp.bfloat16)

    coming = lax.all_to_all(
        result.reshape(devices, quota, width), ("tx", "ty"), split_axis=0, concat_axis=0, tiled=True
    )
    returned = move_rows(
        scatter_kernel, send_pos, order, coming.reshape(point_count, width)
    )
    return returned


def solution(mesh):
    placed = (P(("tx", "ty"), None), P(), P(), P(), P(), P(("tx", "ty"), None), P(), P(), P(), P())
    return jax.shard_map(
        body, mesh=mesh, in_specs=placed, out_specs=P(("tx", "ty"), None), check_vma=False
    )
```

```python
import functools

import jax
import jax.numpy as jnp
from jax import lax
from jax.experimental import pallas as pl
from jax.experimental.pallas import tpu as pltpu
from jax.sharding import PartitionSpec as P

HEADS = 2
TLX = 2
TLY = 2


sharpness = 32.0
epsilon = 1e-06
neighbour_steps = ((-1, -1), (-1, 0), (-1, 1), (0, -1), (0, 1), (1, -1), (1, 0), (1, 1))


def mlp_kernel(x_ref, w1_ref, w2_ref, w3_ref, o_ref):
    def silu(v):
        return v / (1.0 + jnp.exp(-v))

    h = silu(jnp.dot(x_ref[...], w1_ref[...], preferred_element_type=jnp.float32))
    h = h.astype(jnp.bfloat16)
    for layer_id in range(w2_ref.shape[0]):
        h = silu(jnp.dot(h, w2_ref[layer_id], preferred_element_type=jnp.float32))
        h = h.astype(jnp.bfloat16)
    o_ref[...] = jnp.dot(h, w3_ref[...], preferred_element_type=jnp.float32).astype(o_ref.dtype)


def point_mlp(x, w1, w2, w3, block):
    rows = x.shape[0]
    full = lambda shape: pl.BlockSpec(shape, lambda i: (0,) * len(shape))
    return pl.pallas_call(
        mlp_kernel,
        out_shape=jax.ShapeDtypeStruct((rows, w3.shape[1]), jnp.bfloat16),
        grid=(rows // block,),
        in_specs=[
            pl.BlockSpec((block, x.shape[1]), lambda i: (i, 0)),
            full(w1.shape),
            full(w2.shape),
            full(w3.shape),
        ],
        out_specs=pl.BlockSpec((block, w3.shape[1]), lambda i: (i, 0)),
    )(x, w1, w2, w3)


def gather_kernel(unroll, pos_ref, order_ref, x_ref, o_ref, rows_in, rows_out):
    rows_in[...] = x_ref[...].astype(jnp.float32)

    def body(step, carry):
        for lane in range(unroll):
            row = step * unroll + lane
            source = order_ref[pos_ref[row]]
            rows_out[pl.ds(row, 1), :] = rows_in[pl.ds(source, 1), :]
        return carry

    lax.fori_loop(0, o_ref.shape[0] // unroll, body, 0)
    o_ref[...] = rows_out[...].astype(o_ref.dtype)


def scatter_kernel(unroll, pos_ref, order_ref, x_ref, o_ref, rows_in, rows_out):
    rows_in[...] = x_ref[...].astype(jnp.float32)

    def body(step, carry):
        for lane in range(unroll):
            row = step * unroll + lane
            target = order_ref[pos_ref[row]]
            rows_out[pl.ds(target, 1), :] = rows_in[pl.ds(row, 1), :]
        return carry

    lax.fori_loop(0, x_ref.shape[0] // unroll, body, 0)
    o_ref[...] = rows_out[...].astype(o_ref.dtype)


def move_rows(kernel, pos, order, x):
    return pl.pallas_call(
        functools.partial(kernel, 8),
        out_shape=jax.ShapeDtypeStruct(x.shape, jnp.bfloat16),
        in_specs=[
            pl.BlockSpec(memory_space=pltpu.SMEM),
            pl.BlockSpec(memory_space=pltpu.SMEM),
            pl.BlockSpec(memory_space=pltpu.VMEM),
        ],
        out_specs=pl.BlockSpec(memory_space=pltpu.VMEM),
        scratch_shapes=[pltpu.VMEM(x.shape, jnp.float32), pltpu.VMEM(x.shape, jnp.float32)],
    )(pos, order, x)


def mix_kernel(count_x, count_y, x_ref, mixing_ref, o_ref, padded, send_sem, recv_sem, local_sem):
    index_x = lax.axis_index("tx")
    index_y = lax.axis_index("ty")
    size_x, size_y = x_ref.shape[0], x_ref.shape[1]
    mesh_ids = pl.DeviceIdType.MESH
    steps = [(a, b) for a in (-1, 0, 1) for b in (-1, 0, 1) if (a, b) != (0, 0)]

    def inside(px, py):
        return (px >= 0) & (px < count_x) & (py >= 0) & (py < count_y)

    def ranges(step, size):
        if step == 1:
            return pl.ds(size - 1, 1), pl.ds(0, 1)
        if step == -1:
            return pl.ds(0, 1), pl.ds(size + 1, 1)
        return pl.ds(0, size), pl.ds(1, size)

    barrier = pltpu.get_barrier_semaphore()
    for a, b in steps:
        @pl.when(inside(index_x + a, index_y + b))
        def _():
            pl.semaphore_signal(
                barrier, 1, device_id=(index_x + a, index_y + b), device_id_type=mesh_ids
            )
    peers = sum(inside(index_x + a, index_y + b).astype(jnp.int32) for a, b in steps)
    pl.semaphore_wait(barrier, peers)

    center = pltpu.make_async_copy(
        x_ref, padded.at[pl.ds(1, size_x), pl.ds(1, size_y)], local_sem
    )
    center.start()
    copies = []
    for k, (a, b) in enumerate(steps):
        source_x, target_x = ranges(a, size_x)
        source_y, target_y = ranges(b, size_y)
        copy = pltpu.make_async_remote_copy(
            src_ref=x_ref.at[source_x, source_y],
            dst_ref=padded.at[target_x, target_y],
            send_sem=send_sem.at[k],
            recv_sem=recv_sem.at[k],
            device_id=(index_x + a, index_y + b),
            device_id_type=mesh_ids,
        )
        copies.append(copy)
        pl.when(inside(index_x + a, index_y + b))(copy.start)
    for k, (a, b) in enumerate(steps):
        source_x, target_x = ranges(a, size_x)
        source_y, target_y = ranges(b, size_y)

        @pl.when(jnp.logical_not(inside(index_x - a, index_y - b)))
        def _():
            piece = padded.at[target_x, target_y]
            piece[...] = jnp.zeros(piece.shape, piece.dtype)
    for k, (a, b) in enumerate(steps):
        pl.when(inside(index_x + a, index_y + b))(copies[k].wait_send)
        pl.when(inside(index_x - a, index_y - b))(copies[k].wait_recv)
    center.wait()
    for tile_x in range(size_x):
        for tile_y in range(size_y):
            total = x_ref[tile_x, tile_y].astype(jnp.float32)
            for k, (a, b) in enumerate(steps):
                total += jnp.dot(
                    padded[1 + tile_x + a, 1 + tile_y + b],
                    mixing_ref[k],
                    preferred_element_type=jnp.float32,
                )
            o_ref[tile_x, tile_y] = total.astype(o_ref.dtype)


def mix_tiles(block, mixing):
    count_x = lax.axis_size("tx")
    count_y = lax.axis_size("ty")
    shape = (block.shape[0] + 2, block.shape[1] + 2) + block.shape[2:]
    return pl.pallas_call(
        functools.partial(mix_kernel, count_x, count_y),
        out_shape=jax.ShapeDtypeStruct(block.shape, block.dtype),
        in_specs=[pl.BlockSpec(memory_space=pltpu.VMEM)] * 2,
        out_specs=pl.BlockSpec(memory_space=pltpu.VMEM),
        scratch_shapes=[
            pltpu.VMEM(shape, block.dtype),
            pltpu.SemaphoreType.DMA((8,)),
            pltpu.SemaphoreType.DMA((8,)),
            pltpu.SemaphoreType.DMA,
        ],
        compiler_params=pltpu.CompilerParams(collective_id=0, has_side_effects=True),
    )(block, mixing)


def unit_heads(projected, head_count):
    pieces = projected.reshape(
        projected.shape[:-1] + (head_count, projected.shape[-1] // head_count)
    )
    magnitude = jnp.sqrt(jnp.sum(pieces * pieces, axis=-1, keepdims=True) + epsilon)
    return (pieces / magnitude).reshape(projected.shape).astype(jnp.bfloat16)


def unit_rows(projected, head_width):
    lanes = lax.broadcasted_iota(jnp.int32, projected.shape, projected.ndim - 1)
    squares = projected * projected
    magnitude = jnp.zeros_like(projected)
    for head_id in range(projected.shape[-1] // head_width):
        in_head = (lanes >= head_id * head_width) & (lanes < (head_id + 1) * head_width)
        total = jnp.sum(jnp.where(in_head, squares, 0.0), axis=-1, keepdims=True)
        magnitude = jnp.where(in_head, jnp.sqrt(total + epsilon), magnitude)
    return (projected / magnitude).astype(jnp.bfloat16)


def summary_kernel(rows_ref, column_mask_ref, lane_mask_ref, inducing_ref, proj_ref, o_ref):
    width = rows_ref.shape[1]
    head_width = width // HEADS
    tiles = column_mask_ref.shape[1]
    rows = rows_ref[...]
    queries = unit_rows(
        jnp.dot(inducing_ref[...], proj_ref[0], preferred_element_type=jnp.float32), head_width
    )
    keys = unit_rows(jnp.dot(rows, proj_ref[1], preferred_element_type=jnp.float32), head_width)
    values = jnp.dot(rows, proj_ref[2], preferred_element_type=jnp.float32).astype(jnp.bfloat16)
    column_mask = column_mask_ref[...]
    lane_mask = lane_mask_ref[...]
    heads_out = []
    for head_id in range(HEADS):
        lower = head_id * head_width
        upper = lower + head_width
        scores = lax.dot_general(
            queries[:, lower:upper],
            keys[:, lower:upper],
            (((1,), (1,)), ((), ())),
            preferred_element_type=jnp.float32,
        )
        weights = jnp.exp(sharpness * scores)
        rounded = weights.astype(jnp.bfloat16)
        head_values = values[:, lower:upper]
        masked = jnp.concatenate(
            [head_values * column_mask[:, t : t + 1] for t in range(tiles)], axis=1
        )
        numer = jnp.dot(rounded, masked, preferred_element_type=jnp.float32)
        per_tile = []
        for t in range(tiles):
            totals = jnp.sum(weights * lane_mask[t : t + 1, :], axis=1, keepdims=True)
            per_tile.append(numer[:, t * head_width : (t + 1) * head_width] / totals)
        heads_out.append(per_tile)
    inducing = inducing_ref[...].astype(jnp.float32)
    for t in range(tiles):
        attended = jnp.concatenate([heads_out[h][t] for h in range(HEADS)], axis=1)
        attended = attended.astype(jnp.bfloat16)
        o_ref[t] = (
            inducing + jnp.dot(attended, proj_ref[3], preferred_element_type=jnp.float32)
        ).astype(o_ref.dtype)


def summarize(rows, row_mask, inducing, proj):
    tiles = row_mask.shape[1]
    return pl.pallas_call(
        summary_kernel,
        out_shape=jax.ShapeDtypeStruct((tiles,) + inducing.shape, jnp.bfloat16),
        in_specs=[pl.BlockSpec(memory_space=pltpu.VMEM)] * 5,
        out_specs=pl.BlockSpec(memory_space=pltpu.VMEM),
    )(rows, row_mask.astype(jnp.bfloat16), row_mask.T, inducing, proj)


def body(
    points,
    embed_weight,
    inner_weights,
    output_weight,
    counts,
    point_order,
    inducing,
    first_proj,
    second_proj,
    mixing,
):
    along_x = lax.axis_size("tx")
    along_y = lax.axis_size("ty")
    devices = along_x * along_y
    index_x = lax.axis_index("tx")
    index_y = lax.axis_index("ty")
    own_index = index_x * along_y + index_y
    point_count = points.shape[0]
    per_device = TLX * TLY
    width = output_weight.shape[1]
    quota = point_count // devices
    band = quota * along_y
    head_width = width // HEADS
    inducing_count = inducing.shape[0]

    features = point_mlp(points, embed_weight, inner_weights, output_weight, 512)

    own_counts = lax.dynamic_index_in_dim(counts, own_index, 0, keepdims=False)
    own_offsets = jnp.cumsum(own_counts) - own_counts
    grid_counts = own_counts.reshape(along_x, TLX, along_y, TLY)
    grid_offsets = own_offsets.reshape(along_x, TLX, along_y, TLY)
    band_start = grid_offsets[:, 0, 0, 0][:, None]
    first_len = grid_counts[:, 0, :, 0] + grid_counts[:, 0, :, 1]
    first_start = grid_offsets[:, 0, :, 0] - band_start
    second_start = grid_offsets[:, 1, :, 0] - band_start
    slot_ids = jnp.arange(quota, dtype=jnp.int32)
    local_pos = jnp.where(
        slot_ids[None, None, :] < first_len[:, :, None],
        first_start[:, :, None] + slot_ids[None, None, :],
        second_start[:, :, None] + slot_ids[None, None, :] - first_len[:, :, None],
    ).reshape(along_x, band)
    send_pos = (local_pos + band_start).reshape(-1)
    order = point_order[0]
    outgoing = move_rows(gather_kernel, send_pos, order, features)
    outgoing = outgoing.reshape(devices, quota, width)
    arrived = lax.all_to_all(outgoing, ("tx", "ty"), split_axis=0, concat_axis=0, tiled=True)
    all_rows = arrived.reshape(devices * quota, width)

    inbound = counts.reshape(devices, along_x, TLX, along_y, TLY)
    inbound = lax.dynamic_index_in_dim(inbound, index_x, 1, keepdims=False)
    inbound = lax.dynamic_index_in_dim(inbound, index_y, 2, keepdims=False)
    inbound = inbound.reshape(devices, per_device)
    through = jnp.cumsum(inbound, axis=1)
    row_tile = jnp.sum(
        (slot_ids[None, :, None] >= through[:, None, : per_device - 1]).astype(jnp.int32), axis=2
    ).reshape(-1)
    tile_ids = jnp.arange(per_device, dtype=jnp.int32)
    row_mask = (row_tile[:, None] == tile_ids[None, :]).astype(jnp.float32)

    summary = summarize(all_rows, row_mask, inducing, first_proj)
    tile_grid = summary.reshape(TLX, TLY, inducing_count, width)
    mixture = mix_tiles(tile_grid, mixing)
    mixture = mixture.astype(jnp.bfloat16).reshape(per_device * inducing_count, width)

    point_queries = unit_heads(
        jnp.dot(all_rows, second_proj[0], preferred_element_type=jnp.float32), HEADS
    )
    second_keys = unit_heads(
        jnp.dot(mixture, second_proj[1], preferred_element_type=jnp.float32), HEADS
    )
    second_values = jnp.dot(mixture, second_proj[2], preferred_element_type=jnp.float32).astype(
        jnp.bfloat16
    )
    key_mask = jnp.repeat(row_mask, inducing_count, axis=1)
    heads_out = []
    for head_id in range(HEADS):
        lower = head_id * head_width
        upper = lower + head_width
        scores = jnp.dot(
            point_queries[:, lower:upper],
            second_keys[:, lower:upper].T,
            preferred_element_type=jnp.float32,
        )
        weights = jnp.exp(sharpness * scores) * key_mask
        totals = jnp.sum(weights, axis=1, keepdims=True)
        numer = jnp.dot(
            weights.astype(jnp.bfloat16),
            second_values[:, lower:upper],
            preferred_element_type=jnp.float32,
        )
        heads_out.append(numer / totals)
    second_attended = jnp.concatenate(heads_out, axis=1).astype(jnp.bfloat16)
    result = (
        all_rows.astype(jnp.float32)
        + jnp.dot(second_attended, second_proj[3], preferred_element_type=jnp.float32)
    ).astype(jnp.bfloat16)

    coming = lax.all_to_all(
        result.reshape(devices, quota, width), ("tx", "ty"), split_axis=0, concat_axis=0, tiled=True
    )
    returned = move_rows(
        scatter_kernel, send_pos, order, coming.reshape(point_count, width)
    )
    return returned


def solution(mesh):
    placed = (P(("tx", "ty"), None), P(), P(), P(), P(), P(("tx", "ty"), None), P(), P(), P(), P())
    return jax.shard_map(
        body, mesh=mesh, in_specs=placed, out_specs=P(("tx", "ty"), None), check_vma=False
    )
```

```python
import functools

import jax
import jax.numpy as jnp
from jax import lax
from jax.experimental import pallas as pl
from jax.experimental.pallas import tpu as pltpu
from jax.sharding import PartitionSpec as P

HEADS = 2
TLX = 2
TLY = 2


sharpness = 32.0
epsilon = 1e-06
neighbour_steps = ((-1, -1), (-1, 0), (-1, 1), (0, -1), (0, 1), (1, -1), (1, 0), (1, 1))


def mlp_kernel(x_ref, w1_ref, w2_ref, w3_ref, o_ref):
    def silu(v):
        return v / (1.0 + jnp.exp(-v))

    h = silu(jnp.dot(x_ref[...], w1_ref[...], preferred_element_type=jnp.float32))
    h = h.astype(jnp.bfloat16)
    for layer_id in range(w2_ref.shape[0]):
        h = silu(jnp.dot(h, w2_ref[layer_id], preferred_element_type=jnp.float32))
        h = h.astype(jnp.bfloat16)
    o_ref[...] = jnp.dot(h, w3_ref[...], preferred_element_type=jnp.float32).astype(o_ref.dtype)


def point_mlp(x, w1, w2, w3, block):
    rows = x.shape[0]
    full = lambda shape: pl.BlockSpec(shape, lambda i: (0,) * len(shape))
    return pl.pallas_call(
        mlp_kernel,
        out_shape=jax.ShapeDtypeStruct((rows, w3.shape[1]), jnp.bfloat16),
        grid=(rows // block,),
        in_specs=[
            pl.BlockSpec((block, x.shape[1]), lambda i: (i, 0)),
            full(w1.shape),
            full(w2.shape),
            full(w3.shape),
        ],
        out_specs=pl.BlockSpec((block, w3.shape[1]), lambda i: (i, 0)),
    )(x, w1, w2, w3)


def gather_kernel(unroll, pos_ref, order_ref, x_ref, o_ref, rows_in, rows_out):
    rows_in[...] = x_ref[...].astype(jnp.float32)

    def body(step, carry):
        for lane in range(unroll):
            row = step * unroll + lane
            source = order_ref[pos_ref[row]]
            rows_out[pl.ds(row, 1), :] = rows_in[pl.ds(source, 1), :]
        return carry

    lax.fori_loop(0, o_ref.shape[0] // unroll, body, 0)
    o_ref[...] = rows_out[...].astype(o_ref.dtype)


def scatter_kernel(unroll, pos_ref, order_ref, x_ref, o_ref, rows_in, rows_out):
    rows_in[...] = x_ref[...].astype(jnp.float32)

    def body(step, carry):
        for lane in range(unroll):
            row = step * unroll + lane
            target = order_ref[pos_ref[row]]
            rows_out[pl.ds(target, 1), :] = rows_in[pl.ds(row, 1), :]
        return carry

    lax.fori_loop(0, x_ref.shape[0] // unroll, body, 0)
    o_ref[...] = rows_out[...].astype(o_ref.dtype)


def move_rows(kernel, pos, order, x):
    return pl.pallas_call(
        functools.partial(kernel, 8),
        out_shape=jax.ShapeDtypeStruct(x.shape, jnp.bfloat16),
        in_specs=[
            pl.BlockSpec(memory_space=pltpu.SMEM),
            pl.BlockSpec(memory_space=pltpu.SMEM),
            pl.BlockSpec(memory_space=pltpu.VMEM),
        ],
        out_specs=pl.BlockSpec(memory_space=pltpu.VMEM),
        scratch_shapes=[pltpu.VMEM(x.shape, jnp.float32), pltpu.VMEM(x.shape, jnp.float32)],
    )(pos, order, x)


def mix_kernel(count_x, count_y, x_ref, mixing_ref, o_ref, padded, send_sem, recv_sem, local_sem):
    index_x = lax.axis_index("tx")
    index_y = lax.axis_index("ty")
    size_x, size_y = x_ref.shape[0], x_ref.shape[1]
    mesh_ids = pl.DeviceIdType.MESH
    steps = [(a, b) for a in (-1, 0, 1) for b in (-1, 0, 1) if (a, b) != (0, 0)]

    def inside(px, py):
        return (px >= 0) & (px < count_x) & (py >= 0) & (py < count_y)

    def ranges(step, size):
        if step == 1:
            return pl.ds(size - 1, 1), pl.ds(0, 1)
        if step == -1:
            return pl.ds(0, 1), pl.ds(size + 1, 1)
        return pl.ds(0, size), pl.ds(1, size)

    barrier = pltpu.get_barrier_semaphore()
    for a, b in steps:
        @pl.when(inside(index_x + a, index_y + b))
        def _():
            pl.semaphore_signal(
                barrier, 1, device_id=(index_x + a, index_y + b), device_id_type=mesh_ids
            )
    peers = sum(inside(index_x + a, index_y + b).astype(jnp.int32) for a, b in steps)
    pl.semaphore_wait(barrier, peers)

    center = pltpu.make_async_copy(
        x_ref, padded.at[pl.ds(1, size_x), pl.ds(1, size_y)], local_sem
    )
    center.start()
    copies = []
    for k, (a, b) in enumerate(steps):
        source_x, target_x = ranges(a, size_x)
        source_y, target_y = ranges(b, size_y)
        copy = pltpu.make_async_remote_copy(
            src_ref=x_ref.at[source_x, source_y],
            dst_ref=padded.at[target_x, target_y],
            send_sem=send_sem.at[k],
            recv_sem=recv_sem.at[k],
            device_id=(index_x + a, index_y + b),
            device_id_type=mesh_ids,
        )
        copies.append(copy)
        pl.when(inside(index_x + a, index_y + b))(copy.start)
    for k, (a, b) in enumerate(steps):
        source_x, target_x = ranges(a, size_x)
        source_y, target_y = ranges(b, size_y)

        @pl.when(jnp.logical_not(inside(index_x - a, index_y - b)))
        def _():
            piece = padded.at[target_x, target_y]
            piece[...] = jnp.zeros(piece.shape, piece.dtype)
    for k, (a, b) in enumerate(steps):
        pl.when(inside(index_x + a, index_y + b))(copies[k].wait_send)
        pl.when(inside(index_x - a, index_y - b))(copies[k].wait_recv)
    center.wait()
    for tile_x in range(size_x):
        for tile_y in range(size_y):
            total = x_ref[tile_x, tile_y].astype(jnp.float32)
            for k, (a, b) in enumerate(steps):
                total += jnp.dot(
                    padded[1 + tile_x + a, 1 + tile_y + b],
                    mixing_ref[k],
                    preferred_element_type=jnp.float32,
                )
            o_ref[tile_x, tile_y] = total.astype(o_ref.dtype)


def mix_tiles(block, mixing):
    count_x = lax.axis_size("tx")
    count_y = lax.axis_size("ty")
    shape = (block.shape[0] + 2, block.shape[1] + 2) + block.shape[2:]
    return pl.pallas_call(
        functools.partial(mix_kernel, count_x, count_y),
        out_shape=jax.ShapeDtypeStruct(block.shape, block.dtype),
        in_specs=[pl.BlockSpec(memory_space=pltpu.VMEM)] * 2,
        out_specs=pl.BlockSpec(memory_space=pltpu.VMEM),
        scratch_shapes=[
            pltpu.VMEM(shape, block.dtype),
            pltpu.SemaphoreType.DMA((8,)),
            pltpu.SemaphoreType.DMA((8,)),
            pltpu.SemaphoreType.DMA,
        ],
        compiler_params=pltpu.CompilerParams(collective_id=0, has_side_effects=True),
    )(block, mixing)


def unit_heads(projected, head_count):
    pieces = projected.reshape(
        projected.shape[:-1] + (head_count, projected.shape[-1] // head_count)
    )
    magnitude = jnp.sqrt(jnp.sum(pieces * pieces, axis=-1, keepdims=True) + epsilon)
    return (pieces / magnitude).reshape(projected.shape).astype(jnp.bfloat16)


def unit_rows(projected, head_width):
    lanes = lax.broadcasted_iota(jnp.int32, projected.shape, projected.ndim - 1)
    squares = projected * projected
    magnitude = jnp.zeros_like(projected)
    for head_id in range(projected.shape[-1] // head_width):
        in_head = (lanes >= head_id * head_width) & (lanes < (head_id + 1) * head_width)
        total = jnp.sum(jnp.where(in_head, squares, 0.0), axis=-1, keepdims=True)
        magnitude = jnp.where(in_head, jnp.sqrt(total + epsilon), magnitude)
    return (projected / magnitude).astype(jnp.bfloat16)


def summary_kernel(rows_ref, column_mask_ref, lane_mask_ref, inducing_ref, proj_ref, o_ref):
    width = rows_ref.shape[1]
    head_width = width // HEADS
    tiles = column_mask_ref.shape[1]
    rows = rows_ref[...]
    queries = unit_rows(
        jnp.dot(inducing_ref[...], proj_ref[0], preferred_element_type=jnp.float32), head_width
    )
    keys = unit_rows(jnp.dot(rows, proj_ref[1], preferred_element_type=jnp.float32), head_width)
    values = jnp.dot(rows, proj_ref[2], preferred_element_type=jnp.float32).astype(jnp.bfloat16)
    column_mask = column_mask_ref[...]
    lane_mask = lane_mask_ref[...]
    heads_out = []
    for head_id in range(HEADS):
        lower = head_id * head_width
        upper = lower + head_width
        scores = lax.dot_general(
            queries[:, lower:upper],
            keys[:, lower:upper],
            (((1,), (1,)), ((), ())),
            preferred_element_type=jnp.float32,
        )
        weights = jnp.exp(sharpness * scores)
        rounded = weights.astype(jnp.bfloat16)
        head_values = values[:, lower:upper]
        masked = jnp.concatenate(
            [head_values * column_mask[:, t : t + 1] for t in range(tiles)], axis=1
        )
        numer = jnp.dot(rounded, masked, preferred_element_type=jnp.float32)
        per_tile = []
        for t in range(tiles):
            totals = jnp.sum(weights * lane_mask[t : t + 1, :], axis=1, keepdims=True)
            per_tile.append(numer[:, t * head_width : (t + 1) * head_width] / totals)
        heads_out.append(per_tile)
    inducing = inducing_ref[...].astype(jnp.float32)
    for t in range(tiles):
        attended = jnp.concatenate([heads_out[h][t] for h in range(HEADS)], axis=1)
        attended = attended.astype(jnp.bfloat16)
        o_ref[t] = (
            inducing + jnp.dot(attended, proj_ref[3], preferred_element_type=jnp.float32)
        ).astype(o_ref.dtype)


def summarize(rows, row_mask, inducing, proj):
    tiles = row_mask.shape[1]
    return pl.pallas_call(
        summary_kernel,
        out_shape=jax.ShapeDtypeStruct((tiles,) + inducing.shape, jnp.bfloat16),
        in_specs=[pl.BlockSpec(memory_space=pltpu.VMEM)] * 5,
        out_specs=pl.BlockSpec(memory_space=pltpu.VMEM),
    )(rows, row_mask.astype(jnp.bfloat16), row_mask.T, inducing, proj)


def finish_kernel(rows_ref, row_tile_ref, mixture_ref, proj_ref, o_ref):
    width = rows_ref.shape[1]
    head_width = width // HEADS
    keys_per_tile = mixture_ref.shape[0] // TLX // TLY
    mixture = mixture_ref[...]
    keys = unit_rows(jnp.dot(mixture, proj_ref[1], preferred_element_type=jnp.float32), head_width)
    values = jnp.dot(mixture, proj_ref[2], preferred_element_type=jnp.float32).astype(jnp.bfloat16)
    rows = rows_ref[...]
    queries = unit_rows(jnp.dot(rows, proj_ref[0], preferred_element_type=jnp.float32), head_width)
    key_tile = lax.broadcasted_iota(jnp.int32, (rows.shape[0], mixture.shape[0]), 1) // keys_per_tile
    own = key_tile == row_tile_ref[...]
    heads_out = []
    for head_id in range(HEADS):
        lower = head_id * head_width
        upper = lower + head_width
        scores = lax.dot_general(
            queries[:, lower:upper],
            keys[:, lower:upper],
            (((1,), (1,)), ((), ())),
            preferred_element_type=jnp.float32,
        )
        weights = jnp.where(own, jnp.exp(sharpness * scores), 0.0)
        totals = jnp.sum(weights, axis=1, keepdims=True)
        numer = jnp.dot(
            weights.astype(jnp.bfloat16), values[:, lower:upper], preferred_element_type=jnp.float32
        )
        heads_out.append(numer / totals)
    attended = jnp.concatenate(heads_out, axis=1).astype(jnp.bfloat16)
    o_ref[...] = (
        rows.astype(jnp.float32) + jnp.dot(attended, proj_ref[3], preferred_element_type=jnp.float32)
    ).astype(o_ref.dtype)


def finish(rows, row_tile, mixture, proj, block):
    count = rows.shape[0]
    full = lambda shape: pl.BlockSpec(shape, lambda i: (0,) * len(shape))
    return pl.pallas_call(
        finish_kernel,
        out_shape=jax.ShapeDtypeStruct(rows.shape, jnp.bfloat16),
        grid=(count // block,),
        in_specs=[
            pl.BlockSpec((block, rows.shape[1]), lambda i: (i, 0)),
            pl.BlockSpec((block, 1), lambda i: (i, 0)),
            full(mixture.shape),
            full(proj.shape),
        ],
        out_specs=pl.BlockSpec((block, rows.shape[1]), lambda i: (i, 0)),
    )(rows, row_tile.reshape(count, 1), mixture, proj)


def body(
    points,
    embed_weight,
    inner_weights,
    output_weight,
    counts,
    point_order,
    inducing,
    first_proj,
    second_proj,
    mixing,
):
    along_x = lax.axis_size("tx")
    along_y = lax.axis_size("ty")
    devices = along_x * along_y
    index_x = lax.axis_index("tx")
    index_y = lax.axis_index("ty")
    own_index = index_x * along_y + index_y
    point_count = points.shape[0]
    per_device = TLX * TLY
    width = output_weight.shape[1]
    quota = point_count // devices
    band = quota * along_y
    head_width = width // HEADS
    inducing_count = inducing.shape[0]

    features = point_mlp(points, embed_weight, inner_weights, output_weight, 512)

    own_counts = lax.dynamic_index_in_dim(counts, own_index, 0, keepdims=False)
    own_offsets = jnp.cumsum(own_counts) - own_counts
    grid_counts = own_counts.reshape(along_x, TLX, along_y, TLY)
    grid_offsets = own_offsets.reshape(along_x, TLX, along_y, TLY)
    band_start = grid_offsets[:, 0, 0, 0][:, None]
    first_len = grid_counts[:, 0, :, 0] + grid_counts[:, 0, :, 1]
    first_start = grid_offsets[:, 0, :, 0] - band_start
    second_start = grid_offsets[:, 1, :, 0] - band_start
    slot_ids = jnp.arange(quota, dtype=jnp.int32)
    local_pos = jnp.where(
        slot_ids[None, None, :] < first_len[:, :, None],
        first_start[:, :, None] + slot_ids[None, None, :],
        second_start[:, :, None] + slot_ids[None, None, :] - first_len[:, :, None],
    ).reshape(along_x, band)
    send_pos = (local_pos + band_start).reshape(-1)
    order = point_order[0]
    outgoing = move_rows(gather_kernel, send_pos, order, features)
    outgoing = outgoing.reshape(devices, quota, width)
    arrived = lax.all_to_all(outgoing, ("tx", "ty"), split_axis=0, concat_axis=0, tiled=True)
    all_rows = arrived.reshape(devices * quota, width)

    inbound = counts.reshape(devices, along_x, TLX, along_y, TLY)
    inbound = lax.dynamic_index_in_dim(inbound, index_x, 1, keepdims=False)
    inbound = lax.dynamic_index_in_dim(inbound, index_y, 2, keepdims=False)
    inbound = inbound.reshape(devices, per_device)
    through = jnp.cumsum(inbound, axis=1)
    row_tile = jnp.sum(
        (slot_ids[None, :, None] >= through[:, None, : per_device - 1]).astype(jnp.int32), axis=2
    ).reshape(-1)
    tile_ids = jnp.arange(per_device, dtype=jnp.int32)
    row_mask = (row_tile[:, None] == tile_ids[None, :]).astype(jnp.float32)

    summary = summarize(all_rows, row_mask, inducing, first_proj)
    tile_grid = summary.reshape(TLX, TLY, inducing_count, width)
    mixture = mix_tiles(tile_grid, mixing)
    mixture = mixture.astype(jnp.bfloat16).reshape(per_device * inducing_count, width)

    result = finish(all_rows, row_tile, mixture, second_proj, 512)

    coming = lax.all_to_all(
        result.reshape(devices, quota, width), ("tx", "ty"), split_axis=0, concat_axis=0, tiled=True
    )
    returned = move_rows(
        scatter_kernel, send_pos, order, coming.reshape(point_count, width)
    )
    return returned


def solution(mesh):
    placed = (P(("tx", "ty"), None), P(), P(), P(), P(), P(("tx", "ty"), None), P(), P(), P(), P())
    return jax.shard_map(
        body, mesh=mesh, in_specs=placed, out_specs=P(("tx", "ty"), None), check_vma=False
    )
```

```python
import functools

import jax
import jax.numpy as jnp
from jax import lax
from jax.experimental import pallas as pl
from jax.experimental.pallas import tpu as pltpu
from jax.sharding import PartitionSpec as P

HEADS = 2
TLX = 2
TLY = 2


sharpness = 32.0
epsilon = 1e-06
neighbour_steps = ((-1, -1), (-1, 0), (-1, 1), (0, -1), (0, 1), (1, -1), (1, 0), (1, 1))


def mlp_kernel(x_ref, w1_ref, w2_ref, w3_ref, o_ref):
    def silu(v):
        return v / (1.0 + jnp.exp(-v))

    h = silu(jnp.dot(x_ref[...], w1_ref[...], preferred_element_type=jnp.float32))
    h = h.astype(jnp.bfloat16)
    for layer_id in range(w2_ref.shape[0]):
        h = silu(jnp.dot(h, w2_ref[layer_id], preferred_element_type=jnp.float32))
        h = h.astype(jnp.bfloat16)
    o_ref[...] = jnp.dot(h, w3_ref[...], preferred_element_type=jnp.float32).astype(o_ref.dtype)


def point_mlp(x, w1, w2, w3, block):
    rows = x.shape[0]
    full = lambda shape: pl.BlockSpec(shape, lambda i: (0,) * len(shape))
    return pl.pallas_call(
        mlp_kernel,
        out_shape=jax.ShapeDtypeStruct((rows, w3.shape[1]), jnp.bfloat16),
        grid=(rows // block,),
        in_specs=[
            pl.BlockSpec((block, x.shape[1]), lambda i: (i, 0)),
            full(w1.shape),
            full(w2.shape),
            full(w3.shape),
        ],
        out_specs=pl.BlockSpec((block, w3.shape[1]), lambda i: (i, 0)),
    )(x, w1, w2, w3)


def gather_kernel(unroll, pos_ref, order_ref, x_ref, o_ref, rows_in, rows_out):
    rows_in[...] = x_ref[...].astype(jnp.float32)

    def body(step, carry):
        for lane in range(unroll):
            row = step * unroll + lane
            source = order_ref[pos_ref[row]]
            rows_out[pl.ds(row, 1), :] = rows_in[pl.ds(source, 1), :]
        return carry

    lax.fori_loop(0, o_ref.shape[0] // unroll, body, 0)
    o_ref[...] = rows_out[...].astype(o_ref.dtype)


def scatter_kernel(unroll, pos_ref, order_ref, x_ref, o_ref, rows_in, rows_out):
    rows_in[...] = x_ref[...].astype(jnp.float32)

    def body(step, carry):
        for lane in range(unroll):
            row = step * unroll + lane
            target = order_ref[pos_ref[row]]
            rows_out[pl.ds(target, 1), :] = rows_in[pl.ds(row, 1), :]
        return carry

    lax.fori_loop(0, x_ref.shape[0] // unroll, body, 0)
    o_ref[...] = rows_out[...].astype(o_ref.dtype)


def move_rows(kernel, pos, order, x):
    return pl.pallas_call(
        functools.partial(kernel, 8),
        out_shape=jax.ShapeDtypeStruct(x.shape, jnp.bfloat16),
        in_specs=[
            pl.BlockSpec(memory_space=pltpu.SMEM),
            pl.BlockSpec(memory_space=pltpu.SMEM),
            pl.BlockSpec(memory_space=pltpu.VMEM),
        ],
        out_specs=pl.BlockSpec(memory_space=pltpu.VMEM),
        scratch_shapes=[pltpu.VMEM(x.shape, jnp.float32), pltpu.VMEM(x.shape, jnp.float32)],
    )(pos, order, x)


def mix_kernel(count_x, count_y, x_ref, mixing_ref, o_ref, padded, send_sem, recv_sem, local_sem):
    index_x = lax.axis_index("tx")
    index_y = lax.axis_index("ty")
    size_x, size_y = x_ref.shape[0], x_ref.shape[1]
    mesh_ids = pl.DeviceIdType.MESH
    steps = [(a, b) for a in (-1, 0, 1) for b in (-1, 0, 1) if (a, b) != (0, 0)]

    def inside(px, py):
        return (px >= 0) & (px < count_x) & (py >= 0) & (py < count_y)

    def ranges(step, size):
        if step == 1:
            return pl.ds(size - 1, 1), pl.ds(0, 1)
        if step == -1:
            return pl.ds(0, 1), pl.ds(size + 1, 1)
        return pl.ds(0, size), pl.ds(1, size)

    barrier = pltpu.get_barrier_semaphore()
    for a, b in steps:
        @pl.when(inside(index_x + a, index_y + b))
        def _():
            pl.semaphore_signal(
                barrier, 1, device_id=(index_x + a, index_y + b), device_id_type=mesh_ids
            )
    peers = sum(inside(index_x + a, index_y + b).astype(jnp.int32) for a, b in steps)
    pl.semaphore_wait(barrier, peers)

    center = pltpu.make_async_copy(
        x_ref, padded.at[pl.ds(1, size_x), pl.ds(1, size_y)], local_sem
    )
    center.start()
    copies = []
    for k, (a, b) in enumerate(steps):
        source_x, target_x = ranges(a, size_x)
        source_y, target_y = ranges(b, size_y)
        copy = pltpu.make_async_remote_copy(
            src_ref=x_ref.at[source_x, source_y],
            dst_ref=padded.at[target_x, target_y],
            send_sem=send_sem.at[k],
            recv_sem=recv_sem.at[k],
            device_id=(index_x + a, index_y + b),
            device_id_type=mesh_ids,
        )
        copies.append(copy)
        pl.when(inside(index_x + a, index_y + b))(copy.start)
    for k, (a, b) in enumerate(steps):
        source_x, target_x = ranges(a, size_x)
        source_y, target_y = ranges(b, size_y)

        @pl.when(jnp.logical_not(inside(index_x - a, index_y - b)))
        def _():
            piece = padded.at[target_x, target_y]
            piece[...] = jnp.zeros(piece.shape, piece.dtype)
    for k, (a, b) in enumerate(steps):
        pl.when(inside(index_x + a, index_y + b))(copies[k].wait_send)
        pl.when(inside(index_x - a, index_y - b))(copies[k].wait_recv)
    center.wait()
    for tile_x in range(size_x):
        for tile_y in range(size_y):
            total = x_ref[tile_x, tile_y].astype(jnp.float32)
            for k, (a, b) in enumerate(steps):
                total += jnp.dot(
                    padded[1 + tile_x + a, 1 + tile_y + b],
                    mixing_ref[k],
                    preferred_element_type=jnp.float32,
                )
            o_ref[tile_x, tile_y] = total.astype(o_ref.dtype)


def mix_tiles(block, mixing):
    count_x = lax.axis_size("tx")
    count_y = lax.axis_size("ty")
    shape = (block.shape[0] + 2, block.shape[1] + 2) + block.shape[2:]
    return pl.pallas_call(
        functools.partial(mix_kernel, count_x, count_y),
        out_shape=jax.ShapeDtypeStruct(block.shape, block.dtype),
        in_specs=[pl.BlockSpec(memory_space=pltpu.VMEM)] * 2,
        out_specs=pl.BlockSpec(memory_space=pltpu.VMEM),
        scratch_shapes=[
            pltpu.VMEM(shape, block.dtype),
            pltpu.SemaphoreType.DMA((8,)),
            pltpu.SemaphoreType.DMA((8,)),
            pltpu.SemaphoreType.DMA,
        ],
        compiler_params=pltpu.CompilerParams(collective_id=0, has_side_effects=True),
    )(block, mixing)


def unit_heads(projected, head_count):
    pieces = projected.reshape(
        projected.shape[:-1] + (head_count, projected.shape[-1] // head_count)
    )
    magnitude = jnp.sqrt(jnp.sum(pieces * pieces, axis=-1, keepdims=True) + epsilon)
    return (pieces / magnitude).reshape(projected.shape).astype(jnp.bfloat16)


def unit_rows(projected, head_width):
    lanes = lax.broadcasted_iota(jnp.int32, projected.shape, projected.ndim - 1)
    squares = projected * projected
    magnitude = jnp.zeros_like(projected)
    for head_id in range(projected.shape[-1] // head_width):
        in_head = (lanes >= head_id * head_width) & (lanes < (head_id + 1) * head_width)
        total = jnp.sum(jnp.where(in_head, squares, 0.0), axis=-1, keepdims=True)
        magnitude = jnp.where(in_head, jnp.sqrt(total + epsilon), magnitude)
    return (projected / magnitude).astype(jnp.bfloat16)


def summary_kernel(rows_ref, column_mask_ref, lane_mask_ref, inducing_ref, proj_ref, o_ref):
    width = rows_ref.shape[1]
    head_width = width // HEADS
    tiles = column_mask_ref.shape[1]
    rows = rows_ref[...]
    queries = unit_rows(
        jnp.dot(inducing_ref[...], proj_ref[0], preferred_element_type=jnp.float32), head_width
    )
    keys = unit_rows(jnp.dot(rows, proj_ref[1], preferred_element_type=jnp.float32), head_width)
    values = jnp.dot(rows, proj_ref[2], preferred_element_type=jnp.float32).astype(jnp.bfloat16)
    column_mask = column_mask_ref[...]
    lane_mask = lane_mask_ref[...]
    heads_out = []
    for head_id in range(HEADS):
        lower = head_id * head_width
        upper = lower + head_width
        scores = lax.dot_general(
            queries[:, lower:upper],
            keys[:, lower:upper],
            (((1,), (1,)), ((), ())),
            preferred_element_type=jnp.float32,
        )
        weights = jnp.exp(sharpness * scores)
        rounded = weights.astype(jnp.bfloat16)
        head_values = values[:, lower:upper]
        masked = jnp.concatenate(
            [head_values * column_mask[:, t : t + 1] for t in range(tiles)], axis=1
        )
        numer = jnp.dot(rounded, masked, preferred_element_type=jnp.float32)
        per_tile = []
        for t in range(tiles):
            totals = jnp.sum(weights * lane_mask[t : t + 1, :], axis=1, keepdims=True)
            per_tile.append(numer[:, t * head_width : (t + 1) * head_width] / totals)
        heads_out.append(per_tile)
    inducing = inducing_ref[...].astype(jnp.float32)
    for t in range(tiles):
        attended = jnp.concatenate([heads_out[h][t] for h in range(HEADS)], axis=1)
        attended = attended.astype(jnp.bfloat16)
        o_ref[t] = (
            inducing + jnp.dot(attended, proj_ref[3], preferred_element_type=jnp.float32)
        ).astype(o_ref.dtype)


def summarize(rows, row_mask, inducing, proj):
    tiles = row_mask.shape[1]
    return pl.pallas_call(
        summary_kernel,
        out_shape=jax.ShapeDtypeStruct((tiles,) + inducing.shape, jnp.bfloat16),
        in_specs=[pl.BlockSpec(memory_space=pltpu.VMEM)] * 5,
        out_specs=pl.BlockSpec(memory_space=pltpu.VMEM),
    )(rows, row_mask.astype(jnp.bfloat16), row_mask.T, inducing, proj)


def finish_kernel(rows_ref, row_tile_ref, mixture_ref, proj_ref, o_ref):
    width = rows_ref.shape[1]
    head_width = width // HEADS
    keys_per_tile = mixture_ref.shape[0] // TLX // TLY
    mixture = mixture_ref[...]
    keys = unit_rows(jnp.dot(mixture, proj_ref[1], preferred_element_type=jnp.float32), head_width)
    values = jnp.dot(mixture, proj_ref[2], preferred_element_type=jnp.float32).astype(jnp.bfloat16)
    rows = rows_ref[...]
    queries = unit_rows(jnp.dot(rows, proj_ref[0], preferred_element_type=jnp.float32), head_width)
    row_tile = row_tile_ref[...]
    tiles = mixture.shape[0] // keys_per_tile
    heads_out = []
    for head_id in range(HEADS):
        lower = head_id * head_width
        upper = lower + head_width
        scores = lax.dot_general(
            queries[:, lower:upper],
            keys[:, lower:upper],
            (((1,), (1,)), ((), ())),
            preferred_element_type=jnp.float32,
        )
        own_scores = scores[:, :keys_per_tile]
        for t in range(1, tiles):
            own_scores = jnp.where(
                row_tile == t, scores[:, t * keys_per_tile : (t + 1) * keys_per_tile], own_scores
            )
        weights = jnp.exp(sharpness * own_scores)
        totals = jnp.sum(weights, axis=1, keepdims=True)
        rounded = weights.astype(jnp.bfloat16)
        numer = jnp.zeros((rows.shape[0], head_width), jnp.float32)
        for t in range(tiles):
            numer += jnp.dot(
                jnp.where(row_tile == t, rounded, jnp.zeros_like(rounded)),
                values[t * keys_per_tile : (t + 1) * keys_per_tile, lower:upper],
                preferred_element_type=jnp.float32,
            )
        heads_out.append(numer / totals)
    attended = jnp.concatenate(heads_out, axis=1).astype(jnp.bfloat16)
    o_ref[...] = (
        rows.astype(jnp.float32) + jnp.dot(attended, proj_ref[3], preferred_element_type=jnp.float32)
    ).astype(o_ref.dtype)


def finish(rows, row_tile, mixture, proj, block):
    count = rows.shape[0]
    full = lambda shape: pl.BlockSpec(shape, lambda i: (0,) * len(shape))
    return pl.pallas_call(
        finish_kernel,
        out_shape=jax.ShapeDtypeStruct(rows.shape, jnp.bfloat16),
        grid=(count // block,),
        in_specs=[
            pl.BlockSpec((block, rows.shape[1]), lambda i: (i, 0)),
            pl.BlockSpec((block, 1), lambda i: (i, 0)),
            full(mixture.shape),
            full(proj.shape),
        ],
        out_specs=pl.BlockSpec((block, rows.shape[1]), lambda i: (i, 0)),
    )(rows, row_tile.reshape(count, 1), mixture, proj)


def body(
    points,
    embed_weight,
    inner_weights,
    output_weight,
    counts,
    point_order,
    inducing,
    first_proj,
    second_proj,
    mixing,
):
    along_x = lax.axis_size("tx")
    along_y = lax.axis_size("ty")
    devices = along_x * along_y
    index_x = lax.axis_index("tx")
    index_y = lax.axis_index("ty")
    own_index = index_x * along_y + index_y
    point_count = points.shape[0]
    per_device = TLX * TLY
    width = output_weight.shape[1]
    quota = point_count // devices
    band = quota * along_y
    head_width = width // HEADS
    inducing_count = inducing.shape[0]

    features = point_mlp(points, embed_weight, inner_weights, output_weight, 512)

    own_counts = lax.dynamic_index_in_dim(counts, own_index, 0, keepdims=False)
    own_offsets = jnp.cumsum(own_counts) - own_counts
    grid_counts = own_counts.reshape(along_x, TLX, along_y, TLY)
    grid_offsets = own_offsets.reshape(along_x, TLX, along_y, TLY)
    band_start = grid_offsets[:, 0, 0, 0][:, None]
    first_len = grid_counts[:, 0, :, 0] + grid_counts[:, 0, :, 1]
    first_start = grid_offsets[:, 0, :, 0] - band_start
    second_start = grid_offsets[:, 1, :, 0] - band_start
    slot_ids = jnp.arange(quota, dtype=jnp.int32)
    local_pos = jnp.where(
        slot_ids[None, None, :] < first_len[:, :, None],
        first_start[:, :, None] + slot_ids[None, None, :],
        second_start[:, :, None] + slot_ids[None, None, :] - first_len[:, :, None],
    ).reshape(along_x, band)
    send_pos = (local_pos + band_start).reshape(-1)
    order = point_order[0]
    outgoing = move_rows(gather_kernel, send_pos, order, features)
    outgoing = outgoing.reshape(devices, quota, width)
    arrived = lax.all_to_all(outgoing, ("tx", "ty"), split_axis=0, concat_axis=0, tiled=True)
    all_rows = arrived.reshape(devices * quota, width)

    inbound = counts.reshape(devices, along_x, TLX, along_y, TLY)
    inbound = lax.dynamic_index_in_dim(inbound, index_x, 1, keepdims=False)
    inbound = lax.dynamic_index_in_dim(inbound, index_y, 2, keepdims=False)
    inbound = inbound.reshape(devices, per_device)
    through = jnp.cumsum(inbound, axis=1)
    row_tile = jnp.sum(
        (slot_ids[None, :, None] >= through[:, None, : per_device - 1]).astype(jnp.int32), axis=2
    ).reshape(-1)
    tile_ids = jnp.arange(per_device, dtype=jnp.int32)
    row_mask = (row_tile[:, None] == tile_ids[None, :]).astype(jnp.float32)

    summary = summarize(all_rows, row_mask, inducing, first_proj)
    tile_grid = summary.reshape(TLX, TLY, inducing_count, width)
    mixture = mix_tiles(tile_grid, mixing)
    mixture = mixture.astype(jnp.bfloat16).reshape(per_device * inducing_count, width)

    result = finish(all_rows, row_tile, mixture, second_proj, 512)

    coming = lax.all_to_all(
        result.reshape(devices, quota, width), ("tx", "ty"), split_axis=0, concat_axis=0, tiled=True
    )
    returned = move_rows(
        scatter_kernel, send_pos, order, coming.reshape(point_count, width)
    )
    return returned


def solution(mesh):
    placed = (P(("tx", "ty"), None), P(), P(), P(), P(), P(("tx", "ty"), None), P(), P(), P(), P())
    return jax.shard_map(
        body, mesh=mesh, in_specs=placed, out_specs=P(("tx", "ty"), None), check_vma=False
    )
```

```python
import functools

import jax
import jax.numpy as jnp
from jax import lax
from jax.experimental import pallas as pl
from jax.experimental.pallas import tpu as pltpu
from jax.sharding import PartitionSpec as P

HEADS = 2
TLX = 2
TLY = 2


sharpness = 32.0
epsilon = 1e-06
neighbour_steps = ((-1, -1), (-1, 0), (-1, 1), (0, -1), (0, 1), (1, -1), (1, 0), (1, 1))


def mlp_kernel(x_ref, w1_ref, w2_ref, w3_ref, o_ref):
    def silu(v):
        return v / (1.0 + jnp.exp(-v))

    h = silu(jnp.dot(x_ref[...], w1_ref[...], preferred_element_type=jnp.float32))
    h = h.astype(jnp.bfloat16)
    for layer_id in range(w2_ref.shape[0]):
        h = silu(jnp.dot(h, w2_ref[layer_id], preferred_element_type=jnp.float32))
        h = h.astype(jnp.bfloat16)
    o_ref[...] = jnp.dot(h, w3_ref[...], preferred_element_type=jnp.float32).astype(o_ref.dtype)


def point_mlp(x, w1, w2, w3, block):
    rows = x.shape[0]
    full = lambda shape: pl.BlockSpec(shape, lambda i: (0,) * len(shape))
    return pl.pallas_call(
        mlp_kernel,
        out_shape=jax.ShapeDtypeStruct((rows, w3.shape[1]), jnp.bfloat16),
        grid=(rows // block,),
        in_specs=[
            pl.BlockSpec((block, x.shape[1]), lambda i: (i, 0)),
            full(w1.shape),
            full(w2.shape),
            full(w3.shape),
        ],
        out_specs=pl.BlockSpec((block, w3.shape[1]), lambda i: (i, 0)),
    )(x, w1, w2, w3)


def gather_kernel(unroll, pos_ref, order_ref, x_ref, o_ref, rows_in, rows_out):
    rows_in[...] = x_ref[...].astype(jnp.float32)

    def body(step, carry):
        for lane in range(unroll):
            row = step * unroll + lane
            source = order_ref[pos_ref[row]]
            rows_out[pl.ds(row, 1), :] = rows_in[pl.ds(source, 1), :]
        return carry

    lax.fori_loop(0, o_ref.shape[0] // unroll, body, 0)
    o_ref[...] = rows_out[...].astype(o_ref.dtype)


def scatter_kernel(unroll, pos_ref, order_ref, x_ref, o_ref, rows_in, rows_out):
    rows_in[...] = x_ref[...].astype(jnp.float32)

    def body(step, carry):
        for lane in range(unroll):
            row = step * unroll + lane
            target = order_ref[pos_ref[row]]
            rows_out[pl.ds(target, 1), :] = rows_in[pl.ds(row, 1), :]
        return carry

    lax.fori_loop(0, x_ref.shape[0] // unroll, body, 0)
    o_ref[...] = rows_out[...].astype(o_ref.dtype)


def move_rows(kernel, pos, order, x):
    return pl.pallas_call(
        functools.partial(kernel, 8),
        out_shape=jax.ShapeDtypeStruct(x.shape, jnp.bfloat16),
        in_specs=[
            pl.BlockSpec(memory_space=pltpu.SMEM),
            pl.BlockSpec(memory_space=pltpu.SMEM),
            pl.BlockSpec(memory_space=pltpu.VMEM),
        ],
        out_specs=pl.BlockSpec(memory_space=pltpu.VMEM),
        scratch_shapes=[pltpu.VMEM(x.shape, jnp.float32), pltpu.VMEM(x.shape, jnp.float32)],
    )(pos, order, x)


def mix_kernel(count_x, count_y, x_ref, mixing_ref, o_ref, padded, send_sem, recv_sem, local_sem):
    index_x = lax.axis_index("tx")
    index_y = lax.axis_index("ty")
    size_x, size_y = x_ref.shape[0], x_ref.shape[1]
    mesh_ids = pl.DeviceIdType.MESH
    steps = [(a, b) for a in (-1, 0, 1) for b in (-1, 0, 1) if (a, b) != (0, 0)]

    def inside(px, py):
        return (px >= 0) & (px < count_x) & (py >= 0) & (py < count_y)

    def ranges(step, size):
        if step == 1:
            return pl.ds(size - 1, 1), pl.ds(0, 1)
        if step == -1:
            return pl.ds(0, 1), pl.ds(size + 1, 1)
        return pl.ds(0, size), pl.ds(1, size)

    barrier = pltpu.get_barrier_semaphore()
    for a, b in steps:
        @pl.when(inside(index_x + a, index_y + b))
        def _():
            pl.semaphore_signal(
                barrier, 1, device_id=(index_x + a, index_y + b), device_id_type=mesh_ids
            )
    peers = sum(inside(index_x + a, index_y + b).astype(jnp.int32) for a, b in steps)
    pl.semaphore_wait(barrier, peers)

    center = pltpu.make_async_copy(
        x_ref, padded.at[pl.ds(1, size_x), pl.ds(1, size_y)], local_sem
    )
    center.start()
    copies = []
    for k, (a, b) in enumerate(steps):
        source_x, target_x = ranges(a, size_x)
        source_y, target_y = ranges(b, size_y)
        copy = pltpu.make_async_remote_copy(
            src_ref=x_ref.at[source_x, source_y],
            dst_ref=padded.at[target_x, target_y],
            send_sem=send_sem.at[k],
            recv_sem=recv_sem.at[k],
            device_id=(index_x + a, index_y + b),
            device_id_type=mesh_ids,
        )
        copies.append(copy)
        pl.when(inside(index_x + a, index_y + b))(copy.start)
    for k, (a, b) in enumerate(steps):
        source_x, target_x = ranges(a, size_x)
        source_y, target_y = ranges(b, size_y)

        @pl.when(jnp.logical_not(inside(index_x - a, index_y - b)))
        def _():
            piece = padded.at[target_x, target_y]
            piece[...] = jnp.zeros(piece.shape, piece.dtype)
    for k, (a, b) in enumerate(steps):
        pl.when(inside(index_x + a, index_y + b))(copies[k].wait_send)
        pl.when(inside(index_x - a, index_y - b))(copies[k].wait_recv)
    center.wait()
    for tile_x in range(size_x):
        for tile_y in range(size_y):
            total = x_ref[tile_x, tile_y].astype(jnp.float32)
            for k, (a, b) in enumerate(steps):
                total += jnp.dot(
                    padded[1 + tile_x + a, 1 + tile_y + b],
                    mixing_ref[k],
                    preferred_element_type=jnp.float32,
                )
            o_ref[tile_x, tile_y] = total.astype(o_ref.dtype)


def mix_tiles(block, mixing):
    count_x = lax.axis_size("tx")
    count_y = lax.axis_size("ty")
    shape = (block.shape[0] + 2, block.shape[1] + 2) + block.shape[2:]
    return pl.pallas_call(
        functools.partial(mix_kernel, count_x, count_y),
        out_shape=jax.ShapeDtypeStruct(block.shape, block.dtype),
        in_specs=[pl.BlockSpec(memory_space=pltpu.VMEM)] * 2,
        out_specs=pl.BlockSpec(memory_space=pltpu.VMEM),
        scratch_shapes=[
            pltpu.VMEM(shape, block.dtype),
            pltpu.SemaphoreType.DMA((8,)),
            pltpu.SemaphoreType.DMA((8,)),
            pltpu.SemaphoreType.DMA,
        ],
        compiler_params=pltpu.CompilerParams(collective_id=0, has_side_effects=True),
    )(block, mixing)


def unit_heads(projected, head_count):
    pieces = projected.reshape(
        projected.shape[:-1] + (head_count, projected.shape[-1] // head_count)
    )
    magnitude = jnp.sqrt(jnp.sum(pieces * pieces, axis=-1, keepdims=True) + epsilon)
    return (pieces / magnitude).reshape(projected.shape).astype(jnp.bfloat16)


def unit_rows(projected, head_width):
    lanes = lax.broadcasted_iota(jnp.int32, projected.shape, projected.ndim - 1)
    squares = projected * projected
    magnitude = jnp.zeros_like(projected)
    for head_id in range(projected.shape[-1] // head_width):
        in_head = (lanes >= head_id * head_width) & (lanes < (head_id + 1) * head_width)
        total = jnp.sum(jnp.where(in_head, squares, 0.0), axis=-1, keepdims=True)
        magnitude = jnp.where(in_head, jnp.sqrt(total + epsilon), magnitude)
    return (projected / magnitude).astype(jnp.bfloat16)


def summary_kernel(rows_ref, column_mask_ref, lane_mask_ref, inducing_ref, proj_ref, o_ref):
    width = rows_ref.shape[1]
    head_width = width // HEADS
    tiles = column_mask_ref.shape[1]
    rows = rows_ref[...]
    queries = unit_rows(
        jnp.dot(inducing_ref[...], proj_ref[0], preferred_element_type=jnp.float32), head_width
    )
    keys = unit_rows(jnp.dot(rows, proj_ref[1], preferred_element_type=jnp.float32), head_width)
    values = jnp.dot(rows, proj_ref[2], preferred_element_type=jnp.float32).astype(jnp.bfloat16)
    column_mask = column_mask_ref[...]
    lane_mask = lane_mask_ref[...]
    heads_out = []
    for head_id in range(HEADS):
        lower = head_id * head_width
        upper = lower + head_width
        scores = lax.dot_general(
            queries[:, lower:upper],
            keys[:, lower:upper],
            (((1,), (1,)), ((), ())),
            preferred_element_type=jnp.float32,
        )
        weights = jnp.exp(sharpness * scores)
        rounded = weights.astype(jnp.bfloat16)
        head_values = values[:, lower:upper]
        masked = jnp.concatenate(
            [head_values * column_mask[:, t : t + 1] for t in range(tiles)], axis=1
        )
        numer = jnp.dot(rounded, masked, preferred_element_type=jnp.float32)
        per_tile = []
        for t in range(tiles):
            totals = jnp.sum(weights * lane_mask[t : t + 1, :], axis=1, keepdims=True)
            per_tile.append(numer[:, t * head_width : (t + 1) * head_width] / totals)
        heads_out.append(per_tile)
    inducing = inducing_ref[...].astype(jnp.float32)
    for t in range(tiles):
        attended = jnp.concatenate([heads_out[h][t] for h in range(HEADS)], axis=1)
        attended = attended.astype(jnp.bfloat16)
        o_ref[t] = (
            inducing + jnp.dot(attended, proj_ref[3], preferred_element_type=jnp.float32)
        ).astype(o_ref.dtype)


def summarize(rows, row_mask, inducing, proj):
    tiles = row_mask.shape[1]
    return pl.pallas_call(
        summary_kernel,
        out_shape=jax.ShapeDtypeStruct((tiles,) + inducing.shape, jnp.bfloat16),
        in_specs=[pl.BlockSpec(memory_space=pltpu.VMEM)] * 5,
        out_specs=pl.BlockSpec(memory_space=pltpu.VMEM),
    )(rows, row_mask.astype(jnp.bfloat16), row_mask.T, inducing, proj)


def finish_kernel(rows_ref, row_tile_ref, keys_ref, values_ref, proj_ref, o_ref):
    width = rows_ref.shape[1]
    head_width = width // HEADS
    keys_per_tile = keys_ref.shape[0] // TLX // TLY
    keys = keys_ref[...]
    values = values_ref[...]
    rows = rows_ref[...]
    queries = unit_rows(jnp.dot(rows, proj_ref[0], preferred_element_type=jnp.float32), head_width)
    row_tile = row_tile_ref[...]
    tiles = keys.shape[0] // keys_per_tile
    heads_out = []
    for head_id in range(HEADS):
        lower = head_id * head_width
        upper = lower + head_width
        scores = lax.dot_general(
            queries[:, lower:upper],
            keys[:, lower:upper],
            (((1,), (1,)), ((), ())),
            preferred_element_type=jnp.float32,
        )
        own_scores = scores[:, :keys_per_tile]
        for t in range(1, tiles):
            own_scores = jnp.where(
                row_tile == t, scores[:, t * keys_per_tile : (t + 1) * keys_per_tile], own_scores
            )
        weights = jnp.exp(sharpness * own_scores)
        totals = jnp.sum(weights, axis=1, keepdims=True)
        rounded = weights.astype(jnp.bfloat16)
        numer = jnp.zeros((rows.shape[0], head_width), jnp.float32)
        for t in range(tiles):
            numer += jnp.dot(
                jnp.where(row_tile == t, rounded, jnp.zeros_like(rounded)),
                values[t * keys_per_tile : (t + 1) * keys_per_tile, lower:upper],
                preferred_element_type=jnp.float32,
            )
        heads_out.append(numer / totals)
    attended = jnp.concatenate(heads_out, axis=1).astype(jnp.bfloat16)
    o_ref[...] = (
        rows.astype(jnp.float32) + jnp.dot(attended, proj_ref[3], preferred_element_type=jnp.float32)
    ).astype(o_ref.dtype)


def finish(rows, row_tile, mixture, proj, block):
    count = rows.shape[0]
    keys = unit_heads(jnp.dot(mixture, proj[1], preferred_element_type=jnp.float32), HEADS)
    values = jnp.dot(mixture, proj[2], preferred_element_type=jnp.float32).astype(jnp.bfloat16)
    full = lambda shape: pl.BlockSpec(shape, lambda i: (0,) * len(shape))
    return pl.pallas_call(
        finish_kernel,
        out_shape=jax.ShapeDtypeStruct(rows.shape, jnp.bfloat16),
        grid=(count // block,),
        in_specs=[
            pl.BlockSpec((block, rows.shape[1]), lambda i: (i, 0)),
            pl.BlockSpec((block, 1), lambda i: (i, 0)),
            full(keys.shape),
            full(values.shape),
            full(proj.shape),
        ],
        out_specs=pl.BlockSpec((block, rows.shape[1]), lambda i: (i, 0)),
    )(rows, row_tile.reshape(count, 1), keys, values, proj)


def body(
    points,
    embed_weight,
    inner_weights,
    output_weight,
    counts,
    point_order,
    inducing,
    first_proj,
    second_proj,
    mixing,
):
    along_x = lax.axis_size("tx")
    along_y = lax.axis_size("ty")
    devices = along_x * along_y
    index_x = lax.axis_index("tx")
    index_y = lax.axis_index("ty")
    own_index = index_x * along_y + index_y
    point_count = points.shape[0]
    per_device = TLX * TLY
    width = output_weight.shape[1]
    quota = point_count // devices
    band = quota * along_y
    head_width = width // HEADS
    inducing_count = inducing.shape[0]

    features = point_mlp(points, embed_weight, inner_weights, output_weight, 512)

    own_counts = lax.dynamic_index_in_dim(counts, own_index, 0, keepdims=False)
    own_offsets = jnp.cumsum(own_counts) - own_counts
    grid_counts = own_counts.reshape(along_x, TLX, along_y, TLY)
    grid_offsets = own_offsets.reshape(along_x, TLX, along_y, TLY)
    band_start = grid_offsets[:, 0, 0, 0][:, None]
    first_len = grid_counts[:, 0, :, 0] + grid_counts[:, 0, :, 1]
    first_start = grid_offsets[:, 0, :, 0] - band_start
    second_start = grid_offsets[:, 1, :, 0] - band_start
    slot_ids = jnp.arange(quota, dtype=jnp.int32)
    local_pos = jnp.where(
        slot_ids[None, None, :] < first_len[:, :, None],
        first_start[:, :, None] + slot_ids[None, None, :],
        second_start[:, :, None] + slot_ids[None, None, :] - first_len[:, :, None],
    ).reshape(along_x, band)
    send_pos = (local_pos + band_start).reshape(-1)
    order = point_order[0]
    outgoing = move_rows(gather_kernel, send_pos, order, features)
    outgoing = outgoing.reshape(devices, quota, width)
    arrived = lax.all_to_all(outgoing, ("tx", "ty"), split_axis=0, concat_axis=0, tiled=True)
    all_rows = arrived.reshape(devices * quota, width)

    inbound = counts.reshape(devices, along_x, TLX, along_y, TLY)
    inbound = lax.dynamic_index_in_dim(inbound, index_x, 1, keepdims=False)
    inbound = lax.dynamic_index_in_dim(inbound, index_y, 2, keepdims=False)
    inbound = inbound.reshape(devices, per_device)
    through = jnp.cumsum(inbound, axis=1)
    row_tile = jnp.sum(
        (slot_ids[None, :, None] >= through[:, None, : per_device - 1]).astype(jnp.int32), axis=2
    ).reshape(-1)
    tile_ids = jnp.arange(per_device, dtype=jnp.int32)
    row_mask = (row_tile[:, None] == tile_ids[None, :]).astype(jnp.float32)

    summary = summarize(all_rows, row_mask, inducing, first_proj)
    tile_grid = summary.reshape(TLX, TLY, inducing_count, width)
    mixture = mix_tiles(tile_grid, mixing)
    mixture = mixture.astype(jnp.bfloat16).reshape(per_device * inducing_count, width)

    result = finish(all_rows, row_tile, mixture, second_proj, 512)

    coming = lax.all_to_all(
        result.reshape(devices, quota, width), ("tx", "ty"), split_axis=0, concat_axis=0, tiled=True
    )
    returned = move_rows(
        scatter_kernel, send_pos, order, coming.reshape(point_count, width)
    )
    return returned


def solution(mesh):
    placed = (P(("tx", "ty"), None), P(), P(), P(), P(), P(("tx", "ty"), None), P(), P(), P(), P())
    return jax.shard_map(
        body, mesh=mesh, in_specs=placed, out_specs=P(("tx", "ty"), None), check_vma=False
    )
```

```python
import functools

import jax
import jax.numpy as jnp
from jax import lax
from jax.experimental import pallas as pl
from jax.experimental.pallas import tpu as pltpu
from jax.sharding import PartitionSpec as P

HEADS = 2
TLX = 2
TLY = 2


sharpness = 32.0
epsilon = 1e-06
neighbour_steps = ((-1, -1), (-1, 0), (-1, 1), (0, -1), (0, 1), (1, -1), (1, 0), (1, 1))


def mlp_kernel(x_ref, w1_ref, w2_ref, w3_ref, o_ref):
    def silu(v):
        return v / (1.0 + jnp.exp(-v))

    h = silu(jnp.dot(x_ref[...], w1_ref[...], preferred_element_type=jnp.float32))
    h = h.astype(jnp.bfloat16)
    for layer_id in range(w2_ref.shape[0]):
        h = silu(jnp.dot(h, w2_ref[layer_id], preferred_element_type=jnp.float32))
        h = h.astype(jnp.bfloat16)
    o_ref[...] = jnp.dot(h, w3_ref[...], preferred_element_type=jnp.float32).astype(o_ref.dtype)


def point_mlp(x, w1, w2, w3, block):
    rows = x.shape[0]
    full = lambda shape: pl.BlockSpec(shape, lambda i: (0,) * len(shape))
    return pl.pallas_call(
        mlp_kernel,
        out_shape=jax.ShapeDtypeStruct((rows, w3.shape[1]), jnp.bfloat16),
        grid=(rows // block,),
        in_specs=[
            pl.BlockSpec((block, x.shape[1]), lambda i: (i, 0)),
            full(w1.shape),
            full(w2.shape),
            full(w3.shape),
        ],
        out_specs=pl.BlockSpec((block, w3.shape[1]), lambda i: (i, 0)),
    )(x, w1, w2, w3)


def gather_kernel(unroll, pos_ref, order_ref, x_ref, o_ref, rows_in, rows_out):
    rows_in[...] = x_ref[...].astype(jnp.float32)

    def body(step, carry):
        for lane in range(unroll):
            row = step * unroll + lane
            source = order_ref[pos_ref[row]]
            rows_out[pl.ds(row, 1), :] = rows_in[pl.ds(source, 1), :]
        return carry

    lax.fori_loop(0, o_ref.shape[0] // unroll, body, 0)
    o_ref[...] = rows_out[...].astype(o_ref.dtype)


def scatter_kernel(unroll, pos_ref, order_ref, x_ref, o_ref, rows_in, rows_out):
    rows_in[...] = x_ref[...].astype(jnp.float32)

    def body(step, carry):
        for lane in range(unroll):
            row = step * unroll + lane
            target = order_ref[pos_ref[row]]
            rows_out[pl.ds(target, 1), :] = rows_in[pl.ds(row, 1), :]
        return carry

    lax.fori_loop(0, x_ref.shape[0] // unroll, body, 0)
    o_ref[...] = rows_out[...].astype(o_ref.dtype)


def move_rows(kernel, pos, order, x):
    return pl.pallas_call(
        functools.partial(kernel, 32),
        out_shape=jax.ShapeDtypeStruct(x.shape, jnp.bfloat16),
        in_specs=[
            pl.BlockSpec(memory_space=pltpu.SMEM),
            pl.BlockSpec(memory_space=pltpu.SMEM),
            pl.BlockSpec(memory_space=pltpu.VMEM),
        ],
        out_specs=pl.BlockSpec(memory_space=pltpu.VMEM),
        scratch_shapes=[pltpu.VMEM(x.shape, jnp.float32), pltpu.VMEM(x.shape, jnp.float32)],
    )(pos, order, x)


def mix_kernel(count_x, count_y, x_ref, mixing_ref, o_ref, padded, send_sem, recv_sem, local_sem):
    index_x = lax.axis_index("tx")
    index_y = lax.axis_index("ty")
    size_x, size_y = x_ref.shape[0], x_ref.shape[1]
    mesh_ids = pl.DeviceIdType.MESH
    steps = [(a, b) for a in (-1, 0, 1) for b in (-1, 0, 1) if (a, b) != (0, 0)]

    def inside(px, py):
        return (px >= 0) & (px < count_x) & (py >= 0) & (py < count_y)

    def ranges(step, size):
        if step == 1:
            return pl.ds(size - 1, 1), pl.ds(0, 1)
        if step == -1:
            return pl.ds(0, 1), pl.ds(size + 1, 1)
        return pl.ds(0, size), pl.ds(1, size)

    barrier = pltpu.get_barrier_semaphore()
    for a, b in steps:
        @pl.when(inside(index_x + a, index_y + b))
        def _():
            pl.semaphore_signal(
                barrier, 1, device_id=(index_x + a, index_y + b), device_id_type=mesh_ids
            )
    peers = sum(inside(index_x + a, index_y + b).astype(jnp.int32) for a, b in steps)
    pl.semaphore_wait(barrier, peers)

    center = pltpu.make_async_copy(
        x_ref, padded.at[pl.ds(1, size_x), pl.ds(1, size_y)], local_sem
    )
    center.start()
    copies = []
    for k, (a, b) in enumerate(steps):
        source_x, target_x = ranges(a, size_x)
        source_y, target_y = ranges(b, size_y)
        copy = pltpu.make_async_remote_copy(
            src_ref=x_ref.at[source_x, source_y],
            dst_ref=padded.at[target_x, target_y],
            send_sem=send_sem.at[k],
            recv_sem=recv_sem.at[k],
            device_id=(index_x + a, index_y + b),
            device_id_type=mesh_ids,
        )
        copies.append(copy)
        pl.when(inside(index_x + a, index_y + b))(copy.start)
    for k, (a, b) in enumerate(steps):
        source_x, target_x = ranges(a, size_x)
        source_y, target_y = ranges(b, size_y)

        @pl.when(jnp.logical_not(inside(index_x - a, index_y - b)))
        def _():
            piece = padded.at[target_x, target_y]
            piece[...] = jnp.zeros(piece.shape, piece.dtype)
    for k, (a, b) in enumerate(steps):
        pl.when(inside(index_x + a, index_y + b))(copies[k].wait_send)
        pl.when(inside(index_x - a, index_y - b))(copies[k].wait_recv)
    center.wait()
    for tile_x in range(size_x):
        for tile_y in range(size_y):
            total = x_ref[tile_x, tile_y].astype(jnp.float32)
            for k, (a, b) in enumerate(steps):
                total += jnp.dot(
                    padded[1 + tile_x + a, 1 + tile_y + b],
                    mixing_ref[k],
                    preferred_element_type=jnp.float32,
                )
            o_ref[tile_x, tile_y] = total.astype(o_ref.dtype)


def mix_tiles(block, mixing):
    count_x = lax.axis_size("tx")
    count_y = lax.axis_size("ty")
    shape = (block.shape[0] + 2, block.shape[1] + 2) + block.shape[2:]
    return pl.pallas_call(
        functools.partial(mix_kernel, count_x, count_y),
        out_shape=jax.ShapeDtypeStruct(block.shape, block.dtype),
        in_specs=[pl.BlockSpec(memory_space=pltpu.VMEM)] * 2,
        out_specs=pl.BlockSpec(memory_space=pltpu.VMEM),
        scratch_shapes=[
            pltpu.VMEM(shape, block.dtype),
            pltpu.SemaphoreType.DMA((8,)),
            pltpu.SemaphoreType.DMA((8,)),
            pltpu.SemaphoreType.DMA,
        ],
        compiler_params=pltpu.CompilerParams(collective_id=0, has_side_effects=True),
    )(block, mixing)


def unit_heads(projected, head_count):
    pieces = projected.reshape(
        projected.shape[:-1] + (head_count, projected.shape[-1] // head_count)
    )
    magnitude = jnp.sqrt(jnp.sum(pieces * pieces, axis=-1, keepdims=True) + epsilon)
    return (pieces / magnitude).reshape(projected.shape).astype(jnp.bfloat16)


def unit_rows(projected, head_width):
    lanes = lax.broadcasted_iota(jnp.int32, projected.shape, projected.ndim - 1)
    squares = projected * projected
    magnitude = jnp.zeros_like(projected)
    for head_id in range(projected.shape[-1] // head_width):
        in_head = (lanes >= head_id * head_width) & (lanes < (head_id + 1) * head_width)
        total = jnp.sum(jnp.where(in_head, squares, 0.0), axis=-1, keepdims=True)
        magnitude = jnp.where(in_head, jnp.sqrt(total + epsilon), magnitude)
    return (projected / magnitude).astype(jnp.bfloat16)


def summary_kernel(rows_ref, column_mask_ref, lane_mask_ref, inducing_ref, proj_ref, o_ref):
    width = rows_ref.shape[1]
    head_width = width // HEADS
    tiles = column_mask_ref.shape[1]
    rows = rows_ref[...]
    queries = unit_rows(
        jnp.dot(inducing_ref[...], proj_ref[0], preferred_element_type=jnp.float32), head_width
    )
    keys = unit_rows(jnp.dot(rows, proj_ref[1], preferred_element_type=jnp.float32), head_width)
    values = jnp.dot(rows, proj_ref[2], preferred_element_type=jnp.float32).astype(jnp.bfloat16)
    column_mask = column_mask_ref[...]
    lane_mask = lane_mask_ref[...]
    heads_out = []
    for head_id in range(HEADS):
        lower = head_id * head_width
        upper = lower + head_width
        scores = lax.dot_general(
            queries[:, lower:upper],
            keys[:, lower:upper],
            (((1,), (1,)), ((), ())),
            preferred_element_type=jnp.float32,
        )
        weights = jnp.exp(sharpness * scores)
        rounded = weights.astype(jnp.bfloat16)
        head_values = values[:, lower:upper]
        masked = jnp.concatenate(
            [head_values * column_mask[:, t : t + 1] for t in range(tiles)], axis=1
        )
        numer = jnp.dot(rounded, masked, preferred_element_type=jnp.float32)
        per_tile = []
        for t in range(tiles):
            totals = jnp.sum(weights * lane_mask[t : t + 1, :], axis=1, keepdims=True)
            per_tile.append(numer[:, t * head_width : (t + 1) * head_width] / totals)
        heads_out.append(per_tile)
    inducing = inducing_ref[...].astype(jnp.float32)
    for t in range(tiles):
        attended = jnp.concatenate([heads_out[h][t] for h in range(HEADS)], axis=1)
        attended = attended.astype(jnp.bfloat16)
        o_ref[t] = (
            inducing + jnp.dot(attended, proj_ref[3], preferred_element_type=jnp.float32)
        ).astype(o_ref.dtype)


def summarize(rows, row_mask, inducing, proj):
    tiles = row_mask.shape[1]
    return pl.pallas_call(
        summary_kernel,
        out_shape=jax.ShapeDtypeStruct((tiles,) + inducing.shape, jnp.bfloat16),
        in_specs=[pl.BlockSpec(memory_space=pltpu.VMEM)] * 5,
        out_specs=pl.BlockSpec(memory_space=pltpu.VMEM),
    )(rows, row_mask.astype(jnp.bfloat16), row_mask.T, inducing, proj)


def body(
    points,
    embed_weight,
    inner_weights,
    output_weight,
    counts,
    point_order,
    inducing,
    first_proj,
    second_proj,
    mixing,
):
    along_x = lax.axis_size("tx")
    along_y = lax.axis_size("ty")
    devices = along_x * along_y
    index_x = lax.axis_index("tx")
    index_y = lax.axis_index("ty")
    own_index = index_x * along_y + index_y
    point_count = points.shape[0]
    per_device = TLX * TLY
    width = output_weight.shape[1]
    quota = point_count // devices
    band = quota * along_y
    head_width = width // HEADS
    inducing_count = inducing.shape[0]

    features = point_mlp(points, embed_weight, inner_weights, output_weight, 2048)

    own_counts = lax.dynamic_index_in_dim(counts, own_index, 0, keepdims=False)
    own_offsets = jnp.cumsum(own_counts) - own_counts
    grid_counts = own_counts.reshape(along_x, TLX, along_y, TLY)
    grid_offsets = own_offsets.reshape(along_x, TLX, along_y, TLY)
    band_start = grid_offsets[:, 0, 0, 0][:, None]
    first_len = grid_counts[:, 0, :, 0] + grid_counts[:, 0, :, 1]
    first_start = grid_offsets[:, 0, :, 0] - band_start
    second_start = grid_offsets[:, 1, :, 0] - band_start
    slot_ids = jnp.arange(quota, dtype=jnp.int32)
    local_pos = jnp.where(
        slot_ids[None, None, :] < first_len[:, :, None],
        first_start[:, :, None] + slot_ids[None, None, :],
        second_start[:, :, None] + slot_ids[None, None, :] - first_len[:, :, None],
    ).reshape(along_x, band)
    send_pos = (local_pos + band_start).reshape(-1)
    order = point_order[0]
    outgoing = move_rows(gather_kernel, send_pos, order, features)
    outgoing = outgoing.reshape(devices, quota, width)
    arrived = lax.all_to_all(outgoing, ("tx", "ty"), split_axis=0, concat_axis=0, tiled=True)
    all_rows = arrived.reshape(devices * quota, width)

    inbound = counts.reshape(devices, along_x, TLX, along_y, TLY)
    inbound = lax.dynamic_index_in_dim(inbound, index_x, 1, keepdims=False)
    inbound = lax.dynamic_index_in_dim(inbound, index_y, 2, keepdims=False)
    inbound = inbound.reshape(devices, per_device)
    through = jnp.cumsum(inbound, axis=1)
    row_tile = jnp.sum(
        (slot_ids[None, :, None] >= through[:, None, : per_device - 1]).astype(jnp.int32), axis=2
    ).reshape(-1)
    tile_ids = jnp.arange(per_device, dtype=jnp.int32)
    row_mask = (row_tile[:, None] == tile_ids[None, :]).astype(jnp.float32)

    summary = summarize(all_rows, row_mask, inducing, first_proj)
    tile_grid = summary.reshape(TLX, TLY, inducing_count, width)
    mixture = mix_tiles(tile_grid, mixing)
    mixture = mixture.astype(jnp.bfloat16).reshape(per_device * inducing_count, width)

    point_queries = unit_heads(
        jnp.dot(all_rows, second_proj[0], preferred_element_type=jnp.float32), HEADS
    )
    second_keys = unit_heads(
        jnp.dot(mixture, second_proj[1], preferred_element_type=jnp.float32), HEADS
    )
    second_values = jnp.dot(mixture, second_proj[2], preferred_element_type=jnp.float32).astype(
        jnp.bfloat16
    )
    key_mask = jnp.repeat(row_mask, inducing_count, axis=1)
    heads_out = []
    for head_id in range(HEADS):
        lower = head_id * head_width
        upper = lower + head_width
        scores = jnp.dot(
            point_queries[:, lower:upper],
            second_keys[:, lower:upper].T,
            preferred_element_type=jnp.float32,
        )
        weights = jnp.exp(sharpness * scores) * key_mask
        totals = jnp.sum(weights, axis=1, keepdims=True)
        numer = jnp.dot(
            weights.astype(jnp.bfloat16),
            second_values[:, lower:upper],
            preferred_element_type=jnp.float32,
        )
        heads_out.append(numer / totals)
    second_attended = jnp.concatenate(heads_out, axis=1).astype(jnp.bfloat16)
    result = (
        all_rows.astype(jnp.float32)
        + jnp.dot(second_attended, second_proj[3], preferred_element_type=jnp.float32)
    ).astype(jnp.bfloat16)

    coming = lax.all_to_all(
        result.reshape(devices, quota, width), ("tx", "ty"), split_axis=0, concat_axis=0, tiled=True
    )
    returned = move_rows(
        scatter_kernel, send_pos, order, coming.reshape(point_count, width)
    )
    return returned


def solution(mesh):
    placed = (P(("tx", "ty"), None), P(), P(), P(), P(), P(("tx", "ty"), None), P(), P(), P(), P())
    return jax.shard_map(
        body, mesh=mesh, in_specs=placed, out_specs=P(("tx", "ty"), None), check_vma=False
    )
```

```python
import functools

import jax
import jax.numpy as jnp
from jax import lax
from jax.experimental import pallas as pl
from jax.experimental.pallas import tpu as pltpu
from jax.sharding import PartitionSpec as P

HEADS = 2
TLX = 2
TLY = 2


sharpness = 32.0
epsilon = 1e-06
neighbour_steps = ((-1, -1), (-1, 0), (-1, 1), (0, -1), (0, 1), (1, -1), (1, 0), (1, 1))


def mlp_kernel(x_ref, w1_ref, w2_ref, w3_ref, o_ref):
    def silu(v):
        return v / (1.0 + jnp.exp(-v))

    h = silu(jnp.dot(x_ref[...], w1_ref[...], preferred_element_type=jnp.float32))
    h = h.astype(jnp.bfloat16)
    for layer_id in range(w2_ref.shape[0]):
        h = silu(jnp.dot(h, w2_ref[layer_id], preferred_element_type=jnp.float32))
        h = h.astype(jnp.bfloat16)
    o_ref[...] = jnp.dot(h, w3_ref[...], preferred_element_type=jnp.float32).astype(o_ref.dtype)


def point_mlp(x, w1, w2, w3, block):
    rows = x.shape[0]
    full = lambda shape: pl.BlockSpec(shape, lambda i: (0,) * len(shape))
    return pl.pallas_call(
        mlp_kernel,
        out_shape=jax.ShapeDtypeStruct((rows, w3.shape[1]), jnp.bfloat16),
        grid=(rows // block,),
        in_specs=[
            pl.BlockSpec((block, x.shape[1]), lambda i: (i, 0)),
            full(w1.shape),
            full(w2.shape),
            full(w3.shape),
        ],
        out_specs=pl.BlockSpec((block, w3.shape[1]), lambda i: (i, 0)),
    )(x, w1, w2, w3)


def gather_kernel(unroll, pos_ref, order_ref, x_ref, o_ref, rows_in, rows_out):
    rows_in[...] = x_ref[...].astype(jnp.float32)

    def body(step, carry):
        for lane in range(unroll):
            row = step * unroll + lane
            source = order_ref[pos_ref[row]]
            rows_out[pl.ds(row, 1), :] = rows_in[pl.ds(source, 1), :]
        return carry

    lax.fori_loop(0, o_ref.shape[0] // unroll, body, 0)
    o_ref[...] = rows_out[...].astype(o_ref.dtype)


def scatter_kernel(unroll, pos_ref, order_ref, x_ref, o_ref, rows_in, rows_out):
    rows_in[...] = x_ref[...].astype(jnp.float32)

    def body(step, carry):
        for lane in range(unroll):
            row = step * unroll + lane
            target = order_ref[pos_ref[row]]
            rows_out[pl.ds(target, 1), :] = rows_in[pl.ds(row, 1), :]
        return carry

    lax.fori_loop(0, x_ref.shape[0] // unroll, body, 0)
    o_ref[...] = rows_out[...].astype(o_ref.dtype)


def move_rows(kernel, pos, order, x):
    return pl.pallas_call(
        functools.partial(kernel, 32),
        out_shape=jax.ShapeDtypeStruct(x.shape, jnp.bfloat16),
        in_specs=[
            pl.BlockSpec(memory_space=pltpu.SMEM),
            pl.BlockSpec(memory_space=pltpu.SMEM),
            pl.BlockSpec(memory_space=pltpu.VMEM),
        ],
        out_specs=pl.BlockSpec(memory_space=pltpu.VMEM),
        scratch_shapes=[pltpu.VMEM(x.shape, jnp.float32), pltpu.VMEM(x.shape, jnp.float32)],
    )(pos, order, x)


def mix_kernel(count_x, count_y, x_ref, mixing_ref, o_ref, padded, send_sem, recv_sem, local_sem):
    index_x = lax.axis_index("tx")
    index_y = lax.axis_index("ty")
    size_x, size_y = x_ref.shape[0], x_ref.shape[1]
    mesh_ids = pl.DeviceIdType.MESH
    steps = [(a, b) for a in (-1, 0, 1) for b in (-1, 0, 1) if (a, b) != (0, 0)]

    def inside(px, py):
        return (px >= 0) & (px < count_x) & (py >= 0) & (py < count_y)

    def ranges(step, size):
        if step == 1:
            return pl.ds(size - 1, 1), pl.ds(0, 1)
        if step == -1:
            return pl.ds(0, 1), pl.ds(size + 1, 1)
        return pl.ds(0, size), pl.ds(1, size)

    barrier = pltpu.get_barrier_semaphore()
    for a, b in steps:
        @pl.when(inside(index_x + a, index_y + b))
        def _():
            pl.semaphore_signal(
                barrier, 1, device_id=(index_x + a, index_y + b), device_id_type=mesh_ids
            )
    peers = sum(inside(index_x + a, index_y + b).astype(jnp.int32) for a, b in steps)
    pl.semaphore_wait(barrier, peers)

    center = pltpu.make_async_copy(
        x_ref, padded.at[pl.ds(1, size_x), pl.ds(1, size_y)], local_sem
    )
    center.start()
    copies = []
    for k, (a, b) in enumerate(steps):
        source_x, target_x = ranges(a, size_x)
        source_y, target_y = ranges(b, size_y)
        copy = pltpu.make_async_remote_copy(
            src_ref=x_ref.at[source_x, source_y],
            dst_ref=padded.at[target_x, target_y],
            send_sem=send_sem.at[k],
            recv_sem=recv_sem.at[k],
            device_id=(index_x + a, index_y + b),
            device_id_type=mesh_ids,
        )
        copies.append(copy)
        pl.when(inside(index_x + a, index_y + b))(copy.start)
    for k, (a, b) in enumerate(steps):
        source_x, target_x = ranges(a, size_x)
        source_y, target_y = ranges(b, size_y)

        @pl.when(jnp.logical_not(inside(index_x - a, index_y - b)))
        def _():
            piece = padded.at[target_x, target_y]
            piece[...] = jnp.zeros(piece.shape, piece.dtype)
    for k, (a, b) in enumerate(steps):
        pl.when(inside(index_x + a, index_y + b))(copies[k].wait_send)
        pl.when(inside(index_x - a, index_y - b))(copies[k].wait_recv)
    center.wait()
    for tile_x in range(size_x):
        for tile_y in range(size_y):
            total = x_ref[tile_x, tile_y].astype(jnp.float32)
            for k, (a, b) in enumerate(steps):
                total += jnp.dot(
                    padded[1 + tile_x + a, 1 + tile_y + b],
                    mixing_ref[k],
                    preferred_element_type=jnp.float32,
                )
            o_ref[tile_x, tile_y] = total.astype(o_ref.dtype)


def mix_tiles(block, mixing):
    count_x = lax.axis_size("tx")
    count_y = lax.axis_size("ty")
    shape = (block.shape[0] + 2, block.shape[1] + 2) + block.shape[2:]
    return pl.pallas_call(
        functools.partial(mix_kernel, count_x, count_y),
        out_shape=jax.ShapeDtypeStruct(block.shape, block.dtype),
        in_specs=[pl.BlockSpec(memory_space=pltpu.VMEM)] * 2,
        out_specs=pl.BlockSpec(memory_space=pltpu.VMEM),
        scratch_shapes=[
            pltpu.VMEM(shape, block.dtype),
            pltpu.SemaphoreType.DMA((8,)),
            pltpu.SemaphoreType.DMA((8,)),
            pltpu.SemaphoreType.DMA,
        ],
        compiler_params=pltpu.CompilerParams(collective_id=0, has_side_effects=True),
    )(block, mixing)


def unit_heads(projected, head_count):
    pieces = projected.reshape(
        projected.shape[:-1] + (head_count, projected.shape[-1] // head_count)
    )
    magnitude = jnp.sqrt(jnp.sum(pieces * pieces, axis=-1, keepdims=True) + epsilon)
    return (pieces / magnitude).reshape(projected.shape).astype(jnp.bfloat16)


def unit_rows(projected, head_width):
    width = projected.shape[-1]
    lane_head = lax.broadcasted_iota(jnp.int32, (width, width), 0) // head_width
    column_head = lax.broadcasted_iota(jnp.int32, (width, width), 1) // head_width
    same_head = (lane_head == column_head).astype(jnp.float32)
    totals = jnp.dot(
        projected * projected,
        same_head,
        precision=lax.Precision.HIGHEST,
        preferred_element_type=jnp.float32,
    )
    return (projected / jnp.sqrt(totals + epsilon)).astype(jnp.bfloat16)


def summary_kernel(rows_ref, column_mask_ref, lane_mask_ref, inducing_ref, proj_ref, o_ref):
    width = rows_ref.shape[1]
    head_width = width // HEADS
    tiles = column_mask_ref.shape[1]
    rows = rows_ref[...]
    queries = unit_rows(
        jnp.dot(inducing_ref[...], proj_ref[0], preferred_element_type=jnp.float32), head_width
    )
    keys = unit_rows(jnp.dot(rows, proj_ref[1], preferred_element_type=jnp.float32), head_width)
    values = jnp.dot(rows, proj_ref[2], preferred_element_type=jnp.float32).astype(jnp.bfloat16)
    column_mask = column_mask_ref[...]
    lane_mask = lane_mask_ref[...]
    heads_out = []
    for head_id in range(HEADS):
        lower = head_id * head_width
        upper = lower + head_width
        scores = lax.dot_general(
            queries[:, lower:upper],
            keys[:, lower:upper],
            (((1,), (1,)), ((), ())),
            preferred_element_type=jnp.float32,
        )
        weights = jnp.exp(sharpness * scores)
        rounded = weights.astype(jnp.bfloat16)
        head_values = values[:, lower:upper]
        masked = jnp.concatenate(
            [head_values * column_mask[:, t : t + 1] for t in range(tiles)], axis=1
        )
        numer = jnp.dot(rounded, masked, preferred_element_type=jnp.float32)
        per_tile = []
        for t in range(tiles):
            totals = jnp.sum(weights * lane_mask[t : t + 1, :], axis=1, keepdims=True)
            per_tile.append(numer[:, t * head_width : (t + 1) * head_width] / totals)
        heads_out.append(per_tile)
    inducing = inducing_ref[...].astype(jnp.float32)
    for t in range(tiles):
        attended = jnp.concatenate([heads_out[h][t] for h in range(HEADS)], axis=1)
        attended = attended.astype(jnp.bfloat16)
        o_ref[t] = (
            inducing + jnp.dot(attended, proj_ref[3], preferred_element_type=jnp.float32)
        ).astype(o_ref.dtype)


def summarize(rows, row_mask, inducing, proj):
    tiles = row_mask.shape[1]
    return pl.pallas_call(
        summary_kernel,
        out_shape=jax.ShapeDtypeStruct((tiles,) + inducing.shape, jnp.bfloat16),
        in_specs=[pl.BlockSpec(memory_space=pltpu.VMEM)] * 5,
        out_specs=pl.BlockSpec(memory_space=pltpu.VMEM),
    )(rows, row_mask.astype(jnp.bfloat16), row_mask.T, inducing, proj)


def body(
    points,
    embed_weight,
    inner_weights,
    output_weight,
    counts,
    point_order,
    inducing,
    first_proj,
    second_proj,
    mixing,
):
    along_x = lax.axis_size("tx")
    along_y = lax.axis_size("ty")
    devices = along_x * along_y
    index_x = lax.axis_index("tx")
    index_y = lax.axis_index("ty")
    own_index = index_x * along_y + index_y
    point_count = points.shape[0]
    per_device = TLX * TLY
    width = output_weight.shape[1]
    quota = point_count // devices
    band = quota * along_y
    head_width = width // HEADS
    inducing_count = inducing.shape[0]

    features = point_mlp(points, embed_weight, inner_weights, output_weight, 2048)

    own_counts = lax.dynamic_index_in_dim(counts, own_index, 0, keepdims=False)
    own_offsets = jnp.cumsum(own_counts) - own_counts
    grid_counts = own_counts.reshape(along_x, TLX, along_y, TLY)
    grid_offsets = own_offsets.reshape(along_x, TLX, along_y, TLY)
    band_start = grid_offsets[:, 0, 0, 0][:, None]
    first_len = grid_counts[:, 0, :, 0] + grid_counts[:, 0, :, 1]
    first_start = grid_offsets[:, 0, :, 0] - band_start
    second_start = grid_offsets[:, 1, :, 0] - band_start
    slot_ids = jnp.arange(quota, dtype=jnp.int32)
    local_pos = jnp.where(
        slot_ids[None, None, :] < first_len[:, :, None],
        first_start[:, :, None] + slot_ids[None, None, :],
        second_start[:, :, None] + slot_ids[None, None, :] - first_len[:, :, None],
    ).reshape(along_x, band)
    send_pos = (local_pos + band_start).reshape(-1)
    order = point_order[0]
    outgoing = move_rows(gather_kernel, send_pos, order, features)
    outgoing = outgoing.reshape(devices, quota, width)
    arrived = lax.all_to_all(outgoing, ("tx", "ty"), split_axis=0, concat_axis=0, tiled=True)
    all_rows = arrived.reshape(devices * quota, width)

    inbound = counts.reshape(devices, along_x, TLX, along_y, TLY)
    inbound = lax.dynamic_index_in_dim(inbound, index_x, 1, keepdims=False)
    inbound = lax.dynamic_index_in_dim(inbound, index_y, 2, keepdims=False)
    inbound = inbound.reshape(devices, per_device)
    through = jnp.cumsum(inbound, axis=1)
    row_tile = jnp.sum(
        (slot_ids[None, :, None] >= through[:, None, : per_device - 1]).astype(jnp.int32), axis=2
    ).reshape(-1)
    tile_ids = jnp.arange(per_device, dtype=jnp.int32)
    row_mask = (row_tile[:, None] == tile_ids[None, :]).astype(jnp.float32)

    summary = summarize(all_rows, row_mask, inducing, first_proj)
    tile_grid = summary.reshape(TLX, TLY, inducing_count, width)
    mixture = mix_tiles(tile_grid, mixing)
    mixture = mixture.astype(jnp.bfloat16).reshape(per_device * inducing_count, width)

    point_queries = unit_heads(
        jnp.dot(all_rows, second_proj[0], preferred_element_type=jnp.float32), HEADS
    )
    second_keys = unit_heads(
        jnp.dot(mixture, second_proj[1], preferred_element_type=jnp.float32), HEADS
    )
    second_values = jnp.dot(mixture, second_proj[2], preferred_element_type=jnp.float32).astype(
        jnp.bfloat16
    )
    key_mask = jnp.repeat(row_mask, inducing_count, axis=1)
    heads_out = []
    for head_id in range(HEADS):
        lower = head_id * head_width
        upper = lower + head_width
        scores = jnp.dot(
            point_queries[:, lower:upper],
            second_keys[:, lower:upper].T,
            preferred_element_type=jnp.float32,
        )
        weights = jnp.exp(sharpness * scores) * key_mask
        totals = jnp.sum(weights, axis=1, keepdims=True)
        numer = jnp.dot(
            weights.astype(jnp.bfloat16),
            second_values[:, lower:upper],
            preferred_element_type=jnp.float32,
        )
        heads_out.append(numer / totals)
    second_attended = jnp.concatenate(heads_out, axis=1).astype(jnp.bfloat16)
    result = (
        all_rows.astype(jnp.float32)
        + jnp.dot(second_attended, second_proj[3], preferred_element_type=jnp.float32)
    ).astype(jnp.bfloat16)

    coming = lax.all_to_all(
        result.reshape(devices, quota, width), ("tx", "ty"), split_axis=0, concat_axis=0, tiled=True
    )
    returned = move_rows(
        scatter_kernel, send_pos, order, coming.reshape(point_count, width)
    )
    return returned


def solution(mesh):
    placed = (P(("tx", "ty"), None), P(), P(), P(), P(), P(("tx", "ty"), None), P(), P(), P(), P())
    return jax.shard_map(
        body, mesh=mesh, in_specs=placed, out_specs=P(("tx", "ty"), None), check_vma=False
    )
```

```python
import functools

import jax
import jax.numpy as jnp
from jax import lax
from jax.experimental import pallas as pl
from jax.experimental.pallas import tpu as pltpu
from jax.sharding import PartitionSpec as P

HEADS = 2
TLX = 2
TLY = 2


sharpness = 32.0
epsilon = 1e-06
neighbour_steps = ((-1, -1), (-1, 0), (-1, 1), (0, -1), (0, 1), (1, -1), (1, 0), (1, 1))


def mlp_kernel(x_ref, w1_ref, w2_ref, w3_ref, o_ref):
    def silu(v):
        return v / (1.0 + jnp.exp(-v))

    h = silu(jnp.dot(x_ref[...], w1_ref[...], preferred_element_type=jnp.float32))
    h = h.astype(jnp.bfloat16)
    for layer_id in range(w2_ref.shape[0]):
        h = silu(jnp.dot(h, w2_ref[layer_id], preferred_element_type=jnp.float32))
        h = h.astype(jnp.bfloat16)
    o_ref[...] = jnp.dot(h, w3_ref[...], preferred_element_type=jnp.float32).astype(o_ref.dtype)


def point_mlp(x, w1, w2, w3, block):
    rows = x.shape[0]
    full = lambda shape: pl.BlockSpec(shape, lambda i: (0,) * len(shape))
    return pl.pallas_call(
        mlp_kernel,
        out_shape=jax.ShapeDtypeStruct((rows, w3.shape[1]), jnp.bfloat16),
        grid=(rows // block,),
        in_specs=[
            pl.BlockSpec((block, x.shape[1]), lambda i: (i, 0)),
            full(w1.shape),
            full(w2.shape),
            full(w3.shape),
        ],
        out_specs=pl.BlockSpec((block, w3.shape[1]), lambda i: (i, 0)),
    )(x, w1, w2, w3)


def gather_kernel(unroll, pos_ref, order_ref, x_ref, o_ref, rows_in, rows_out):
    rows_in[...] = x_ref[...].astype(jnp.float32)

    def body(step, carry):
        for lane in range(unroll):
            row = step * unroll + lane
            source = order_ref[pos_ref[row]]
            rows_out[pl.ds(row, 1), :] = rows_in[pl.ds(source, 1), :]
        return carry

    lax.fori_loop(0, o_ref.shape[0] // unroll, body, 0)
    o_ref[...] = rows_out[...].astype(o_ref.dtype)


def scatter_kernel(unroll, pos_ref, order_ref, x_ref, o_ref, rows_in, rows_out):
    rows_in[...] = x_ref[...].astype(jnp.float32)

    def body(step, carry):
        for lane in range(unroll):
            row = step * unroll + lane
            target = order_ref[pos_ref[row]]
            rows_out[pl.ds(target, 1), :] = rows_in[pl.ds(row, 1), :]
        return carry

    lax.fori_loop(0, x_ref.shape[0] // unroll, body, 0)
    o_ref[...] = rows_out[...].astype(o_ref.dtype)


def move_rows(kernel, pos, order, x):
    return pl.pallas_call(
        functools.partial(kernel, 64),
        out_shape=jax.ShapeDtypeStruct(x.shape, jnp.bfloat16),
        in_specs=[
            pl.BlockSpec(memory_space=pltpu.SMEM),
            pl.BlockSpec(memory_space=pltpu.SMEM),
            pl.BlockSpec(memory_space=pltpu.VMEM),
        ],
        out_specs=pl.BlockSpec(memory_space=pltpu.VMEM),
        scratch_shapes=[pltpu.VMEM(x.shape, jnp.float32), pltpu.VMEM(x.shape, jnp.float32)],
    )(pos, order, x)


def mix_kernel(count_x, count_y, x_ref, mixing_ref, o_ref, padded, send_sem, recv_sem, local_sem):
    index_x = lax.axis_index("tx")
    index_y = lax.axis_index("ty")
    size_x, size_y = x_ref.shape[0], x_ref.shape[1]
    mesh_ids = pl.DeviceIdType.MESH
    steps = [(a, b) for a in (-1, 0, 1) for b in (-1, 0, 1) if (a, b) != (0, 0)]

    def inside(px, py):
        return (px >= 0) & (px < count_x) & (py >= 0) & (py < count_y)

    def ranges(step, size):
        if step == 1:
            return pl.ds(size - 1, 1), pl.ds(0, 1)
        if step == -1:
            return pl.ds(0, 1), pl.ds(size + 1, 1)
        return pl.ds(0, size), pl.ds(1, size)

    barrier = pltpu.get_barrier_semaphore()
    for a, b in steps:
        @pl.when(inside(index_x + a, index_y + b))
        def _():
            pl.semaphore_signal(
                barrier, 1, device_id=(index_x + a, index_y + b), device_id_type=mesh_ids
            )
    peers = sum(inside(index_x + a, index_y + b).astype(jnp.int32) for a, b in steps)
    pl.semaphore_wait(barrier, peers)

    center = pltpu.make_async_copy(
        x_ref, padded.at[pl.ds(1, size_x), pl.ds(1, size_y)], local_sem
    )
    center.start()
    copies = []
    for k, (a, b) in enumerate(steps):
        source_x, target_x = ranges(a, size_x)
        source_y, target_y = ranges(b, size_y)
        copy = pltpu.make_async_remote_copy(
            src_ref=x_ref.at[source_x, source_y],
            dst_ref=padded.at[target_x, target_y],
            send_sem=send_sem.at[k],
            recv_sem=recv_sem.at[k],
            device_id=(index_x + a, index_y + b),
            device_id_type=mesh_ids,
        )
        copies.append(copy)
        pl.when(inside(index_x + a, index_y + b))(copy.start)
    for k, (a, b) in enumerate(steps):
        source_x, target_x = ranges(a, size_x)
        source_y, target_y = ranges(b, size_y)

        @pl.when(jnp.logical_not(inside(index_x - a, index_y - b)))
        def _():
            piece = padded.at[target_x, target_y]
            piece[...] = jnp.zeros(piece.shape, piece.dtype)
    for k, (a, b) in enumerate(steps):
        pl.when(inside(index_x + a, index_y + b))(copies[k].wait_send)
        pl.when(inside(index_x - a, index_y - b))(copies[k].wait_recv)
    center.wait()
    for tile_x in range(size_x):
        for tile_y in range(size_y):
            total = x_ref[tile_x, tile_y].astype(jnp.float32)
            for k, (a, b) in enumerate(steps):
                total += jnp.dot(
                    padded[1 + tile_x + a, 1 + tile_y + b],
                    mixing_ref[k],
                    preferred_element_type=jnp.float32,
                )
            o_ref[tile_x, tile_y] = total.astype(o_ref.dtype)


def mix_tiles(block, mixing):
    count_x = lax.axis_size("tx")
    count_y = lax.axis_size("ty")
    shape = (block.shape[0] + 2, block.shape[1] + 2) + block.shape[2:]
    return pl.pallas_call(
        functools.partial(mix_kernel, count_x, count_y),
        out_shape=jax.ShapeDtypeStruct(block.shape, block.dtype),
        in_specs=[pl.BlockSpec(memory_space=pltpu.VMEM)] * 2,
        out_specs=pl.BlockSpec(memory_space=pltpu.VMEM),
        scratch_shapes=[
            pltpu.VMEM(shape, block.dtype),
            pltpu.SemaphoreType.DMA((8,)),
            pltpu.SemaphoreType.DMA((8,)),
            pltpu.SemaphoreType.DMA,
        ],
        compiler_params=pltpu.CompilerParams(collective_id=0, has_side_effects=True),
    )(block, mixing)


def unit_heads(projected, head_count):
    pieces = projected.reshape(
        projected.shape[:-1] + (head_count, projected.shape[-1] // head_count)
    )
    magnitude = jnp.sqrt(jnp.sum(pieces * pieces, axis=-1, keepdims=True) + epsilon)
    return (pieces / magnitude).reshape(projected.shape).astype(jnp.bfloat16)


def unit_rows(projected, head_width):
    width = projected.shape[-1]
    lane_head = lax.broadcasted_iota(jnp.int32, (width, width), 0) // head_width
    column_head = lax.broadcasted_iota(jnp.int32, (width, width), 1) // head_width
    same_head = (lane_head == column_head).astype(jnp.float32)
    totals = jnp.dot(
        projected * projected,
        same_head,
        precision=lax.Precision.HIGHEST,
        preferred_element_type=jnp.float32,
    )
    return (projected / jnp.sqrt(totals + epsilon)).astype(jnp.bfloat16)


def summary_kernel(rows_ref, column_mask_ref, lane_mask_ref, inducing_ref, proj_ref, o_ref):
    width = rows_ref.shape[1]
    head_width = width // HEADS
    tiles = column_mask_ref.shape[1]
    rows = rows_ref[...]
    queries = unit_rows(
        jnp.dot(inducing_ref[...], proj_ref[0], preferred_element_type=jnp.float32), head_width
    )
    keys = unit_rows(jnp.dot(rows, proj_ref[1], preferred_element_type=jnp.float32), head_width)
    values = jnp.dot(rows, proj_ref[2], preferred_element_type=jnp.float32).astype(jnp.bfloat16)
    column_mask = column_mask_ref[...]
    lane_mask = lane_mask_ref[...]
    heads_out = []
    for head_id in range(HEADS):
        lower = head_id * head_width
        upper = lower + head_width
        scores = lax.dot_general(
            queries[:, lower:upper],
            keys[:, lower:upper],
            (((1,), (1,)), ((), ())),
            preferred_element_type=jnp.float32,
        )
        weights = jnp.exp(sharpness * scores)
        rounded = weights.astype(jnp.bfloat16)
        head_values = values[:, lower:upper]
        masked = jnp.concatenate(
            [head_values * column_mask[:, t : t + 1] for t in range(tiles)], axis=1
        )
        numer = jnp.dot(rounded, masked, preferred_element_type=jnp.float32)
        per_tile = []
        for t in range(tiles):
            totals = jnp.sum(weights * lane_mask[t : t + 1, :], axis=1, keepdims=True)
            per_tile.append(numer[:, t * head_width : (t + 1) * head_width] / totals)
        heads_out.append(per_tile)
    inducing = inducing_ref[...].astype(jnp.float32)
    for t in range(tiles):
        attended = jnp.concatenate([heads_out[h][t] for h in range(HEADS)], axis=1)
        attended = attended.astype(jnp.bfloat16)
        o_ref[t] = (
            inducing + jnp.dot(attended, proj_ref[3], preferred_element_type=jnp.float32)
        ).astype(o_ref.dtype)


def summarize(rows, row_mask, inducing, proj):
    tiles = row_mask.shape[1]
    return pl.pallas_call(
        summary_kernel,
        out_shape=jax.ShapeDtypeStruct((tiles,) + inducing.shape, jnp.bfloat16),
        in_specs=[pl.BlockSpec(memory_space=pltpu.VMEM)] * 5,
        out_specs=pl.BlockSpec(memory_space=pltpu.VMEM),
    )(rows, row_mask.astype(jnp.bfloat16), row_mask.T, inducing, proj)


def body(
    points,
    embed_weight,
    inner_weights,
    output_weight,
    counts,
    point_order,
    inducing,
    first_proj,
    second_proj,
    mixing,
):
    along_x = lax.axis_size("tx")
    along_y = lax.axis_size("ty")
    devices = along_x * along_y
    index_x = lax.axis_index("tx")
    index_y = lax.axis_index("ty")
    own_index = index_x * along_y + index_y
    point_count = points.shape[0]
    per_device = TLX * TLY
    width = output_weight.shape[1]
    quota = point_count // devices
    band = quota * along_y
    head_width = width // HEADS
    inducing_count = inducing.shape[0]

    features = point_mlp(points, embed_weight, inner_weights, output_weight, 2048)

    own_counts = lax.dynamic_index_in_dim(counts, own_index, 0, keepdims=False)
    own_offsets = jnp.cumsum(own_counts) - own_counts
    grid_counts = own_counts.reshape(along_x, TLX, along_y, TLY)
    grid_offsets = own_offsets.reshape(along_x, TLX, along_y, TLY)
    band_start = grid_offsets[:, 0, 0, 0][:, None]
    first_len = grid_counts[:, 0, :, 0] + grid_counts[:, 0, :, 1]
    first_start = grid_offsets[:, 0, :, 0] - band_start
    second_start = grid_offsets[:, 1, :, 0] - band_start
    slot_ids = jnp.arange(quota, dtype=jnp.int32)
    local_pos = jnp.where(
        slot_ids[None, None, :] < first_len[:, :, None],
        first_start[:, :, None] + slot_ids[None, None, :],
        second_start[:, :, None] + slot_ids[None, None, :] - first_len[:, :, None],
    ).reshape(along_x, band)
    send_pos = (local_pos + band_start).reshape(-1)
    order = point_order[0]
    outgoing = move_rows(gather_kernel, send_pos, order, features)
    outgoing = outgoing.reshape(devices, quota, width)
    arrived = lax.all_to_all(outgoing, ("tx", "ty"), split_axis=0, concat_axis=0, tiled=True)
    all_rows = arrived.reshape(devices * quota, width)

    inbound = counts.reshape(devices, along_x, TLX, along_y, TLY)
    inbound = lax.dynamic_index_in_dim(inbound, index_x, 1, keepdims=False)
    inbound = lax.dynamic_index_in_dim(inbound, index_y, 2, keepdims=False)
    inbound = inbound.reshape(devices, per_device)
    through = jnp.cumsum(inbound, axis=1)
    row_tile = jnp.sum(
        (slot_ids[None, :, None] >= through[:, None, : per_device - 1]).astype(jnp.int32), axis=2
    ).reshape(-1)
    tile_ids = jnp.arange(per_device, dtype=jnp.int32)
    row_mask = (row_tile[:, None] == tile_ids[None, :]).astype(jnp.float32)

    summary = summarize(all_rows, row_mask, inducing, first_proj)
    tile_grid = summary.reshape(TLX, TLY, inducing_count, width)
    mixture = mix_tiles(tile_grid, mixing)
    mixture = mixture.astype(jnp.bfloat16).reshape(per_device * inducing_count, width)

    point_queries = unit_heads(
        jnp.dot(all_rows, second_proj[0], preferred_element_type=jnp.float32), HEADS
    )
    second_keys = unit_heads(
        jnp.dot(mixture, second_proj[1], preferred_element_type=jnp.float32), HEADS
    )
    second_values = jnp.dot(mixture, second_proj[2], preferred_element_type=jnp.float32).astype(
        jnp.bfloat16
    )
    key_mask = jnp.repeat(row_mask, inducing_count, axis=1)
    heads_out = []
    for head_id in range(HEADS):
        lower = head_id * head_width
        upper = lower + head_width
        scores = jnp.dot(
            point_queries[:, lower:upper],
            second_keys[:, lower:upper].T,
            preferred_element_type=jnp.float32,
        )
        weights = jnp.exp(sharpness * scores) * key_mask
        totals = jnp.sum(weights, axis=1, keepdims=True)
        numer = jnp.dot(
            weights.astype(jnp.bfloat16),
            second_values[:, lower:upper],
            preferred_element_type=jnp.float32,
        )
        heads_out.append(numer / totals)
    second_attended = jnp.concatenate(heads_out, axis=1).astype(jnp.bfloat16)
    result = (
        all_rows.astype(jnp.float32)
        + jnp.dot(second_attended, second_proj[3], preferred_element_type=jnp.float32)
    ).astype(jnp.bfloat16)

    coming = lax.all_to_all(
        result.reshape(devices, quota, width), ("tx", "ty"), split_axis=0, concat_axis=0, tiled=True
    )
    returned = move_rows(
        scatter_kernel, send_pos, order, coming.reshape(point_count, width)
    )
    return returned


def solution(mesh):
    placed = (P(("tx", "ty"), None), P(), P(), P(), P(), P(("tx", "ty"), None), P(), P(), P(), P())
    return jax.shard_map(
        body, mesh=mesh, in_specs=placed, out_specs=P(("tx", "ty"), None), check_vma=False
    )
```

```python
import functools

import jax
import jax.numpy as jnp
from jax import lax
from jax.experimental import pallas as pl
from jax.experimental.pallas import tpu as pltpu
from jax.sharding import PartitionSpec as P

HEADS = 2
TLX = 2
TLY = 2


sharpness = 32.0
epsilon = 1e-06
neighbour_steps = ((-1, -1), (-1, 0), (-1, 1), (0, -1), (0, 1), (1, -1), (1, 0), (1, 1))


def mlp_kernel(x_ref, w1_ref, w2_ref, w3_ref, o_ref):
    def silu(v):
        return v / (1.0 + jnp.exp(-v))

    h = silu(jnp.dot(x_ref[...], w1_ref[...], preferred_element_type=jnp.float32))
    h = h.astype(jnp.bfloat16)
    for layer_id in range(w2_ref.shape[0]):
        h = silu(jnp.dot(h, w2_ref[layer_id], preferred_element_type=jnp.float32))
        h = h.astype(jnp.bfloat16)
    o_ref[...] = jnp.dot(h, w3_ref[...], preferred_element_type=jnp.float32).astype(o_ref.dtype)


def point_mlp(x, w1, w2, w3, block):
    rows = x.shape[0]
    full = lambda shape: pl.BlockSpec(shape, lambda i: (0,) * len(shape))
    return pl.pallas_call(
        mlp_kernel,
        out_shape=jax.ShapeDtypeStruct((rows, w3.shape[1]), jnp.bfloat16),
        grid=(rows // block,),
        in_specs=[
            pl.BlockSpec((block, x.shape[1]), lambda i: (i, 0)),
            full(w1.shape),
            full(w2.shape),
            full(w3.shape),
        ],
        out_specs=pl.BlockSpec((block, w3.shape[1]), lambda i: (i, 0)),
    )(x, w1, w2, w3)


def gather_kernel(unroll, pos_ref, order_ref, x_ref, o_ref, rows_in, rows_out):
    rows_in[...] = x_ref[...].astype(jnp.float32)

    def body(step, carry):
        for lane in range(unroll):
            row = step * unroll + lane
            source = order_ref[pos_ref[row]]
            rows_out[pl.ds(row, 1), :] = rows_in[pl.ds(source, 1), :]
        return carry

    lax.fori_loop(0, o_ref.shape[0] // unroll, body, 0)
    o_ref[...] = rows_out[...].astype(o_ref.dtype)


def scatter_kernel(unroll, pos_ref, order_ref, x_ref, o_ref, rows_in, rows_out):
    rows_in[...] = x_ref[...].astype(jnp.float32)

    def body(step, carry):
        for lane in range(unroll):
            row = step * unroll + lane
            target = order_ref[pos_ref[row]]
            rows_out[pl.ds(target, 1), :] = rows_in[pl.ds(row, 1), :]
        return carry

    lax.fori_loop(0, x_ref.shape[0] // unroll, body, 0)
    o_ref[...] = rows_out[...].astype(o_ref.dtype)


def move_rows(kernel, pos, order, x):
    return pl.pallas_call(
        functools.partial(kernel, 64),
        out_shape=jax.ShapeDtypeStruct(x.shape, jnp.bfloat16),
        in_specs=[
            pl.BlockSpec(memory_space=pltpu.SMEM),
            pl.BlockSpec(memory_space=pltpu.SMEM),
            pl.BlockSpec(memory_space=pltpu.VMEM),
        ],
        out_specs=pl.BlockSpec(memory_space=pltpu.VMEM),
        scratch_shapes=[pltpu.VMEM(x.shape, jnp.float32), pltpu.VMEM(x.shape, jnp.float32)],
    )(pos, order, x)


def mix_kernel(
    count_x,
    count_y,
    x_ref,
    mixing_ref,
    rows_ref,
    proj_ref,
    queries_ref,
    keys_ref,
    values_ref,
    padded,
    mixed,
    send_sem,
    recv_sem,
    local_sem,
):
    index_x = lax.axis_index("tx")
    index_y = lax.axis_index("ty")
    size_x, size_y = x_ref.shape[0], x_ref.shape[1]
    mesh_ids = pl.DeviceIdType.MESH
    steps = [(a, b) for a in (-1, 0, 1) for b in (-1, 0, 1) if (a, b) != (0, 0)]

    def inside(px, py):
        return (px >= 0) & (px < count_x) & (py >= 0) & (py < count_y)

    def ranges(step, size):
        if step == 1:
            return pl.ds(size - 1, 1), pl.ds(0, 1)
        if step == -1:
            return pl.ds(0, 1), pl.ds(size + 1, 1)
        return pl.ds(0, size), pl.ds(1, size)

    barrier = pltpu.get_barrier_semaphore()
    for a, b in steps:
        @pl.when(inside(index_x + a, index_y + b))
        def _():
            pl.semaphore_signal(
                barrier, 1, device_id=(index_x + a, index_y + b), device_id_type=mesh_ids
            )
    peers = sum(inside(index_x + a, index_y + b).astype(jnp.int32) for a, b in steps)
    pl.semaphore_wait(barrier, peers)

    center = pltpu.make_async_copy(
        x_ref, padded.at[pl.ds(1, size_x), pl.ds(1, size_y)], local_sem
    )
    center.start()
    copies = []
    for k, (a, b) in enumerate(steps):
        source_x, target_x = ranges(a, size_x)
        source_y, target_y = ranges(b, size_y)
        copy = pltpu.make_async_remote_copy(
            src_ref=x_ref.at[source_x, source_y],
            dst_ref=padded.at[target_x, target_y],
            send_sem=send_sem.at[k],
            recv_sem=recv_sem.at[k],
            device_id=(index_x + a, index_y + b),
            device_id_type=mesh_ids,
        )
        copies.append(copy)
        pl.when(inside(index_x + a, index_y + b))(copy.start)
    for k, (a, b) in enumerate(steps):
        source_x, target_x = ranges(a, size_x)
        source_y, target_y = ranges(b, size_y)

        @pl.when(jnp.logical_not(inside(index_x - a, index_y - b)))
        def _():
            piece = padded.at[target_x, target_y]
            piece[...] = jnp.zeros(piece.shape, piece.dtype)
    head_width = rows_ref.shape[1] // HEADS
    queries_ref[...] = unit_rows(
        jnp.dot(rows_ref[...], proj_ref[0], preferred_element_type=jnp.float32), head_width
    )
    for k, (a, b) in enumerate(steps):
        pl.when(inside(index_x + a, index_y + b))(copies[k].wait_send)
        pl.when(inside(index_x - a, index_y - b))(copies[k].wait_recv)
    center.wait()
    for tile_x in range(size_x):
        for tile_y in range(size_y):
            total = x_ref[tile_x, tile_y].astype(jnp.float32)
            for k, (a, b) in enumerate(steps):
                total += jnp.dot(
                    padded[1 + tile_x + a, 1 + tile_y + b],
                    mixing_ref[k],
                    preferred_element_type=jnp.float32,
                )
            tile_rows = pl.ds((tile_x * size_y + tile_y) * x_ref.shape[2], x_ref.shape[2])
            mixed[tile_rows, :] = total.astype(mixed.dtype)
    mixture = mixed[...]
    keys_ref[...] = unit_rows(
        jnp.dot(mixture, proj_ref[1], preferred_element_type=jnp.float32), head_width
    )
    values_ref[...] = jnp.dot(mixture, proj_ref[2], preferred_element_type=jnp.float32).astype(
        values_ref.dtype
    )


def mix_tiles(block, mixing, rows, proj):
    count_x = lax.axis_size("tx")
    count_y = lax.axis_size("ty")
    shape = (block.shape[0] + 2, block.shape[1] + 2) + block.shape[2:]
    keys_shape = (block.shape[0] * block.shape[1] * block.shape[2], block.shape[3])
    return pl.pallas_call(
        functools.partial(mix_kernel, count_x, count_y),
        out_shape=(
            jax.ShapeDtypeStruct(rows.shape, jnp.bfloat16),
            jax.ShapeDtypeStruct(keys_shape, jnp.bfloat16),
            jax.ShapeDtypeStruct(keys_shape, jnp.bfloat16),
        ),
        in_specs=[pl.BlockSpec(memory_space=pltpu.VMEM)] * 4,
        out_specs=[pl.BlockSpec(memory_space=pltpu.VMEM)] * 3,
        scratch_shapes=[
            pltpu.VMEM(shape, block.dtype),
            pltpu.VMEM(keys_shape, jnp.bfloat16),
            pltpu.SemaphoreType.DMA((8,)),
            pltpu.SemaphoreType.DMA((8,)),
            pltpu.SemaphoreType.DMA,
        ],
        compiler_params=pltpu.CompilerParams(collective_id=0, has_side_effects=True),
    )(block, mixing, rows, proj)


def unit_heads(projected, head_count):
    pieces = projected.reshape(
        projected.shape[:-1] + (head_count, projected.shape[-1] // head_count)
    )
    magnitude = jnp.sqrt(jnp.sum(pieces * pieces, axis=-1, keepdims=True) + epsilon)
    return (pieces / magnitude).reshape(projected.shape).astype(jnp.bfloat16)


def unit_rows(projected, head_width):
    width = projected.shape[-1]
    lane_head = lax.broadcasted_iota(jnp.int32, (width, width), 0) // head_width
    column_head = lax.broadcasted_iota(jnp.int32, (width, width), 1) // head_width
    same_head = (lane_head == column_head).astype(jnp.float32)
    totals = jnp.dot(
        projected * projected,
        same_head,
        precision=lax.Precision.HIGHEST,
        preferred_element_type=jnp.float32,
    )
    return (projected / jnp.sqrt(totals + epsilon)).astype(jnp.bfloat16)


def summary_kernel(rows_ref, column_mask_ref, lane_mask_ref, inducing_ref, proj_ref, o_ref):
    width = rows_ref.shape[1]
    head_width = width // HEADS
    tiles = column_mask_ref.shape[1]
    rows = rows_ref[...]
    queries = unit_rows(
        jnp.dot(inducing_ref[...], proj_ref[0], preferred_element_type=jnp.float32), head_width
    )
    keys = unit_rows(jnp.dot(rows, proj_ref[1], preferred_element_type=jnp.float32), head_width)
    values = jnp.dot(rows, proj_ref[2], preferred_element_type=jnp.float32).astype(jnp.bfloat16)
    column_mask = column_mask_ref[...]
    lane_mask = lane_mask_ref[...]
    heads_out = []
    for head_id in range(HEADS):
        lower = head_id * head_width
        upper = lower + head_width
        scores = lax.dot_general(
            queries[:, lower:upper],
            keys[:, lower:upper],
            (((1,), (1,)), ((), ())),
            preferred_element_type=jnp.float32,
        )
        weights = jnp.exp(sharpness * scores)
        rounded = weights.astype(jnp.bfloat16)
        head_values = values[:, lower:upper]
        masked = jnp.concatenate(
            [head_values * column_mask[:, t : t + 1] for t in range(tiles)], axis=1
        )
        numer = jnp.dot(rounded, masked, preferred_element_type=jnp.float32)
        per_tile = []
        for t in range(tiles):
            totals = jnp.sum(weights * lane_mask[t : t + 1, :], axis=1, keepdims=True)
            per_tile.append(numer[:, t * head_width : (t + 1) * head_width] / totals)
        heads_out.append(per_tile)
    inducing = inducing_ref[...].astype(jnp.float32)
    for t in range(tiles):
        attended = jnp.concatenate([heads_out[h][t] for h in range(HEADS)], axis=1)
        attended = attended.astype(jnp.bfloat16)
        o_ref[t] = (
            inducing + jnp.dot(attended, proj_ref[3], preferred_element_type=jnp.float32)
        ).astype(o_ref.dtype)


def summarize(rows, row_mask, inducing, proj):
    tiles = row_mask.shape[1]
    return pl.pallas_call(
        summary_kernel,
        out_shape=jax.ShapeDtypeStruct((tiles,) + inducing.shape, jnp.bfloat16),
        in_specs=[pl.BlockSpec(memory_space=pltpu.VMEM)] * 5,
        out_specs=pl.BlockSpec(memory_space=pltpu.VMEM),
    )(rows, row_mask.astype(jnp.bfloat16), row_mask.T, inducing, proj)


def body(
    points,
    embed_weight,
    inner_weights,
    output_weight,
    counts,
    point_order,
    inducing,
    first_proj,
    second_proj,
    mixing,
):
    along_x = lax.axis_size("tx")
    along_y = lax.axis_size("ty")
    devices = along_x * along_y
    index_x = lax.axis_index("tx")
    index_y = lax.axis_index("ty")
    own_index = index_x * along_y + index_y
    point_count = points.shape[0]
    per_device = TLX * TLY
    width = output_weight.shape[1]
    quota = point_count // devices
    band = quota * along_y
    head_width = width // HEADS
    inducing_count = inducing.shape[0]

    features = point_mlp(points, embed_weight, inner_weights, output_weight, 2048)

    own_counts = lax.dynamic_index_in_dim(counts, own_index, 0, keepdims=False)
    own_offsets = jnp.cumsum(own_counts) - own_counts
    grid_counts = own_counts.reshape(along_x, TLX, along_y, TLY)
    grid_offsets = own_offsets.reshape(along_x, TLX, along_y, TLY)
    band_start = grid_offsets[:, 0, 0, 0][:, None]
    first_len = grid_counts[:, 0, :, 0] + grid_counts[:, 0, :, 1]
    first_start = grid_offsets[:, 0, :, 0] - band_start
    second_start = grid_offsets[:, 1, :, 0] - band_start
    slot_ids = jnp.arange(quota, dtype=jnp.int32)
    local_pos = jnp.where(
        slot_ids[None, None, :] < first_len[:, :, None],
        first_start[:, :, None] + slot_ids[None, None, :],
        second_start[:, :, None] + slot_ids[None, None, :] - first_len[:, :, None],
    ).reshape(along_x, band)
    send_pos = (local_pos + band_start).reshape(-1)
    order = point_order[0]
    outgoing = move_rows(gather_kernel, send_pos, order, features)
    outgoing = outgoing.reshape(devices, quota, width)
    arrived = lax.all_to_all(outgoing, ("tx", "ty"), split_axis=0, concat_axis=0, tiled=True)
    all_rows = arrived.reshape(devices * quota, width)

    inbound = counts.reshape(devices, along_x, TLX, along_y, TLY)
    inbound = lax.dynamic_index_in_dim(inbound, index_x, 1, keepdims=False)
    inbound = lax.dynamic_index_in_dim(inbound, index_y, 2, keepdims=False)
    inbound = inbound.reshape(devices, per_device)
    through = jnp.cumsum(inbound, axis=1)
    row_tile = jnp.sum(
        (slot_ids[None, :, None] >= through[:, None, : per_device - 1]).astype(jnp.int32), axis=2
    ).reshape(-1)
    tile_ids = jnp.arange(per_device, dtype=jnp.int32)
    row_mask = (row_tile[:, None] == tile_ids[None, :]).astype(jnp.float32)

    summary = summarize(all_rows, row_mask, inducing, first_proj)
    tile_grid = summary.reshape(TLX, TLY, inducing_count, width)
    point_queries, second_keys, second_values = mix_tiles(
        tile_grid, mixing, all_rows, second_proj
    )
    key_mask = jnp.repeat(row_mask, inducing_count, axis=1)
    heads_out = []
    for head_id in range(HEADS):
        lower = head_id * head_width
        upper = lower + head_width
        scores = jnp.dot(
            point_queries[:, lower:upper],
            second_keys[:, lower:upper].T,
            preferred_element_type=jnp.float32,
        )
        weights = jnp.exp(sharpness * scores) * key_mask
        totals = jnp.sum(weights, axis=1, keepdims=True)
        numer = jnp.dot(
            weights.astype(jnp.bfloat16),
            second_values[:, lower:upper],
            preferred_element_type=jnp.float32,
        )
        heads_out.append(numer / totals)
    second_attended = jnp.concatenate(heads_out, axis=1).astype(jnp.bfloat16)
    result = (
        all_rows.astype(jnp.float32)
        + jnp.dot(second_attended, second_proj[3], preferred_element_type=jnp.float32)
    ).astype(jnp.bfloat16)

    coming = lax.all_to_all(
        result.reshape(devices, quota, width), ("tx", "ty"), split_axis=0, concat_axis=0, tiled=True
    )
    returned = move_rows(
        scatter_kernel, send_pos, order, coming.reshape(point_count, width)
    )
    return returned


def solution(mesh):
    placed = (P(("tx", "ty"), None), P(), P(), P(), P(), P(("tx", "ty"), None), P(), P(), P(), P())
    return jax.shard_map(
        body, mesh=mesh, in_specs=placed, out_specs=P(("tx", "ty"), None), check_vma=False
    )
```

```python
import functools

import jax
import jax.numpy as jnp
from jax import lax
from jax.experimental import pallas as pl
from jax.experimental.pallas import tpu as pltpu
from jax.sharding import PartitionSpec as P

HEADS = 2
TLX = 2
TLY = 2


sharpness = 32.0
epsilon = 1e-06
neighbour_steps = ((-1, -1), (-1, 0), (-1, 1), (0, -1), (0, 1), (1, -1), (1, 0), (1, 1))


def mlp_kernel(x_ref, w1_ref, w2_ref, w3_ref, o_ref):
    def silu(v):
        return v / (1.0 + jnp.exp(-v))

    h = silu(jnp.dot(x_ref[...], w1_ref[...], preferred_element_type=jnp.float32))
    h = h.astype(jnp.bfloat16)
    for layer_id in range(w2_ref.shape[0]):
        h = silu(jnp.dot(h, w2_ref[layer_id], preferred_element_type=jnp.float32))
        h = h.astype(jnp.bfloat16)
    o_ref[...] = jnp.dot(h, w3_ref[...], preferred_element_type=jnp.float32).astype(o_ref.dtype)


def point_mlp(x, w1, w2, w3, block):
    rows = x.shape[0]
    full = lambda shape: pl.BlockSpec(shape, lambda i: (0,) * len(shape))
    return pl.pallas_call(
        mlp_kernel,
        out_shape=jax.ShapeDtypeStruct((rows, w3.shape[1]), jnp.bfloat16),
        grid=(rows // block,),
        in_specs=[
            pl.BlockSpec((block, x.shape[1]), lambda i: (i, 0)),
            full(w1.shape),
            full(w2.shape),
            full(w3.shape),
        ],
        out_specs=pl.BlockSpec((block, w3.shape[1]), lambda i: (i, 0)),
    )(x, w1, w2, w3)


def gather_kernel(unroll, pos_ref, order_ref, x_ref, o_ref, rows_in, rows_out):
    rows_in[...] = x_ref[...].astype(jnp.float32)

    def body(step, carry):
        for lane in range(unroll):
            row = step * unroll + lane
            source = order_ref[pos_ref[row]]
            rows_out[pl.ds(row, 1), :] = rows_in[pl.ds(source, 1), :]
        return carry

    lax.fori_loop(0, o_ref.shape[0] // unroll, body, 0)
    o_ref[...] = rows_out[...].astype(o_ref.dtype)


def scatter_kernel(unroll, pos_ref, order_ref, x_ref, o_ref, rows_in, rows_out):
    rows_in[...] = x_ref[...].astype(jnp.float32)

    def body(step, carry):
        for lane in range(unroll):
            row = step * unroll + lane
            target = order_ref[pos_ref[row]]
            rows_out[pl.ds(target, 1), :] = rows_in[pl.ds(row, 1), :]
        return carry

    lax.fori_loop(0, x_ref.shape[0] // unroll, body, 0)
    o_ref[...] = rows_out[...].astype(o_ref.dtype)


def move_rows(kernel, pos, order, x):
    return pl.pallas_call(
        functools.partial(kernel, 64),
        out_shape=jax.ShapeDtypeStruct(x.shape, jnp.bfloat16),
        in_specs=[
            pl.BlockSpec(memory_space=pltpu.SMEM),
            pl.BlockSpec(memory_space=pltpu.SMEM),
            pl.BlockSpec(memory_space=pltpu.VMEM),
        ],
        out_specs=pl.BlockSpec(memory_space=pltpu.VMEM),
        scratch_shapes=[pltpu.VMEM(x.shape, jnp.float32), pltpu.VMEM(x.shape, jnp.float32)],
    )(pos, order, x)


def mix_kernel(count_x, count_y, x_ref, mixing_ref, o_ref, padded, send_sem, recv_sem, local_sem):
    index_x = lax.axis_index("tx")
    index_y = lax.axis_index("ty")
    size_x, size_y = x_ref.shape[0], x_ref.shape[1]
    mesh_ids = pl.DeviceIdType.MESH
    steps = [(a, b) for a in (-1, 0, 1) for b in (-1, 0, 1) if (a, b) != (0, 0)]

    def inside(px, py):
        return (px >= 0) & (px < count_x) & (py >= 0) & (py < count_y)

    def ranges(step, size):
        if step == 1:
            return pl.ds(size - 1, 1), pl.ds(0, 1)
        if step == -1:
            return pl.ds(0, 1), pl.ds(size + 1, 1)
        return pl.ds(0, size), pl.ds(1, size)

    barrier = pltpu.get_barrier_semaphore()
    for a, b in steps:
        @pl.when(inside(index_x + a, index_y + b))
        def _():
            pl.semaphore_signal(
                barrier, 1, device_id=(index_x + a, index_y + b), device_id_type=mesh_ids
            )
    peers = sum(inside(index_x + a, index_y + b).astype(jnp.int32) for a, b in steps)
    pl.semaphore_wait(barrier, peers)

    center = pltpu.make_async_copy(
        x_ref, padded.at[pl.ds(1, size_x), pl.ds(1, size_y)], local_sem
    )
    center.start()
    copies = []
    for k, (a, b) in enumerate(steps):
        source_x, target_x = ranges(a, size_x)
        source_y, target_y = ranges(b, size_y)
        copy = pltpu.make_async_remote_copy(
            src_ref=x_ref.at[source_x, source_y],
            dst_ref=padded.at[target_x, target_y],
            send_sem=send_sem.at[k],
            recv_sem=recv_sem.at[k],
            device_id=(index_x + a, index_y + b),
            device_id_type=mesh_ids,
        )
        copies.append(copy)
        pl.when(inside(index_x + a, index_y + b))(copy.start)
    for k, (a, b) in enumerate(steps):
        source_x, target_x = ranges(a, size_x)
        source_y, target_y = ranges(b, size_y)

        @pl.when(jnp.logical_not(inside(index_x - a, index_y - b)))
        def _():
            piece = padded.at[target_x, target_y]
            piece[...] = jnp.zeros(piece.shape, piece.dtype)
    for k, (a, b) in enumerate(steps):
        pl.when(inside(index_x + a, index_y + b))(copies[k].wait_send)
        pl.when(inside(index_x - a, index_y - b))(copies[k].wait_recv)
    center.wait()
    for tile_x in range(size_x):
        for tile_y in range(size_y):
            total = x_ref[tile_x, tile_y].astype(jnp.float32)
            for k, (a, b) in enumerate(steps):
                total += jnp.dot(
                    padded[1 + tile_x + a, 1 + tile_y + b],
                    mixing_ref[k],
                    preferred_element_type=jnp.float32,
                )
            o_ref[tile_x, tile_y] = total.astype(o_ref.dtype)


def mix_tiles(block, mixing):
    count_x = lax.axis_size("tx")
    count_y = lax.axis_size("ty")
    shape = (block.shape[0] + 2, block.shape[1] + 2) + block.shape[2:]
    return pl.pallas_call(
        functools.partial(mix_kernel, count_x, count_y),
        out_shape=jax.ShapeDtypeStruct(block.shape, block.dtype),
        in_specs=[pl.BlockSpec(memory_space=pltpu.VMEM)] * 2,
        out_specs=pl.BlockSpec(memory_space=pltpu.VMEM),
        scratch_shapes=[
            pltpu.VMEM(shape, block.dtype),
            pltpu.SemaphoreType.DMA((8,)),
            pltpu.SemaphoreType.DMA((8,)),
            pltpu.SemaphoreType.DMA,
        ],
        compiler_params=pltpu.CompilerParams(collective_id=0, has_side_effects=True),
    )(block, mixing)


def unit_heads(projected, head_count):
    pieces = projected.reshape(
        projected.shape[:-1] + (head_count, projected.shape[-1] // head_count)
    )
    magnitude = jnp.sqrt(jnp.sum(pieces * pieces, axis=-1, keepdims=True) + epsilon)
    return (pieces / magnitude).reshape(projected.shape).astype(jnp.bfloat16)


def unit_rows(projected, head_width):
    width = projected.shape[-1]
    lane_head = lax.broadcasted_iota(jnp.int32, (width, width), 0) // head_width
    column_head = lax.broadcasted_iota(jnp.int32, (width, width), 1) // head_width
    same_head = (lane_head == column_head).astype(jnp.float32)
    totals = jnp.dot(
        projected * projected,
        same_head,
        precision=lax.Precision.HIGHEST,
        preferred_element_type=jnp.float32,
    )
    return (projected / jnp.sqrt(totals + epsilon)).astype(jnp.bfloat16)


def summary_kernel(rows_ref, column_mask_ref, lane_mask_ref, inducing_ref, proj_ref, o_ref):
    width = rows_ref.shape[1]
    head_width = width // HEADS
    tiles = column_mask_ref.shape[1]
    rows = rows_ref[...]
    queries = unit_rows(
        jnp.dot(inducing_ref[...], proj_ref[0], preferred_element_type=jnp.float32), head_width
    )
    keys = unit_rows(jnp.dot(rows, proj_ref[1], preferred_element_type=jnp.float32), head_width)
    values = jnp.dot(rows, proj_ref[2], preferred_element_type=jnp.float32).astype(jnp.bfloat16)
    column_mask = column_mask_ref[...]
    lane_mask = lane_mask_ref[...]
    heads_out = []
    for head_id in range(HEADS):
        lower = head_id * head_width
        upper = lower + head_width
        scores = lax.dot_general(
            queries[:, lower:upper],
            keys[:, lower:upper],
            (((1,), (1,)), ((), ())),
            preferred_element_type=jnp.float32,
        )
        weights = jnp.exp(sharpness * scores)
        rounded = weights.astype(jnp.bfloat16)
        head_values = values[:, lower:upper]
        masked = jnp.concatenate(
            [head_values * column_mask[:, t : t + 1] for t in range(tiles)], axis=1
        )
        numer = jnp.dot(rounded, masked, preferred_element_type=jnp.float32)
        per_tile = []
        for t in range(tiles):
            totals = jnp.sum(weights * lane_mask[t : t + 1, :], axis=1, keepdims=True)
            per_tile.append(numer[:, t * head_width : (t + 1) * head_width] / totals)
        heads_out.append(per_tile)
    inducing = inducing_ref[...].astype(jnp.float32)
    for t in range(tiles):
        attended = jnp.concatenate([heads_out[h][t] for h in range(HEADS)], axis=1)
        attended = attended.astype(jnp.bfloat16)
        o_ref[t] = (
            inducing + jnp.dot(attended, proj_ref[3], preferred_element_type=jnp.float32)
        ).astype(o_ref.dtype)


def summarize(rows, row_mask, inducing, proj):
    tiles = row_mask.shape[1]
    return pl.pallas_call(
        summary_kernel,
        out_shape=jax.ShapeDtypeStruct((tiles,) + inducing.shape, jnp.bfloat16),
        in_specs=[pl.BlockSpec(memory_space=pltpu.VMEM)] * 5,
        out_specs=pl.BlockSpec(memory_space=pltpu.VMEM),
    )(rows, row_mask.astype(jnp.bfloat16), row_mask.T, inducing, proj)


def body(
    points,
    embed_weight,
    inner_weights,
    output_weight,
    counts,
    point_order,
    inducing,
    first_proj,
    second_proj,
    mixing,
):
    along_x = lax.axis_size("tx")
    along_y = lax.axis_size("ty")
    devices = along_x * along_y
    index_x = lax.axis_index("tx")
    index_y = lax.axis_index("ty")
    own_index = index_x * along_y + index_y
    point_count = points.shape[0]
    per_device = TLX * TLY
    width = output_weight.shape[1]
    quota = point_count // devices
    band = quota * along_y
    head_width = width // HEADS
    inducing_count = inducing.shape[0]

    features = point_mlp(points, embed_weight, inner_weights, output_weight, 2048)

    own_counts = lax.dynamic_index_in_dim(counts, own_index, 0, keepdims=False)
    own_offsets = jnp.cumsum(own_counts) - own_counts
    grid_counts = own_counts.reshape(along_x, TLX, along_y, TLY)
    grid_offsets = own_offsets.reshape(along_x, TLX, along_y, TLY)
    band_start = grid_offsets[:, 0, 0, 0][:, None]
    first_len = grid_counts[:, 0, :, 0] + grid_counts[:, 0, :, 1]
    first_start = grid_offsets[:, 0, :, 0] - band_start
    second_start = grid_offsets[:, 1, :, 0] - band_start
    slot_ids = jnp.arange(quota, dtype=jnp.int32)
    local_pos = jnp.where(
        slot_ids[None, None, :] < first_len[:, :, None],
        first_start[:, :, None] + slot_ids[None, None, :],
        second_start[:, :, None] + slot_ids[None, None, :] - first_len[:, :, None],
    ).reshape(along_x, band)
    send_pos = (local_pos + band_start).reshape(-1)
    order = point_order[0]
    outgoing = move_rows(gather_kernel, send_pos, order, features)
    outgoing = outgoing.reshape(devices, quota, width)
    arrived = lax.all_to_all(outgoing, ("tx", "ty"), split_axis=0, concat_axis=0, tiled=True)
    all_rows = arrived.reshape(devices * quota, width)

    inbound = counts.reshape(devices, along_x, TLX, along_y, TLY)
    inbound = lax.dynamic_index_in_dim(inbound, index_x, 1, keepdims=False)
    inbound = lax.dynamic_index_in_dim(inbound, index_y, 2, keepdims=False)
    inbound = inbound.reshape(devices, per_device)
    through = jnp.cumsum(inbound, axis=1)
    row_tile = jnp.sum(
        (slot_ids[None, :, None] >= through[:, None, : per_device - 1]).astype(jnp.int32), axis=2
    ).reshape(-1)
    tile_ids = jnp.arange(per_device, dtype=jnp.int32)
    row_mask = (row_tile[:, None] == tile_ids[None, :]).astype(jnp.float32)

    summary = summarize(all_rows, row_mask, inducing, first_proj)
    tile_grid = summary.reshape(TLX, TLY, inducing_count, width)
    mixture = mix_tiles(tile_grid, mixing)
    mixture = mixture.astype(jnp.bfloat16).reshape(per_device * inducing_count, width)

    point_queries = unit_heads(
        jnp.dot(all_rows, second_proj[0], preferred_element_type=jnp.float32), HEADS
    )
    second_keys = unit_heads(
        jnp.dot(mixture, second_proj[1], preferred_element_type=jnp.float32), HEADS
    )
    second_values = jnp.dot(mixture, second_proj[2], preferred_element_type=jnp.float32).astype(
        jnp.bfloat16
    )
    own_tile = row_mask > 0
    heads_out = []
    for head_id in range(HEADS):
        lower = head_id * head_width
        upper = lower + head_width
        scores = jnp.dot(
            point_queries[:, lower:upper],
            second_keys[:, lower:upper].T,
            preferred_element_type=jnp.float32,
        ).reshape(-1, per_device, inducing_count)
        own_scores = jnp.sum(jnp.where(own_tile[:, :, None], scores, 0.0), axis=1)
        weights = jnp.exp(sharpness * own_scores)
        totals = jnp.sum(weights, axis=1, keepdims=True)
        spread = jnp.where(own_tile[:, :, None], weights[:, None, :], 0.0)
        numer = jnp.dot(
            spread.reshape(-1, per_device * inducing_count).astype(jnp.bfloat16),
            second_values[:, lower:upper],
            preferred_element_type=jnp.float32,
        )
        heads_out.append(numer / totals)
    second_attended = jnp.concatenate(heads_out, axis=1).astype(jnp.bfloat16)
    result = (
        all_rows.astype(jnp.float32)
        + jnp.dot(second_attended, second_proj[3], preferred_element_type=jnp.float32)
    ).astype(jnp.bfloat16)

    coming = lax.all_to_all(
        result.reshape(devices, quota, width), ("tx", "ty"), split_axis=0, concat_axis=0, tiled=True
    )
    returned = move_rows(
        scatter_kernel, send_pos, order, coming.reshape(point_count, width)
    )
    return returned


def solution(mesh):
    placed = (P(("tx", "ty"), None), P(), P(), P(), P(), P(("tx", "ty"), None), P(), P(), P(), P())
    return jax.shard_map(
        body, mesh=mesh, in_specs=placed, out_specs=P(("tx", "ty"), None), check_vma=False
    )
```

```python
import functools

import jax
import jax.numpy as jnp
from jax import lax
from jax.experimental import pallas as pl
from jax.experimental.pallas import tpu as pltpu
from jax.sharding import PartitionSpec as P

HEADS = 2
TLX = 2
TLY = 2


sharpness = 32.0
epsilon = 1e-06
neighbour_steps = ((-1, -1), (-1, 0), (-1, 1), (0, -1), (0, 1), (1, -1), (1, 0), (1, 1))


def mlp_kernel(x_ref, w1_ref, w2_ref, w3_ref, o_ref):
    def silu(v):
        return v / (1.0 + jnp.exp(-v))

    h = silu(jnp.dot(x_ref[...], w1_ref[...], preferred_element_type=jnp.float32))
    h = h.astype(jnp.bfloat16)
    for layer_id in range(w2_ref.shape[0]):
        h = silu(jnp.dot(h, w2_ref[layer_id], preferred_element_type=jnp.float32))
        h = h.astype(jnp.bfloat16)
    o_ref[...] = jnp.dot(h, w3_ref[...], preferred_element_type=jnp.float32).astype(o_ref.dtype)


def point_mlp(x, w1, w2, w3, block):
    rows = x.shape[0]
    full = lambda shape: pl.BlockSpec(shape, lambda i: (0,) * len(shape))
    return pl.pallas_call(
        mlp_kernel,
        out_shape=jax.ShapeDtypeStruct((rows, w3.shape[1]), jnp.bfloat16),
        grid=(rows // block,),
        in_specs=[
            pl.BlockSpec((block, x.shape[1]), lambda i: (i, 0)),
            full(w1.shape),
            full(w2.shape),
            full(w3.shape),
        ],
        out_specs=pl.BlockSpec((block, w3.shape[1]), lambda i: (i, 0)),
    )(x, w1, w2, w3)


def gather_kernel(unroll, pos_ref, order_ref, x_ref, o_ref, rows_in, rows_out):
    rows_in[...] = x_ref[...].astype(jnp.float32)

    def body(step, carry):
        for lane in range(unroll):
            row = step * unroll + lane
            source = order_ref[pos_ref[row]]
            rows_out[pl.ds(row, 1), :] = rows_in[pl.ds(source, 1), :]
        return carry

    lax.fori_loop(0, o_ref.shape[0] // unroll, body, 0)
    o_ref[...] = rows_out[...].astype(o_ref.dtype)


def scatter_kernel(unroll, pos_ref, order_ref, x_ref, o_ref, rows_in, rows_out):
    rows_in[...] = x_ref[...].astype(jnp.float32)

    def body(step, carry):
        for lane in range(unroll):
            row = step * unroll + lane
            target = order_ref[pos_ref[row]]
            rows_out[pl.ds(target, 1), :] = rows_in[pl.ds(row, 1), :]
        return carry

    lax.fori_loop(0, x_ref.shape[0] // unroll, body, 0)
    o_ref[...] = rows_out[...].astype(o_ref.dtype)


def move_rows(kernel, pos, order, x):
    return pl.pallas_call(
        functools.partial(kernel, 64),
        out_shape=jax.ShapeDtypeStruct(x.shape, jnp.bfloat16),
        in_specs=[
            pl.BlockSpec(memory_space=pltpu.SMEM),
            pl.BlockSpec(memory_space=pltpu.SMEM),
            pl.BlockSpec(memory_space=pltpu.VMEM),
        ],
        out_specs=pl.BlockSpec(memory_space=pltpu.VMEM),
        scratch_shapes=[pltpu.VMEM(x.shape, jnp.float32), pltpu.VMEM(x.shape, jnp.float32)],
    )(pos, order, x)


def mix_kernel(count_x, count_y, x_ref, mixing_ref, o_ref, padded, send_sem, recv_sem, local_sem):
    index_x = lax.axis_index("tx")
    index_y = lax.axis_index("ty")
    size_x, size_y = x_ref.shape[0], x_ref.shape[1]
    mesh_ids = pl.DeviceIdType.MESH
    steps = [(a, b) for a in (-1, 0, 1) for b in (-1, 0, 1) if (a, b) != (0, 0)]

    def inside(px, py):
        return (px >= 0) & (px < count_x) & (py >= 0) & (py < count_y)

    def ranges(step, size):
        if step == 1:
            return pl.ds(size - 1, 1), pl.ds(0, 1)
        if step == -1:
            return pl.ds(0, 1), pl.ds(size + 1, 1)
        return pl.ds(0, size), pl.ds(1, size)

    barrier = pltpu.get_barrier_semaphore()
    for a, b in steps:
        @pl.when(inside(index_x + a, index_y + b))
        def _():
            pl.semaphore_signal(
                barrier, 1, device_id=(index_x + a, index_y + b), device_id_type=mesh_ids
            )
    peers = sum(inside(index_x + a, index_y + b).astype(jnp.int32) for a, b in steps)
    pl.semaphore_wait(barrier, peers)

    center = pltpu.make_async_copy(
        x_ref, padded.at[pl.ds(1, size_x), pl.ds(1, size_y)], local_sem
    )
    center.start()
    copies = []
    for k, (a, b) in enumerate(steps):
        source_x, target_x = ranges(a, size_x)
        source_y, target_y = ranges(b, size_y)
        copy = pltpu.make_async_remote_copy(
            src_ref=x_ref.at[source_x, source_y],
            dst_ref=padded.at[target_x, target_y],
            send_sem=send_sem.at[k],
            recv_sem=recv_sem.at[k],
            device_id=(index_x + a, index_y + b),
            device_id_type=mesh_ids,
        )
        copies.append(copy)
        pl.when(inside(index_x + a, index_y + b))(copy.start)
    for k, (a, b) in enumerate(steps):
        source_x, target_x = ranges(a, size_x)
        source_y, target_y = ranges(b, size_y)

        @pl.when(jnp.logical_not(inside(index_x - a, index_y - b)))
        def _():
            piece = padded.at[target_x, target_y]
            piece[...] = jnp.zeros(piece.shape, piece.dtype)
    for k, (a, b) in enumerate(steps):
        pl.when(inside(index_x + a, index_y + b))(copies[k].wait_send)
        pl.when(inside(index_x - a, index_y - b))(copies[k].wait_recv)
    center.wait()
    for tile_x in range(size_x):
        for tile_y in range(size_y):
            total = x_ref[tile_x, tile_y].astype(jnp.float32)
            for k, (a, b) in enumerate(steps):
                total += jnp.dot(
                    padded[1 + tile_x + a, 1 + tile_y + b],
                    mixing_ref[k],
                    preferred_element_type=jnp.float32,
                )
            o_ref[tile_x, tile_y] = total.astype(o_ref.dtype)


def mix_tiles(block, mixing):
    count_x = lax.axis_size("tx")
    count_y = lax.axis_size("ty")
    shape = (block.shape[0] + 2, block.shape[1] + 2) + block.shape[2:]
    return pl.pallas_call(
        functools.partial(mix_kernel, count_x, count_y),
        out_shape=jax.ShapeDtypeStruct(block.shape, block.dtype),
        in_specs=[pl.BlockSpec(memory_space=pltpu.VMEM)] * 2,
        out_specs=pl.BlockSpec(memory_space=pltpu.VMEM),
        scratch_shapes=[
            pltpu.VMEM(shape, block.dtype),
            pltpu.SemaphoreType.DMA((8,)),
            pltpu.SemaphoreType.DMA((8,)),
            pltpu.SemaphoreType.DMA,
        ],
        compiler_params=pltpu.CompilerParams(collective_id=0, has_side_effects=True),
    )(block, mixing)


def unit_heads(projected, head_count):
    pieces = projected.reshape(
        projected.shape[:-1] + (head_count, projected.shape[-1] // head_count)
    )
    magnitude = jnp.sqrt(jnp.sum(pieces * pieces, axis=-1, keepdims=True) + epsilon)
    return (pieces / magnitude).reshape(projected.shape).astype(jnp.bfloat16)


def unit_rows(projected, head_width):
    width = projected.shape[-1]
    lane_head = lax.broadcasted_iota(jnp.int32, (width, width), 0) // head_width
    column_head = lax.broadcasted_iota(jnp.int32, (width, width), 1) // head_width
    same_head = (lane_head == column_head).astype(jnp.float32)
    totals = jnp.dot(
        projected * projected,
        same_head,
        precision=lax.Precision.HIGHEST,
        preferred_element_type=jnp.float32,
    )
    return (projected / jnp.sqrt(totals + epsilon)).astype(jnp.bfloat16)


def summary_kernel(rows_ref, column_mask_ref, lane_mask_ref, inducing_ref, proj_ref, o_ref):
    width = rows_ref.shape[1]
    head_width = width // HEADS
    tiles = column_mask_ref.shape[1]
    rows = rows_ref[...]
    queries = unit_rows(
        jnp.dot(inducing_ref[...], proj_ref[0], preferred_element_type=jnp.float32), head_width
    )
    keys = unit_rows(jnp.dot(rows, proj_ref[1], preferred_element_type=jnp.float32), head_width)
    values = jnp.dot(rows, proj_ref[2], preferred_element_type=jnp.float32).astype(jnp.bfloat16)
    column_mask = column_mask_ref[...]
    lane_mask = lane_mask_ref[...]
    lane_head = lax.broadcasted_iota(jnp.int32, queries.shape, 1) // head_width
    masked = [values * column_mask[:, t : t + 1] for t in range(tiles)]
    attended = [jnp.zeros(queries.shape, jnp.float32) for t in range(tiles)]
    for head_id in range(HEADS):
        in_head = lane_head == head_id
        head_queries = jnp.where(in_head, queries, jnp.zeros_like(queries))
        scores = lax.dot_general(
            head_queries,
            keys,
            (((1,), (1,)), ((), ())),
            preferred_element_type=jnp.float32,
        )
        weights = jnp.exp(sharpness * scores)
        rounded = weights.astype(jnp.bfloat16)
        for t in range(tiles):
            numer = jnp.dot(rounded, masked[t], preferred_element_type=jnp.float32)
            totals = jnp.sum(weights * lane_mask[t : t + 1, :], axis=1, keepdims=True)
            attended[t] = jnp.where(in_head, numer / totals, attended[t])
    inducing = inducing_ref[...].astype(jnp.float32)
    for t in range(tiles):
        o_ref[t] = (
            inducing
            + jnp.dot(
                attended[t].astype(jnp.bfloat16), proj_ref[3], preferred_element_type=jnp.float32
            )
        ).astype(o_ref.dtype)


def summarize(rows, row_mask, inducing, proj):
    tiles = row_mask.shape[1]
    return pl.pallas_call(
        summary_kernel,
        out_shape=jax.ShapeDtypeStruct((tiles,) + inducing.shape, jnp.bfloat16),
        in_specs=[pl.BlockSpec(memory_space=pltpu.VMEM)] * 5,
        out_specs=pl.BlockSpec(memory_space=pltpu.VMEM),
    )(rows, row_mask.astype(jnp.bfloat16), row_mask.T, inducing, proj)


def body(
    points,
    embed_weight,
    inner_weights,
    output_weight,
    counts,
    point_order,
    inducing,
    first_proj,
    second_proj,
    mixing,
):
    along_x = lax.axis_size("tx")
    along_y = lax.axis_size("ty")
    devices = along_x * along_y
    index_x = lax.axis_index("tx")
    index_y = lax.axis_index("ty")
    own_index = index_x * along_y + index_y
    point_count = points.shape[0]
    per_device = TLX * TLY
    width = output_weight.shape[1]
    quota = point_count // devices
    band = quota * along_y
    head_width = width // HEADS
    inducing_count = inducing.shape[0]

    features = point_mlp(points, embed_weight, inner_weights, output_weight, 2048)

    own_counts = lax.dynamic_index_in_dim(counts, own_index, 0, keepdims=False)
    own_offsets = jnp.cumsum(own_counts) - own_counts
    grid_counts = own_counts.reshape(along_x, TLX, along_y, TLY)
    grid_offsets = own_offsets.reshape(along_x, TLX, along_y, TLY)
    band_start = grid_offsets[:, 0, 0, 0][:, None]
    first_len = grid_counts[:, 0, :, 0] + grid_counts[:, 0, :, 1]
    first_start = grid_offsets[:, 0, :, 0] - band_start
    second_start = grid_offsets[:, 1, :, 0] - band_start
    slot_ids = jnp.arange(quota, dtype=jnp.int32)
    local_pos = jnp.where(
        slot_ids[None, None, :] < first_len[:, :, None],
        first_start[:, :, None] + slot_ids[None, None, :],
        second_start[:, :, None] + slot_ids[None, None, :] - first_len[:, :, None],
    ).reshape(along_x, band)
    send_pos = (local_pos + band_start).reshape(-1)
    order = point_order[0]
    outgoing = move_rows(gather_kernel, send_pos, order, features)
    outgoing = outgoing.reshape(devices, quota, width)
    arrived = lax.all_to_all(outgoing, ("tx", "ty"), split_axis=0, concat_axis=0, tiled=True)
    all_rows = arrived.reshape(devices * quota, width)

    inbound = counts.reshape(devices, along_x, TLX, along_y, TLY)
    inbound = lax.dynamic_index_in_dim(inbound, index_x, 1, keepdims=False)
    inbound = lax.dynamic_index_in_dim(inbound, index_y, 2, keepdims=False)
    inbound = inbound.reshape(devices, per_device)
    through = jnp.cumsum(inbound, axis=1)
    row_tile = jnp.sum(
        (slot_ids[None, :, None] >= through[:, None, : per_device - 1]).astype(jnp.int32), axis=2
    ).reshape(-1)
    tile_ids = jnp.arange(per_device, dtype=jnp.int32)
    row_mask = (row_tile[:, None] == tile_ids[None, :]).astype(jnp.float32)

    summary = summarize(all_rows, row_mask, inducing, first_proj)
    tile_grid = summary.reshape(TLX, TLY, inducing_count, width)
    mixture = mix_tiles(tile_grid, mixing)
    mixture = mixture.astype(jnp.bfloat16).reshape(per_device * inducing_count, width)

    point_queries = unit_heads(
        jnp.dot(all_rows, second_proj[0], preferred_element_type=jnp.float32), HEADS
    )
    second_keys = unit_heads(
        jnp.dot(mixture, second_proj[1], preferred_element_type=jnp.float32), HEADS
    )
    second_values = jnp.dot(mixture, second_proj[2], preferred_element_type=jnp.float32).astype(
        jnp.bfloat16
    )
    key_mask = jnp.repeat(row_mask, inducing_count, axis=1)
    heads_out = []
    for head_id in range(HEADS):
        lower = head_id * head_width
        upper = lower + head_width
        scores = jnp.dot(
            point_queries[:, lower:upper],
            second_keys[:, lower:upper].T,
            preferred_element_type=jnp.float32,
        )
        weights = jnp.exp(sharpness * scores) * key_mask
        totals = jnp.sum(weights, axis=1, keepdims=True)
        numer = jnp.dot(
            weights.astype(jnp.bfloat16),
            second_values[:, lower:upper],
            preferred_element_type=jnp.float32,
        )
        heads_out.append(numer / totals)
    second_attended = jnp.concatenate(heads_out, axis=1).astype(jnp.bfloat16)
    result = (
        all_rows.astype(jnp.float32)
        + jnp.dot(second_attended, second_proj[3], preferred_element_type=jnp.float32)
    ).astype(jnp.bfloat16)

    coming = lax.all_to_all(
        result.reshape(devices, quota, width), ("tx", "ty"), split_axis=0, concat_axis=0, tiled=True
    )
    returned = move_rows(
        scatter_kernel, send_pos, order, coming.reshape(point_count, width)
    )
    return returned


def solution(mesh):
    placed = (P(("tx", "ty"), None), P(), P(), P(), P(), P(("tx", "ty"), None), P(), P(), P(), P())
    return jax.shard_map(
        body, mesh=mesh, in_specs=placed, out_specs=P(("tx", "ty"), None), check_vma=False
    )
```

```python
import functools

import jax
import jax.numpy as jnp
from jax import lax
from jax.experimental import pallas as pl
from jax.experimental.pallas import tpu as pltpu
from jax.sharding import PartitionSpec as P

HEADS = 2
TLX = 2
TLY = 2


sharpness = 32.0
epsilon = 1e-06
neighbour_steps = ((-1, -1), (-1, 0), (-1, 1), (0, -1), (0, 1), (1, -1), (1, 0), (1, 1))


def mlp_kernel(x_ref, w1_ref, w2_ref, w3_ref, o_ref):
    def silu(v):
        return v / (1.0 + jnp.exp(-v))

    h = silu(jnp.dot(x_ref[...], w1_ref[...], preferred_element_type=jnp.float32))
    h = h.astype(jnp.bfloat16)
    for layer_id in range(w2_ref.shape[0]):
        h = silu(jnp.dot(h, w2_ref[layer_id], preferred_element_type=jnp.float32))
        h = h.astype(jnp.bfloat16)
    o_ref[...] = jnp.dot(h, w3_ref[...], preferred_element_type=jnp.float32).astype(o_ref.dtype)


def point_mlp(x, w1, w2, w3, block):
    rows = x.shape[0]
    full = lambda shape: pl.BlockSpec(shape, lambda i: (0,) * len(shape))
    return pl.pallas_call(
        mlp_kernel,
        out_shape=jax.ShapeDtypeStruct((rows, w3.shape[1]), jnp.bfloat16),
        grid=(rows // block,),
        in_specs=[
            pl.BlockSpec((block, x.shape[1]), lambda i: (i, 0)),
            full(w1.shape),
            full(w2.shape),
            full(w3.shape),
        ],
        out_specs=pl.BlockSpec((block, w3.shape[1]), lambda i: (i, 0)),
    )(x, w1, w2, w3)


def encode_kernel(unroll, block, pos_ref, order_ref, x_ref, w1_ref, w2_ref, w3_ref, o_ref, rows_in, rows_out):
    def silu(v):
        return v / (1.0 + jnp.exp(-v))

    for start in range(0, x_ref.shape[0], block):
        part = pl.ds(start, block)
        h = silu(jnp.dot(x_ref[part, :], w1_ref[...], preferred_element_type=jnp.float32))
        h = h.astype(jnp.bfloat16)
        for layer_id in range(w2_ref.shape[0]):
            h = silu(jnp.dot(h, w2_ref[layer_id], preferred_element_type=jnp.float32))
            h = h.astype(jnp.bfloat16)
        features = jnp.dot(h, w3_ref[...], preferred_element_type=jnp.float32)
        rows_in[part, :] = features.astype(jnp.bfloat16).astype(jnp.float32)

    def body(step, carry):
        for lane in range(unroll):
            row = step * unroll + lane
            source = order_ref[pos_ref[row]]
            rows_out[pl.ds(row, 1), :] = rows_in[pl.ds(source, 1), :]
        return carry

    lax.fori_loop(0, o_ref.shape[0] // unroll, body, 0)
    o_ref[...] = rows_out[...].astype(o_ref.dtype)


def encode_and_gather(pos, order, x, w1, w2, w3, block):
    shape = (x.shape[0], w3.shape[1])
    return pl.pallas_call(
        functools.partial(encode_kernel, 64, block),
        out_shape=jax.ShapeDtypeStruct(shape, jnp.bfloat16),
        in_specs=[pl.BlockSpec(memory_space=pltpu.SMEM)] * 2
        + [pl.BlockSpec(memory_space=pltpu.VMEM)] * 4,
        out_specs=pl.BlockSpec(memory_space=pltpu.VMEM),
        scratch_shapes=[pltpu.VMEM(shape, jnp.float32), pltpu.VMEM(shape, jnp.float32)],
    )(pos, order, x, w1, w2, w3)


def gather_kernel(unroll, pos_ref, order_ref, x_ref, o_ref, rows_in, rows_out):
    rows_in[...] = x_ref[...].astype(jnp.float32)

    def body(step, carry):
        for lane in range(unroll):
            row = step * unroll + lane
            source = order_ref[pos_ref[row]]
            rows_out[pl.ds(row, 1), :] = rows_in[pl.ds(source, 1), :]
        return carry

    lax.fori_loop(0, o_ref.shape[0] // unroll, body, 0)
    o_ref[...] = rows_out[...].astype(o_ref.dtype)


def scatter_kernel(unroll, pos_ref, order_ref, x_ref, o_ref, rows_in, rows_out):
    rows_in[...] = x_ref[...].astype(jnp.float32)

    def body(step, carry):
        for lane in range(unroll):
            row = step * unroll + lane
            target = order_ref[pos_ref[row]]
            rows_out[pl.ds(target, 1), :] = rows_in[pl.ds(row, 1), :]
        return carry

    lax.fori_loop(0, x_ref.shape[0] // unroll, body, 0)
    o_ref[...] = rows_out[...].astype(o_ref.dtype)


def move_rows(kernel, pos, order, x):
    return pl.pallas_call(
        functools.partial(kernel, 64),
        out_shape=jax.ShapeDtypeStruct(x.shape, jnp.bfloat16),
        in_specs=[
            pl.BlockSpec(memory_space=pltpu.SMEM),
            pl.BlockSpec(memory_space=pltpu.SMEM),
            pl.BlockSpec(memory_space=pltpu.VMEM),
        ],
        out_specs=pl.BlockSpec(memory_space=pltpu.VMEM),
        scratch_shapes=[pltpu.VMEM(x.shape, jnp.float32), pltpu.VMEM(x.shape, jnp.float32)],
    )(pos, order, x)


def mix_kernel(count_x, count_y, x_ref, mixing_ref, o_ref, padded, send_sem, recv_sem, local_sem):
    index_x = lax.axis_index("tx")
    index_y = lax.axis_index("ty")
    size_x, size_y = x_ref.shape[0], x_ref.shape[1]
    mesh_ids = pl.DeviceIdType.MESH
    steps = [(a, b) for a in (-1, 0, 1) for b in (-1, 0, 1) if (a, b) != (0, 0)]

    def inside(px, py):
        return (px >= 0) & (px < count_x) & (py >= 0) & (py < count_y)

    def ranges(step, size):
        if step == 1:
            return pl.ds(size - 1, 1), pl.ds(0, 1)
        if step == -1:
            return pl.ds(0, 1), pl.ds(size + 1, 1)
        return pl.ds(0, size), pl.ds(1, size)

    barrier = pltpu.get_barrier_semaphore()
    for a, b in steps:
        @pl.when(inside(index_x + a, index_y + b))
        def _():
            pl.semaphore_signal(
                barrier, 1, device_id=(index_x + a, index_y + b), device_id_type=mesh_ids
            )
    peers = sum(inside(index_x + a, index_y + b).astype(jnp.int32) for a, b in steps)
    pl.semaphore_wait(barrier, peers)

    center = pltpu.make_async_copy(
        x_ref, padded.at[pl.ds(1, size_x), pl.ds(1, size_y)], local_sem
    )
    center.start()
    copies = []
    for k, (a, b) in enumerate(steps):
        source_x, target_x = ranges(a, size_x)
        source_y, target_y = ranges(b, size_y)
        copy = pltpu.make_async_remote_copy(
            src_ref=x_ref.at[source_x, source_y],
            dst_ref=padded.at[target_x, target_y],
            send_sem=send_sem.at[k],
            recv_sem=recv_sem.at[k],
            device_id=(index_x + a, index_y + b),
            device_id_type=mesh_ids,
        )
        copies.append(copy)
        pl.when(inside(index_x + a, index_y + b))(copy.start)
    for k, (a, b) in enumerate(steps):
        source_x, target_x = ranges(a, size_x)
        source_y, target_y = ranges(b, size_y)

        @pl.when(jnp.logical_not(inside(index_x - a, index_y - b)))
        def _():
            piece = padded.at[target_x, target_y]
            piece[...] = jnp.zeros(piece.shape, piece.dtype)
    for k, (a, b) in enumerate(steps):
        pl.when(inside(index_x + a, index_y + b))(copies[k].wait_send)
        pl.when(inside(index_x - a, index_y - b))(copies[k].wait_recv)
    center.wait()
    for tile_x in range(size_x):
        for tile_y in range(size_y):
            total = x_ref[tile_x, tile_y].astype(jnp.float32)
            for k, (a, b) in enumerate(steps):
                total += jnp.dot(
                    padded[1 + tile_x + a, 1 + tile_y + b],
                    mixing_ref[k],
                    preferred_element_type=jnp.float32,
                )
            o_ref[tile_x, tile_y] = total.astype(o_ref.dtype)


def mix_tiles(block, mixing):
    count_x = lax.axis_size("tx")
    count_y = lax.axis_size("ty")
    shape = (block.shape[0] + 2, block.shape[1] + 2) + block.shape[2:]
    return pl.pallas_call(
        functools.partial(mix_kernel, count_x, count_y),
        out_shape=jax.ShapeDtypeStruct(block.shape, block.dtype),
        in_specs=[pl.BlockSpec(memory_space=pltpu.VMEM)] * 2,
        out_specs=pl.BlockSpec(memory_space=pltpu.VMEM),
        scratch_shapes=[
            pltpu.VMEM(shape, block.dtype),
            pltpu.SemaphoreType.DMA((8,)),
            pltpu.SemaphoreType.DMA((8,)),
            pltpu.SemaphoreType.DMA,
        ],
        compiler_params=pltpu.CompilerParams(collective_id=0, has_side_effects=True),
    )(block, mixing)


def unit_heads(projected, head_count):
    pieces = projected.reshape(
        projected.shape[:-1] + (head_count, projected.shape[-1] // head_count)
    )
    magnitude = jnp.sqrt(jnp.sum(pieces * pieces, axis=-1, keepdims=True) + epsilon)
    return (pieces / magnitude).reshape(projected.shape).astype(jnp.bfloat16)


def unit_rows(projected, head_width):
    width = projected.shape[-1]
    lane_head = lax.broadcasted_iota(jnp.int32, (width, width), 0) // head_width
    column_head = lax.broadcasted_iota(jnp.int32, (width, width), 1) // head_width
    same_head = (lane_head == column_head).astype(jnp.float32)
    totals = jnp.dot(
        projected * projected,
        same_head,
        precision=lax.Precision.HIGHEST,
        preferred_element_type=jnp.float32,
    )
    return (projected / jnp.sqrt(totals + epsilon)).astype(jnp.bfloat16)


def summary_kernel(rows_ref, column_mask_ref, lane_mask_ref, inducing_ref, proj_ref, o_ref):
    width = rows_ref.shape[1]
    head_width = width // HEADS
    tiles = column_mask_ref.shape[1]
    rows = rows_ref[...]
    queries = unit_rows(
        jnp.dot(inducing_ref[...], proj_ref[0], preferred_element_type=jnp.float32), head_width
    )
    keys = unit_rows(jnp.dot(rows, proj_ref[1], preferred_element_type=jnp.float32), head_width)
    values = jnp.dot(rows, proj_ref[2], preferred_element_type=jnp.float32).astype(jnp.bfloat16)
    column_mask = column_mask_ref[...]
    lane_mask = lane_mask_ref[...]
    heads_out = []
    for head_id in range(HEADS):
        lower = head_id * head_width
        upper = lower + head_width
        scores = lax.dot_general(
            queries[:, lower:upper],
            keys[:, lower:upper],
            (((1,), (1,)), ((), ())),
            preferred_element_type=jnp.float32,
        )
        weights = jnp.exp(sharpness * scores)
        rounded = weights.astype(jnp.bfloat16)
        head_values = values[:, lower:upper]
        masked = jnp.concatenate(
            [head_values * column_mask[:, t : t + 1] for t in range(tiles)], axis=1
        )
        numer = jnp.dot(rounded, masked, preferred_element_type=jnp.float32)
        per_tile = []
        for t in range(tiles):
            totals = jnp.sum(weights * lane_mask[t : t + 1, :], axis=1, keepdims=True)
            per_tile.append(numer[:, t * head_width : (t + 1) * head_width] / totals)
        heads_out.append(per_tile)
    inducing = inducing_ref[...].astype(jnp.float32)
    for t in range(tiles):
        attended = jnp.concatenate([heads_out[h][t] for h in range(HEADS)], axis=1)
        attended = attended.astype(jnp.bfloat16)
        o_ref[t] = (
            inducing + jnp.dot(attended, proj_ref[3], preferred_element_type=jnp.float32)
        ).astype(o_ref.dtype)


def summarize(rows, row_mask, inducing, proj):
    tiles = row_mask.shape[1]
    return pl.pallas_call(
        summary_kernel,
        out_shape=jax.ShapeDtypeStruct((tiles,) + inducing.shape, jnp.bfloat16),
        in_specs=[pl.BlockSpec(memory_space=pltpu.VMEM)] * 5,
        out_specs=pl.BlockSpec(memory_space=pltpu.VMEM),
    )(rows, row_mask.astype(jnp.bfloat16), row_mask.T, inducing, proj)


def body(
    points,
    embed_weight,
    inner_weights,
    output_weight,
    counts,
    point_order,
    inducing,
    first_proj,
    second_proj,
    mixing,
):
    along_x = lax.axis_size("tx")
    along_y = lax.axis_size("ty")
    devices = along_x * along_y
    index_x = lax.axis_index("tx")
    index_y = lax.axis_index("ty")
    own_index = index_x * along_y + index_y
    point_count = points.shape[0]
    per_device = TLX * TLY
    width = output_weight.shape[1]
    quota = point_count // devices
    band = quota * along_y
    head_width = width // HEADS
    inducing_count = inducing.shape[0]


    own_counts = lax.dynamic_index_in_dim(counts, own_index, 0, keepdims=False)
    own_offsets = jnp.cumsum(own_counts) - own_counts
    grid_counts = own_counts.reshape(along_x, TLX, along_y, TLY)
    grid_offsets = own_offsets.reshape(along_x, TLX, along_y, TLY)
    band_start = grid_offsets[:, 0, 0, 0][:, None]
    first_len = grid_counts[:, 0, :, 0] + grid_counts[:, 0, :, 1]
    first_start = grid_offsets[:, 0, :, 0] - band_start
    second_start = grid_offsets[:, 1, :, 0] - band_start
    slot_ids = jnp.arange(quota, dtype=jnp.int32)
    local_pos = jnp.where(
        slot_ids[None, None, :] < first_len[:, :, None],
        first_start[:, :, None] + slot_ids[None, None, :],
        second_start[:, :, None] + slot_ids[None, None, :] - first_len[:, :, None],
    ).reshape(along_x, band)
    send_pos = (local_pos + band_start).reshape(-1)
    order = point_order[0]
    outgoing = encode_and_gather(
        send_pos, order, points, embed_weight, inner_weights, output_weight, 2048
    )
    outgoing = outgoing.reshape(devices, quota, width)
    arrived = lax.all_to_all(outgoing, ("tx", "ty"), split_axis=0, concat_axis=0, tiled=True)
    all_rows = arrived.reshape(devices * quota, width)

    inbound = counts.reshape(devices, along_x, TLX, along_y, TLY)
    inbound = lax.dynamic_index_in_dim(inbound, index_x, 1, keepdims=False)
    inbound = lax.dynamic_index_in_dim(inbound, index_y, 2, keepdims=False)
    inbound = inbound.reshape(devices, per_device)
    through = jnp.cumsum(inbound, axis=1)
    row_tile = jnp.sum(
        (slot_ids[None, :, None] >= through[:, None, : per_device - 1]).astype(jnp.int32), axis=2
    ).reshape(-1)
    tile_ids = jnp.arange(per_device, dtype=jnp.int32)
    row_mask = (row_tile[:, None] == tile_ids[None, :]).astype(jnp.float32)

    summary = summarize(all_rows, row_mask, inducing, first_proj)
    tile_grid = summary.reshape(TLX, TLY, inducing_count, width)
    mixture = mix_tiles(tile_grid, mixing)
    mixture = mixture.astype(jnp.bfloat16).reshape(per_device * inducing_count, width)

    point_queries = unit_heads(
        jnp.dot(all_rows, second_proj[0], preferred_element_type=jnp.float32), HEADS
    )
    second_keys = unit_heads(
        jnp.dot(mixture, second_proj[1], preferred_element_type=jnp.float32), HEADS
    )
    second_values = jnp.dot(mixture, second_proj[2], preferred_element_type=jnp.float32).astype(
        jnp.bfloat16
    )
    key_mask = jnp.repeat(row_mask, inducing_count, axis=1)
    heads_out = []
    for head_id in range(HEADS):
        lower = head_id * head_width
        upper = lower + head_width
        scores = jnp.dot(
            point_queries[:, lower:upper],
            second_keys[:, lower:upper].T,
            preferred_element_type=jnp.float32,
        )
        weights = jnp.exp(sharpness * scores) * key_mask
        totals = jnp.sum(weights, axis=1, keepdims=True)
        numer = jnp.dot(
            weights.astype(jnp.bfloat16),
            second_values[:, lower:upper],
            preferred_element_type=jnp.float32,
        )
        heads_out.append(numer / totals)
    second_attended = jnp.concatenate(heads_out, axis=1).astype(jnp.bfloat16)
    result = (
        all_rows.astype(jnp.float32)
        + jnp.dot(second_attended, second_proj[3], preferred_element_type=jnp.float32)
    ).astype(jnp.bfloat16)

    coming = lax.all_to_all(
        result.reshape(devices, quota, width), ("tx", "ty"), split_axis=0, concat_axis=0, tiled=True
    )
    returned = move_rows(
        scatter_kernel, send_pos, order, coming.reshape(point_count, width)
    )
    return returned


def solution(mesh):
    placed = (P(("tx", "ty"), None), P(), P(), P(), P(), P(("tx", "ty"), None), P(), P(), P(), P())
    return jax.shard_map(
        body, mesh=mesh, in_specs=placed, out_specs=P(("tx", "ty"), None), check_vma=False
    )
```

```python
import functools

import jax
import jax.numpy as jnp
from jax import lax
from jax.experimental import pallas as pl
from jax.experimental.pallas import tpu as pltpu
from jax.sharding import PartitionSpec as P

HEADS = 2
TLX = 2
TLY = 2


sharpness = 32.0
epsilon = 1e-06
neighbour_steps = ((-1, -1), (-1, 0), (-1, 1), (0, -1), (0, 1), (1, -1), (1, 0), (1, 1))


def mlp_kernel(x_ref, w1_ref, w2_ref, w3_ref, o_ref):
    def silu(v):
        return v / (1.0 + jnp.exp(-v))

    h = silu(jnp.dot(x_ref[...], w1_ref[...], preferred_element_type=jnp.float32))
    h = h.astype(jnp.bfloat16)
    for layer_id in range(w2_ref.shape[0]):
        h = silu(jnp.dot(h, w2_ref[layer_id], preferred_element_type=jnp.float32))
        h = h.astype(jnp.bfloat16)
    o_ref[...] = jnp.dot(h, w3_ref[...], preferred_element_type=jnp.float32).astype(o_ref.dtype)


def point_mlp(x, w1, w2, w3, block):
    rows = x.shape[0]
    full = lambda shape: pl.BlockSpec(shape, lambda i: (0,) * len(shape))
    return pl.pallas_call(
        mlp_kernel,
        out_shape=jax.ShapeDtypeStruct((rows, w3.shape[1]), jnp.bfloat16),
        grid=(rows // block,),
        in_specs=[
            pl.BlockSpec((block, x.shape[1]), lambda i: (i, 0)),
            full(w1.shape),
            full(w2.shape),
            full(w3.shape),
        ],
        out_specs=pl.BlockSpec((block, w3.shape[1]), lambda i: (i, 0)),
    )(x, w1, w2, w3)


def encode_kernel(unroll, block, pos_ref, order_ref, x_ref, w1_ref, w2_ref, w3_ref, o_ref, rows_in, rows_out):
    def silu(v):
        return v / (1.0 + jnp.exp(-v))

    for start in range(0, x_ref.shape[0], block):
        part = pl.ds(start, block)
        h = silu(jnp.dot(x_ref[part, :], w1_ref[...], preferred_element_type=jnp.float32))
        h = h.astype(jnp.bfloat16)
        for layer_id in range(w2_ref.shape[0]):
            h = silu(jnp.dot(h, w2_ref[layer_id], preferred_element_type=jnp.float32))
            h = h.astype(jnp.bfloat16)
        features = jnp.dot(h, w3_ref[...], preferred_element_type=jnp.float32)
        rows_in[part, :] = features.astype(jnp.bfloat16).astype(jnp.float32)

    def body(step, carry):
        for lane in range(unroll):
            row = step * unroll + lane
            source = order_ref[pos_ref[row]]
            rows_out[pl.ds(row, 1), :] = rows_in[pl.ds(source, 1), :]
        return carry

    lax.fori_loop(0, o_ref.shape[0] // unroll, body, 0)
    o_ref[...] = rows_out[...].astype(o_ref.dtype)


def encode_and_gather(pos, order, x, w1, w2, w3, block):
    shape = (x.shape[0], w3.shape[1])
    return pl.pallas_call(
        functools.partial(encode_kernel, 64, block),
        out_shape=jax.ShapeDtypeStruct(shape, jnp.bfloat16),
        in_specs=[pl.BlockSpec(memory_space=pltpu.SMEM)] * 2
        + [pl.BlockSpec(memory_space=pltpu.VMEM)] * 4,
        out_specs=pl.BlockSpec(memory_space=pltpu.VMEM),
        scratch_shapes=[pltpu.VMEM(shape, jnp.float32), pltpu.VMEM(shape, jnp.float32)],
    )(pos, order, x, w1, w2, w3)


def gather_kernel(unroll, pos_ref, order_ref, x_ref, o_ref, rows_in, rows_out):
    rows_in[...] = x_ref[...].astype(jnp.float32)

    def body(step, carry):
        for lane in range(unroll):
            row = step * unroll + lane
            source = order_ref[pos_ref[row]]
            rows_out[pl.ds(row, 1), :] = rows_in[pl.ds(source, 1), :]
        return carry

    lax.fori_loop(0, o_ref.shape[0] // unroll, body, 0)
    o_ref[...] = rows_out[...].astype(o_ref.dtype)


def scatter_kernel(unroll, pos_ref, order_ref, x_ref, o_ref, rows_in, rows_out):
    rows_in[...] = x_ref[...].astype(jnp.float32)

    def body(step, carry):
        for lane in range(unroll):
            row = step * unroll + lane
            target = order_ref[pos_ref[row]]
            rows_out[pl.ds(target, 1), :] = rows_in[pl.ds(row, 1), :]
        return carry

    lax.fori_loop(0, x_ref.shape[0] // unroll, body, 0)
    o_ref[...] = rows_out[...].astype(o_ref.dtype)


def move_rows(kernel, pos, order, x):
    return pl.pallas_call(
        functools.partial(kernel, 64),
        out_shape=jax.ShapeDtypeStruct(x.shape, jnp.bfloat16),
        in_specs=[
            pl.BlockSpec(memory_space=pltpu.SMEM),
            pl.BlockSpec(memory_space=pltpu.SMEM),
            pl.BlockSpec(memory_space=pltpu.VMEM),
        ],
        out_specs=pl.BlockSpec(memory_space=pltpu.VMEM),
        scratch_shapes=[pltpu.VMEM(x.shape, jnp.float32), pltpu.VMEM(x.shape, jnp.float32)],
    )(pos, order, x)


def mix_kernel(
    count_x,
    count_y,
    rows_ref,
    column_mask_ref,
    lane_mask_ref,
    inducing_ref,
    proj_ref,
    mixing_ref,
    o_ref,
    x_ref,
    padded,
    send_sem,
    recv_sem,
    local_sem,
):
    index_x = lax.axis_index("tx")
    index_y = lax.axis_index("ty")
    size_x, size_y = x_ref.shape[0], x_ref.shape[1]
    mesh_ids = pl.DeviceIdType.MESH
    steps = [(a, b) for a in (-1, 0, 1) for b in (-1, 0, 1) if (a, b) != (0, 0)]

    def inside(px, py):
        return (px >= 0) & (px < count_x) & (py >= 0) & (py < count_y)

    def ranges(step, size):
        if step == 1:
            return pl.ds(size - 1, 1), pl.ds(0, 1)
        if step == -1:
            return pl.ds(0, 1), pl.ds(size + 1, 1)
        return pl.ds(0, size), pl.ds(1, size)

    barrier = pltpu.get_barrier_semaphore()
    for a, b in steps:
        @pl.when(inside(index_x + a, index_y + b))
        def _():
            pl.semaphore_signal(
                barrier, 1, device_id=(index_x + a, index_y + b), device_id_type=mesh_ids
            )
    def store(t, value):
        x_ref[t // size_y, t % size_y] = value

    summary_body(rows_ref, column_mask_ref, lane_mask_ref, inducing_ref, proj_ref, store)
    peers = sum(inside(index_x + a, index_y + b).astype(jnp.int32) for a, b in steps)
    pl.semaphore_wait(barrier, peers)

    center = pltpu.make_async_copy(
        x_ref, padded.at[pl.ds(1, size_x), pl.ds(1, size_y)], local_sem
    )
    center.start()
    copies = []
    for k, (a, b) in enumerate(steps):
        source_x, target_x = ranges(a, size_x)
        source_y, target_y = ranges(b, size_y)
        copy = pltpu.make_async_remote_copy(
            src_ref=x_ref.at[source_x, source_y],
            dst_ref=padded.at[target_x, target_y],
            send_sem=send_sem.at[k],
            recv_sem=recv_sem.at[k],
            device_id=(index_x + a, index_y + b),
            device_id_type=mesh_ids,
        )
        copies.append(copy)
        pl.when(inside(index_x + a, index_y + b))(copy.start)
    for k, (a, b) in enumerate(steps):
        source_x, target_x = ranges(a, size_x)
        source_y, target_y = ranges(b, size_y)

        @pl.when(jnp.logical_not(inside(index_x - a, index_y - b)))
        def _():
            piece = padded.at[target_x, target_y]
            piece[...] = jnp.zeros(piece.shape, piece.dtype)
    for k, (a, b) in enumerate(steps):
        pl.when(inside(index_x + a, index_y + b))(copies[k].wait_send)
        pl.when(inside(index_x - a, index_y - b))(copies[k].wait_recv)
    center.wait()
    for tile_x in range(size_x):
        for tile_y in range(size_y):
            total = x_ref[tile_x, tile_y].astype(jnp.float32)
            for k, (a, b) in enumerate(steps):
                total += jnp.dot(
                    padded[1 + tile_x + a, 1 + tile_y + b],
                    mixing_ref[k],
                    preferred_element_type=jnp.float32,
                )
            o_ref[tile_x, tile_y] = total.astype(o_ref.dtype)


def mix_tiles(rows, row_mask, inducing, first_proj, mixing):
    count_x = lax.axis_size("tx")
    count_y = lax.axis_size("ty")
    tiles = (TLX, TLY) + inducing.shape
    shape = (TLX + 2, TLY + 2) + inducing.shape
    return pl.pallas_call(
        functools.partial(mix_kernel, count_x, count_y),
        out_shape=jax.ShapeDtypeStruct(tiles, jnp.bfloat16),
        in_specs=[pl.BlockSpec(memory_space=pltpu.VMEM)] * 6,
        out_specs=pl.BlockSpec(memory_space=pltpu.VMEM),
        scratch_shapes=[
            pltpu.VMEM(tiles, jnp.bfloat16),
            pltpu.VMEM(shape, jnp.bfloat16),
            pltpu.SemaphoreType.DMA((8,)),
            pltpu.SemaphoreType.DMA((8,)),
            pltpu.SemaphoreType.DMA,
        ],
        compiler_params=pltpu.CompilerParams(collective_id=0, has_side_effects=True),
    )(rows, row_mask.astype(jnp.bfloat16), row_mask.T, inducing, first_proj, mixing)


def unit_heads(projected, head_count):
    pieces = projected.reshape(
        projected.shape[:-1] + (head_count, projected.shape[-1] // head_count)
    )
    magnitude = jnp.sqrt(jnp.sum(pieces * pieces, axis=-1, keepdims=True) + epsilon)
    return (pieces / magnitude).reshape(projected.shape).astype(jnp.bfloat16)


def unit_rows(projected, head_width):
    width = projected.shape[-1]
    lane_head = lax.broadcasted_iota(jnp.int32, (width, width), 0) // head_width
    column_head = lax.broadcasted_iota(jnp.int32, (width, width), 1) // head_width
    same_head = (lane_head == column_head).astype(jnp.float32)
    totals = jnp.dot(
        projected * projected,
        same_head,
        precision=lax.Precision.HIGHEST,
        preferred_element_type=jnp.float32,
    )
    return (projected / jnp.sqrt(totals + epsilon)).astype(jnp.bfloat16)


def summary_body(rows_ref, column_mask_ref, lane_mask_ref, inducing_ref, proj_ref, store):
    width = rows_ref.shape[1]
    head_width = width // HEADS
    tiles = column_mask_ref.shape[1]
    rows = rows_ref[...]
    queries = unit_rows(
        jnp.dot(inducing_ref[...], proj_ref[0], preferred_element_type=jnp.float32), head_width
    )
    keys = unit_rows(jnp.dot(rows, proj_ref[1], preferred_element_type=jnp.float32), head_width)
    values = jnp.dot(rows, proj_ref[2], preferred_element_type=jnp.float32).astype(jnp.bfloat16)
    column_mask = column_mask_ref[...]
    lane_mask = lane_mask_ref[...]
    heads_out = []
    for head_id in range(HEADS):
        lower = head_id * head_width
        upper = lower + head_width
        scores = lax.dot_general(
            queries[:, lower:upper],
            keys[:, lower:upper],
            (((1,), (1,)), ((), ())),
            preferred_element_type=jnp.float32,
        )
        weights = jnp.exp(sharpness * scores)
        rounded = weights.astype(jnp.bfloat16)
        head_values = values[:, lower:upper]
        masked = jnp.concatenate(
            [head_values * column_mask[:, t : t + 1] for t in range(tiles)], axis=1
        )
        numer = jnp.dot(rounded, masked, preferred_element_type=jnp.float32)
        per_tile = []
        for t in range(tiles):
            totals = jnp.sum(weights * lane_mask[t : t + 1, :], axis=1, keepdims=True)
            per_tile.append(numer[:, t * head_width : (t + 1) * head_width] / totals)
        heads_out.append(per_tile)
    inducing = inducing_ref[...].astype(jnp.float32)
    for t in range(tiles):
        attended = jnp.concatenate([heads_out[h][t] for h in range(HEADS)], axis=1)
        attended = attended.astype(jnp.bfloat16)
        store(
            t,
            (inducing + jnp.dot(attended, proj_ref[3], preferred_element_type=jnp.float32)).astype(
                jnp.bfloat16
            ),
        )


def body(
    points,
    embed_weight,
    inner_weights,
    output_weight,
    counts,
    point_order,
    inducing,
    first_proj,
    second_proj,
    mixing,
):
    along_x = lax.axis_size("tx")
    along_y = lax.axis_size("ty")
    devices = along_x * along_y
    index_x = lax.axis_index("tx")
    index_y = lax.axis_index("ty")
    own_index = index_x * along_y + index_y
    point_count = points.shape[0]
    per_device = TLX * TLY
    width = output_weight.shape[1]
    quota = point_count // devices
    band = quota * along_y
    head_width = width // HEADS
    inducing_count = inducing.shape[0]


    own_counts = lax.dynamic_index_in_dim(counts, own_index, 0, keepdims=False)
    own_offsets = jnp.cumsum(own_counts) - own_counts
    grid_counts = own_counts.reshape(along_x, TLX, along_y, TLY)
    grid_offsets = own_offsets.reshape(along_x, TLX, along_y, TLY)
    band_start = grid_offsets[:, 0, 0, 0][:, None]
    first_len = grid_counts[:, 0, :, 0] + grid_counts[:, 0, :, 1]
    first_start = grid_offsets[:, 0, :, 0] - band_start
    second_start = grid_offsets[:, 1, :, 0] - band_start
    slot_ids = jnp.arange(quota, dtype=jnp.int32)
    local_pos = jnp.where(
        slot_ids[None, None, :] < first_len[:, :, None],
        first_start[:, :, None] + slot_ids[None, None, :],
        second_start[:, :, None] + slot_ids[None, None, :] - first_len[:, :, None],
    ).reshape(along_x, band)
    send_pos = (local_pos + band_start).reshape(-1)
    order = point_order[0]
    outgoing = encode_and_gather(
        send_pos, order, points, embed_weight, inner_weights, output_weight, 2048
    )
    outgoing = outgoing.reshape(devices, quota, width)
    arrived = lax.all_to_all(outgoing, ("tx", "ty"), split_axis=0, concat_axis=0, tiled=True)
    all_rows = arrived.reshape(devices * quota, width)

    inbound = counts.reshape(devices, along_x, TLX, along_y, TLY)
    inbound = lax.dynamic_index_in_dim(inbound, index_x, 1, keepdims=False)
    inbound = lax.dynamic_index_in_dim(inbound, index_y, 2, keepdims=False)
    inbound = inbound.reshape(devices, per_device)
    through = jnp.cumsum(inbound, axis=1)
    row_tile = jnp.sum(
        (slot_ids[None, :, None] >= through[:, None, : per_device - 1]).astype(jnp.int32), axis=2
    ).reshape(-1)
    tile_ids = jnp.arange(per_device, dtype=jnp.int32)
    row_mask = (row_tile[:, None] == tile_ids[None, :]).astype(jnp.float32)

    mixture = mix_tiles(all_rows, row_mask, inducing, first_proj, mixing)
    mixture = mixture.astype(jnp.bfloat16).reshape(per_device * inducing_count, width)

    point_queries = unit_heads(
        jnp.dot(all_rows, second_proj[0], preferred_element_type=jnp.float32), HEADS
    )
    second_keys = unit_heads(
        jnp.dot(mixture, second_proj[1], preferred_element_type=jnp.float32), HEADS
    )
    second_values = jnp.dot(mixture, second_proj[2], preferred_element_type=jnp.float32).astype(
        jnp.bfloat16
    )
    key_mask = jnp.repeat(row_mask, inducing_count, axis=1)
    heads_out = []
    for head_id in range(HEADS):
        lower = head_id * head_width
        upper = lower + head_width
        scores = jnp.dot(
            point_queries[:, lower:upper],
            second_keys[:, lower:upper].T,
            preferred_element_type=jnp.float32,
        )
        weights = jnp.exp(sharpness * scores) * key_mask
        totals = jnp.sum(weights, axis=1, keepdims=True)
        numer = jnp.dot(
            weights.astype(jnp.bfloat16),
            second_values[:, lower:upper],
            preferred_element_type=jnp.float32,
        )
        heads_out.append(numer / totals)
    second_attended = jnp.concatenate(heads_out, axis=1).astype(jnp.bfloat16)
    result = (
        all_rows.astype(jnp.float32)
        + jnp.dot(second_attended, second_proj[3], preferred_element_type=jnp.float32)
    ).astype(jnp.bfloat16)

    coming = lax.all_to_all(
        result.reshape(devices, quota, width), ("tx", "ty"), split_axis=0, concat_axis=0, tiled=True
    )
    returned = move_rows(
        scatter_kernel, send_pos, order, coming.reshape(point_count, width)
    )
    return returned


def solution(mesh):
    placed = (P(("tx", "ty"), None), P(), P(), P(), P(), P(("tx", "ty"), None), P(), P(), P(), P())
    return jax.shard_map(
        body, mesh=mesh, in_specs=placed, out_specs=P(("tx", "ty"), None), check_vma=False
    )
```

```python
import functools

import jax
import jax.numpy as jnp
from jax import lax
from jax.experimental import pallas as pl
from jax.experimental.pallas import tpu as pltpu
from jax.sharding import PartitionSpec as P

HEADS = 2
TLX = 2
TLY = 2


sharpness = 32.0
epsilon = 1e-06
neighbour_steps = ((-1, -1), (-1, 0), (-1, 1), (0, -1), (0, 1), (1, -1), (1, 0), (1, 1))


def mlp_kernel(x_ref, w1_ref, w2_ref, w3_ref, o_ref):
    def silu(v):
        return v / (1.0 + jnp.exp(-v))

    h = silu(jnp.dot(x_ref[...], w1_ref[...], preferred_element_type=jnp.float32))
    h = h.astype(jnp.bfloat16)
    for layer_id in range(w2_ref.shape[0]):
        h = silu(jnp.dot(h, w2_ref[layer_id], preferred_element_type=jnp.float32))
        h = h.astype(jnp.bfloat16)
    o_ref[...] = jnp.dot(h, w3_ref[...], preferred_element_type=jnp.float32).astype(o_ref.dtype)


def point_mlp(x, w1, w2, w3, block):
    rows = x.shape[0]
    full = lambda shape: pl.BlockSpec(shape, lambda i: (0,) * len(shape))
    return pl.pallas_call(
        mlp_kernel,
        out_shape=jax.ShapeDtypeStruct((rows, w3.shape[1]), jnp.bfloat16),
        grid=(rows // block,),
        in_specs=[
            pl.BlockSpec((block, x.shape[1]), lambda i: (i, 0)),
            full(w1.shape),
            full(w2.shape),
            full(w3.shape),
        ],
        out_specs=pl.BlockSpec((block, w3.shape[1]), lambda i: (i, 0)),
    )(x, w1, w2, w3)


def encode_kernel(unroll, block, pos_ref, order_ref, x_ref, w1_ref, w2_ref, w3_ref, o_ref, rows_in, rows_out):
    def silu(v):
        return v / (1.0 + jnp.exp(-v))

    for start in range(0, x_ref.shape[0], block):
        part = pl.ds(start, block)
        h = silu(jnp.dot(x_ref[part, :], w1_ref[...], preferred_element_type=jnp.float32))
        h = h.astype(jnp.bfloat16)
        for layer_id in range(w2_ref.shape[0]):
            h = silu(jnp.dot(h, w2_ref[layer_id], preferred_element_type=jnp.float32))
            h = h.astype(jnp.bfloat16)
        features = jnp.dot(h, w3_ref[...], preferred_element_type=jnp.float32)
        rows_in[part, :] = features.astype(jnp.bfloat16).astype(jnp.float32)

    def body(step, carry):
        for lane in range(unroll):
            row = step * unroll + lane
            source = order_ref[pos_ref[row]]
            rows_out[pl.ds(row, 1), :] = rows_in[pl.ds(source, 1), :]
        return carry

    lax.fori_loop(0, o_ref.shape[0] // unroll, body, 0)
    o_ref[...] = rows_out[...].astype(o_ref.dtype)


def encode_and_gather(pos, order, x, w1, w2, w3, block):
    shape = (x.shape[0], w3.shape[1])
    return pl.pallas_call(
        functools.partial(encode_kernel, 64, block),
        out_shape=jax.ShapeDtypeStruct(shape, jnp.bfloat16),
        in_specs=[pl.BlockSpec(memory_space=pltpu.SMEM)] * 2
        + [pl.BlockSpec(memory_space=pltpu.VMEM)] * 4,
        out_specs=pl.BlockSpec(memory_space=pltpu.VMEM),
        scratch_shapes=[pltpu.VMEM(shape, jnp.float32), pltpu.VMEM(shape, jnp.float32)],
    )(pos, order, x, w1, w2, w3)


def gather_kernel(unroll, pos_ref, order_ref, x_ref, o_ref, rows_in, rows_out):
    rows_in[...] = x_ref[...].astype(jnp.float32)

    def body(step, carry):
        for lane in range(unroll):
            row = step * unroll + lane
            source = order_ref[pos_ref[row]]
            rows_out[pl.ds(row, 1), :] = rows_in[pl.ds(source, 1), :]
        return carry

    lax.fori_loop(0, o_ref.shape[0] // unroll, body, 0)
    o_ref[...] = rows_out[...].astype(o_ref.dtype)


def scatter_kernel(unroll, pos_ref, order_ref, x_ref, o_ref, rows_in, rows_out):
    rows_in[...] = x_ref[...].astype(jnp.float32)

    def body(step, carry):
        for lane in range(unroll):
            row = step * unroll + lane
            target = order_ref[pos_ref[row]]
            rows_out[pl.ds(target, 1), :] = rows_in[pl.ds(row, 1), :]
        return carry

    lax.fori_loop(0, x_ref.shape[0] // unroll, body, 0)
    o_ref[...] = rows_out[...].astype(o_ref.dtype)


def move_rows(kernel, pos, order, x):
    return pl.pallas_call(
        functools.partial(kernel, 64),
        out_shape=jax.ShapeDtypeStruct(x.shape, jnp.bfloat16),
        in_specs=[
            pl.BlockSpec(memory_space=pltpu.SMEM),
            pl.BlockSpec(memory_space=pltpu.SMEM),
            pl.BlockSpec(memory_space=pltpu.VMEM),
        ],
        out_specs=pl.BlockSpec(memory_space=pltpu.VMEM),
        scratch_shapes=[pltpu.VMEM(x.shape, jnp.float32), pltpu.VMEM(x.shape, jnp.float32)],
    )(pos, order, x)


def mix_kernel(
    count_x,
    count_y,
    rows_ref,
    column_mask_ref,
    lane_mask_ref,
    inducing_ref,
    proj_ref,
    mixing_ref,
    o_ref,
    x_ref,
    padded,
    send_sem,
    recv_sem,
    local_sem,
):
    index_x = lax.axis_index("tx")
    index_y = lax.axis_index("ty")
    size_x, size_y = x_ref.shape[0], x_ref.shape[1]
    mesh_ids = pl.DeviceIdType.MESH
    steps = [(a, b) for a in (-1, 0, 1) for b in (-1, 0, 1) if (a, b) != (0, 0)]

    def inside(px, py):
        return (px >= 0) & (px < count_x) & (py >= 0) & (py < count_y)

    def ranges(step, size):
        if step == 1:
            return pl.ds(size - 1, 1), pl.ds(0, 1)
        if step == -1:
            return pl.ds(0, 1), pl.ds(size + 1, 1)
        return pl.ds(0, size), pl.ds(1, size)

    barrier = pltpu.get_barrier_semaphore()
    for a, b in steps:
        @pl.when(inside(index_x + a, index_y + b))
        def _():
            pl.semaphore_signal(
                barrier, 1, device_id=(index_x + a, index_y + b), device_id_type=mesh_ids
            )
    def store(t, value):
        x_ref[t // size_y, t % size_y] = value

    summary_body(rows_ref, column_mask_ref, lane_mask_ref, inducing_ref, proj_ref, store)
    peers = sum(inside(index_x + a, index_y + b).astype(jnp.int32) for a, b in steps)
    pl.semaphore_wait(barrier, peers)

    center = pltpu.make_async_copy(
        x_ref, padded.at[pl.ds(1, size_x), pl.ds(1, size_y)], local_sem
    )
    center.start()
    copies = []
    for k, (a, b) in enumerate(steps):
        source_x, target_x = ranges(a, size_x)
        source_y, target_y = ranges(b, size_y)
        copy = pltpu.make_async_remote_copy(
            src_ref=x_ref.at[source_x, source_y],
            dst_ref=padded.at[target_x, target_y],
            send_sem=send_sem.at[k],
            recv_sem=recv_sem.at[k],
            device_id=(index_x + a, index_y + b),
            device_id_type=mesh_ids,
        )
        copies.append(copy)
        pl.when(inside(index_x + a, index_y + b))(copy.start)
    for k, (a, b) in enumerate(steps):
        source_x, target_x = ranges(a, size_x)
        source_y, target_y = ranges(b, size_y)

        @pl.when(jnp.logical_not(inside(index_x - a, index_y - b)))
        def _():
            piece = padded.at[target_x, target_y]
            piece[...] = jnp.zeros(piece.shape, piece.dtype)
    for k, (a, b) in enumerate(steps):
        pl.when(inside(index_x + a, index_y + b))(copies[k].wait_send)
        pl.when(inside(index_x - a, index_y - b))(copies[k].wait_recv)
    center.wait()
    for tile_x in range(size_x):
        for tile_y in range(size_y):
            total = x_ref[tile_x, tile_y].astype(jnp.float32)
            for k, (a, b) in enumerate(steps):
                total += jnp.dot(
                    padded[1 + tile_x + a, 1 + tile_y + b],
                    mixing_ref[k],
                    preferred_element_type=jnp.float32,
                )
            o_ref[tile_x, tile_y] = total.astype(o_ref.dtype)


def mix_tiles(rows, row_mask, inducing, first_proj, mixing):
    count_x = lax.axis_size("tx")
    count_y = lax.axis_size("ty")
    tiles = (TLX, TLY) + inducing.shape
    shape = (TLX + 2, TLY + 2) + inducing.shape
    return pl.pallas_call(
        functools.partial(mix_kernel, count_x, count_y),
        out_shape=jax.ShapeDtypeStruct(tiles, jnp.bfloat16),
        in_specs=[pl.BlockSpec(memory_space=pltpu.VMEM)] * 6,
        out_specs=pl.BlockSpec(memory_space=pltpu.VMEM),
        scratch_shapes=[
            pltpu.VMEM(tiles, jnp.bfloat16),
            pltpu.VMEM(shape, jnp.bfloat16),
            pltpu.SemaphoreType.DMA((8,)),
            pltpu.SemaphoreType.DMA((8,)),
            pltpu.SemaphoreType.DMA,
        ],
        compiler_params=pltpu.CompilerParams(collective_id=0, has_side_effects=True),
    )(rows, row_mask.astype(jnp.bfloat16), row_mask.T, inducing, first_proj, mixing)


def unit_heads(projected, head_count):
    pieces = projected.reshape(
        projected.shape[:-1] + (head_count, projected.shape[-1] // head_count)
    )
    magnitude = jnp.sqrt(jnp.sum(pieces * pieces, axis=-1, keepdims=True) + epsilon)
    return (pieces / magnitude).reshape(projected.shape).astype(jnp.bfloat16)


def unit_rows(projected, head_width):
    width = projected.shape[-1]
    lane_head = lax.broadcasted_iota(jnp.int32, (width, width), 0) // head_width
    column_head = lax.broadcasted_iota(jnp.int32, (width, width), 1) // head_width
    same_head = (lane_head == column_head).astype(jnp.float32)
    totals = jnp.dot(
        projected * projected,
        same_head,
        precision=lax.Precision.HIGHEST,
        preferred_element_type=jnp.float32,
    )
    return (projected / jnp.sqrt(totals + epsilon)).astype(jnp.bfloat16)


def summary_body(rows_ref, column_mask_ref, lane_mask_ref, inducing_ref, proj_ref, store):
    width = rows_ref.shape[1]
    head_width = width // HEADS
    tiles = column_mask_ref.shape[1]
    rows = rows_ref[...]
    queries = unit_rows(
        jnp.dot(inducing_ref[...], proj_ref[0], preferred_element_type=jnp.float32), head_width
    )
    keys = unit_rows(jnp.dot(rows, proj_ref[1], preferred_element_type=jnp.float32), head_width)
    values = jnp.dot(rows, proj_ref[2], preferred_element_type=jnp.float32).astype(jnp.bfloat16)
    column_mask = column_mask_ref[...]
    lane_mask = lane_mask_ref[...]
    heads_out = []
    for head_id in range(HEADS):
        lower = head_id * head_width
        upper = lower + head_width
        scores = lax.dot_general(
            queries[:, lower:upper],
            keys[:, lower:upper],
            (((1,), (1,)), ((), ())),
            preferred_element_type=jnp.float32,
        )
        weights = jnp.exp(sharpness * scores)
        rounded = weights.astype(jnp.bfloat16)
        head_values = values[:, lower:upper]
        masked = jnp.concatenate(
            [head_values * column_mask[:, t : t + 1] for t in range(tiles)], axis=1
        )
        numer = jnp.dot(rounded, masked, preferred_element_type=jnp.float32)
        per_tile = []
        for t in range(tiles):
            totals = jnp.sum(weights * lane_mask[t : t + 1, :], axis=1, keepdims=True)
            per_tile.append(numer[:, t * head_width : (t + 1) * head_width] / totals)
        heads_out.append(per_tile)
    inducing = inducing_ref[...].astype(jnp.float32)
    for t in range(tiles):
        attended = jnp.concatenate([heads_out[h][t] for h in range(HEADS)], axis=1)
        attended = attended.astype(jnp.bfloat16)
        store(
            t,
            (inducing + jnp.dot(attended, proj_ref[3], preferred_element_type=jnp.float32)).astype(
                jnp.bfloat16
            ),
        )


def body(
    points,
    embed_weight,
    inner_weights,
    output_weight,
    counts,
    point_order,
    inducing,
    first_proj,
    second_proj,
    mixing,
):
    along_x = lax.axis_size("tx")
    along_y = lax.axis_size("ty")
    devices = along_x * along_y
    index_x = lax.axis_index("tx")
    index_y = lax.axis_index("ty")
    own_index = index_x * along_y + index_y
    point_count = points.shape[0]
    per_device = TLX * TLY
    width = output_weight.shape[1]
    quota = point_count // devices
    band = quota * along_y
    head_width = width // HEADS
    inducing_count = inducing.shape[0]


    own_counts = lax.dynamic_index_in_dim(counts, own_index, 0, keepdims=False)
    band_counts = own_counts.reshape(along_x, -1)
    band_offsets = jnp.cumsum(band_counts, axis=1) - band_counts
    grid_counts = own_counts.reshape(along_x, TLX, along_y, TLY)
    grid_offsets = band_offsets.reshape(along_x, TLX, along_y, TLY)
    band_start = (jnp.arange(along_x, dtype=jnp.int32) * band)[:, None]
    first_len = grid_counts[:, 0, :, 0] + grid_counts[:, 0, :, 1]
    first_start = grid_offsets[:, 0, :, 0]
    second_start = grid_offsets[:, 1, :, 0]
    slot_ids = jnp.arange(quota, dtype=jnp.int32)
    local_pos = jnp.where(
        slot_ids[None, None, :] < first_len[:, :, None],
        first_start[:, :, None] + slot_ids[None, None, :],
        second_start[:, :, None] + slot_ids[None, None, :] - first_len[:, :, None],
    ).reshape(along_x, band)
    send_pos = (local_pos + band_start).reshape(-1)
    order = point_order[0]
    outgoing = encode_and_gather(
        send_pos, order, points, embed_weight, inner_weights, output_weight, 2048
    )
    outgoing = outgoing.reshape(devices, quota, width)
    arrived = lax.all_to_all(outgoing, ("tx", "ty"), split_axis=0, concat_axis=0, tiled=True)
    all_rows = arrived.reshape(devices * quota, width)

    inbound = counts.reshape(devices, along_x, TLX, along_y, TLY)
    inbound = lax.dynamic_index_in_dim(inbound, index_x, 1, keepdims=False)
    inbound = lax.dynamic_index_in_dim(inbound, index_y, 2, keepdims=False)
    inbound = inbound.reshape(devices, per_device)
    through = jnp.cumsum(inbound, axis=1)
    row_tile = jnp.sum(
        (slot_ids[None, :, None] >= through[:, None, : per_device - 1]).astype(jnp.int32), axis=2
    ).reshape(-1)
    tile_ids = jnp.arange(per_device, dtype=jnp.int32)
    row_mask = (row_tile[:, None] == tile_ids[None, :]).astype(jnp.float32)

    mixture = mix_tiles(all_rows, row_mask, inducing, first_proj, mixing)
    mixture = mixture.astype(jnp.bfloat16).reshape(per_device * inducing_count, width)

    point_queries = unit_heads(
        jnp.dot(all_rows, second_proj[0], preferred_element_type=jnp.float32), HEADS
    )
    second_keys = unit_heads(
        jnp.dot(mixture, second_proj[1], preferred_element_type=jnp.float32), HEADS
    )
    second_values = jnp.dot(mixture, second_proj[2], preferred_element_type=jnp.float32).astype(
        jnp.bfloat16
    )
    key_mask = jnp.repeat(row_mask, inducing_count, axis=1)
    heads_out = []
    for head_id in range(HEADS):
        lower = head_id * head_width
        upper = lower + head_width
        scores = jnp.dot(
            point_queries[:, lower:upper],
            second_keys[:, lower:upper].T,
            preferred_element_type=jnp.float32,
        )
        weights = jnp.exp(sharpness * scores) * key_mask
        totals = jnp.sum(weights, axis=1, keepdims=True)
        numer = jnp.dot(
            weights.astype(jnp.bfloat16),
            second_values[:, lower:upper],
            preferred_element_type=jnp.float32,
        )
        heads_out.append(numer / totals)
    second_attended = jnp.concatenate(heads_out, axis=1).astype(jnp.bfloat16)
    result = (
        all_rows.astype(jnp.float32)
        + jnp.dot(second_attended, second_proj[3], preferred_element_type=jnp.float32)
    ).astype(jnp.bfloat16)

    coming = lax.all_to_all(
        result.reshape(devices, quota, width), ("tx", "ty"), split_axis=0, concat_axis=0, tiled=True
    )
    returned = move_rows(
        scatter_kernel, send_pos, order, coming.reshape(point_count, width)
    )
    return returned


def solution(mesh):
    placed = (P(("tx", "ty"), None), P(), P(), P(), P(), P(("tx", "ty"), None), P(), P(), P(), P())
    return jax.shard_map(
        body, mesh=mesh, in_specs=placed, out_specs=P(("tx", "ty"), None), check_vma=False
    )
```

```python
import functools

import jax
import jax.numpy as jnp
from jax import lax
from jax.experimental import pallas as pl
from jax.experimental.pallas import tpu as pltpu
from jax.sharding import PartitionSpec as P

HEADS = 2
TLX = 2
TLY = 2


sharpness = 32.0
epsilon = 1e-06
neighbour_steps = ((-1, -1), (-1, 0), (-1, 1), (0, -1), (0, 1), (1, -1), (1, 0), (1, 1))


def mlp_kernel(x_ref, w1_ref, w2_ref, w3_ref, o_ref):
    def silu(v):
        return v / (1.0 + jnp.exp(-v))

    h = silu(jnp.dot(x_ref[...], w1_ref[...], preferred_element_type=jnp.float32))
    h = h.astype(jnp.bfloat16)
    for layer_id in range(w2_ref.shape[0]):
        h = silu(jnp.dot(h, w2_ref[layer_id], preferred_element_type=jnp.float32))
        h = h.astype(jnp.bfloat16)
    o_ref[...] = jnp.dot(h, w3_ref[...], preferred_element_type=jnp.float32).astype(o_ref.dtype)


def point_mlp(x, w1, w2, w3, block):
    rows = x.shape[0]
    full = lambda shape: pl.BlockSpec(shape, lambda i: (0,) * len(shape))
    return pl.pallas_call(
        mlp_kernel,
        out_shape=jax.ShapeDtypeStruct((rows, w3.shape[1]), jnp.bfloat16),
        grid=(rows // block,),
        in_specs=[
            pl.BlockSpec((block, x.shape[1]), lambda i: (i, 0)),
            full(w1.shape),
            full(w2.shape),
            full(w3.shape),
        ],
        out_specs=pl.BlockSpec((block, w3.shape[1]), lambda i: (i, 0)),
    )(x, w1, w2, w3)


def encode_kernel(unroll, block, pos_ref, order_ref, x_ref, w1_ref, w2_ref, w3_ref, o_ref, rows_in, rows_out):
    def silu(v):
        return v / (1.0 + jnp.exp(-v))

    for start in range(0, x_ref.shape[0], block):
        part = pl.ds(start, block)
        h = silu(jnp.dot(x_ref[part, :], w1_ref[...], preferred_element_type=jnp.float32))
        h = h.astype(jnp.bfloat16)
        for layer_id in range(w2_ref.shape[0]):
            h = silu(jnp.dot(h, w2_ref[layer_id], preferred_element_type=jnp.float32))
            h = h.astype(jnp.bfloat16)
        features = jnp.dot(h, w3_ref[...], preferred_element_type=jnp.float32)
        rows_in[part, :] = features.astype(jnp.bfloat16).astype(jnp.float32)

    def body(step, carry):
        for lane in range(unroll):
            row = step * unroll + lane
            source = order_ref[pos_ref[row]]
            rows_out[pl.ds(row, 1), :] = rows_in[pl.ds(source, 1), :]
        return carry

    lax.fori_loop(0, o_ref.shape[0] // unroll, body, 0)
    o_ref[...] = rows_out[...].astype(o_ref.dtype)


def encode_and_gather(pos, order, x, w1, w2, w3, block):
    shape = (x.shape[0], w3.shape[1])
    return pl.pallas_call(
        functools.partial(encode_kernel, 64, block),
        out_shape=jax.ShapeDtypeStruct(shape, jnp.bfloat16),
        in_specs=[pl.BlockSpec(memory_space=pltpu.SMEM)] * 2
        + [pl.BlockSpec(memory_space=pltpu.VMEM)] * 4,
        out_specs=pl.BlockSpec(memory_space=pltpu.VMEM),
        scratch_shapes=[pltpu.VMEM(shape, jnp.float32), pltpu.VMEM(shape, jnp.float32)],
    )(pos, order, x, w1, w2, w3)


def gather_kernel(unroll, pos_ref, order_ref, x_ref, o_ref, rows_in, rows_out):
    rows_in[...] = x_ref[...].astype(jnp.float32)

    def body(step, carry):
        for lane in range(unroll):
            row = step * unroll + lane
            source = order_ref[pos_ref[row]]
            rows_out[pl.ds(row, 1), :] = rows_in[pl.ds(source, 1), :]
        return carry

    lax.fori_loop(0, o_ref.shape[0] // unroll, body, 0)
    o_ref[...] = rows_out[...].astype(o_ref.dtype)


def scatter_kernel(unroll, pos_ref, order_ref, x_ref, o_ref, rows_in, rows_out):
    rows_in[...] = x_ref[...].astype(jnp.float32)

    def body(step, carry):
        for lane in range(unroll):
            row = step * unroll + lane
            target = order_ref[pos_ref[row]]
            rows_out[pl.ds(target, 1), :] = rows_in[pl.ds(row, 1), :]
        return carry

    lax.fori_loop(0, x_ref.shape[0] // unroll, body, 0)
    o_ref[...] = rows_out[...].astype(o_ref.dtype)


def move_rows(kernel, pos, order, x):
    return pl.pallas_call(
        functools.partial(kernel, 64),
        out_shape=jax.ShapeDtypeStruct(x.shape, jnp.bfloat16),
        in_specs=[
            pl.BlockSpec(memory_space=pltpu.SMEM),
            pl.BlockSpec(memory_space=pltpu.SMEM),
            pl.BlockSpec(memory_space=pltpu.VMEM),
        ],
        out_specs=pl.BlockSpec(memory_space=pltpu.VMEM),
        scratch_shapes=[pltpu.VMEM(x.shape, jnp.float32), pltpu.VMEM(x.shape, jnp.float32)],
    )(pos, order, x)


def mix_kernel(
    count_x,
    count_y,
    rows_ref,
    column_mask_ref,
    lane_mask_ref,
    inducing_ref,
    proj_ref,
    mixing_ref,
    o_ref,
    x_ref,
    padded,
    send_sem,
    recv_sem,
    local_sem,
):
    index_x = lax.axis_index("tx")
    index_y = lax.axis_index("ty")
    size_x, size_y = x_ref.shape[0], x_ref.shape[1]
    mesh_ids = pl.DeviceIdType.MESH
    steps = [(a, b) for a in (-1, 0, 1) for b in (-1, 0, 1) if (a, b) != (0, 0)]

    def inside(px, py):
        return (px >= 0) & (px < count_x) & (py >= 0) & (py < count_y)

    def ranges(step, size):
        if step == 1:
            return pl.ds(size - 1, 1), pl.ds(0, 1)
        if step == -1:
            return pl.ds(0, 1), pl.ds(size + 1, 1)
        return pl.ds(0, size), pl.ds(1, size)

    barrier = pltpu.get_barrier_semaphore()
    for a, b in steps:
        @pl.when(inside(index_x + a, index_y + b))
        def _():
            pl.semaphore_signal(
                barrier, 1, device_id=(index_x + a, index_y + b), device_id_type=mesh_ids
            )
    def store(t, value):
        x_ref[t // size_y, t % size_y] = value

    summary_body(rows_ref, column_mask_ref, lane_mask_ref, inducing_ref, proj_ref, store)
    peers = sum(inside(index_x + a, index_y + b).astype(jnp.int32) for a, b in steps)
    pl.semaphore_wait(barrier, peers)

    center = pltpu.make_async_copy(
        x_ref, padded.at[pl.ds(1, size_x), pl.ds(1, size_y)], local_sem
    )
    center.start()
    copies = []
    for k, (a, b) in enumerate(steps):
        source_x, target_x = ranges(a, size_x)
        source_y, target_y = ranges(b, size_y)
        copy = pltpu.make_async_remote_copy(
            src_ref=x_ref.at[source_x, source_y],
            dst_ref=padded.at[target_x, target_y],
            send_sem=send_sem.at[k],
            recv_sem=recv_sem.at[k],
            device_id=(index_x + a, index_y + b),
            device_id_type=mesh_ids,
        )
        copies.append(copy)
        pl.when(inside(index_x + a, index_y + b))(copy.start)
    for k, (a, b) in enumerate(steps):
        source_x, target_x = ranges(a, size_x)
        source_y, target_y = ranges(b, size_y)

        @pl.when(jnp.logical_not(inside(index_x - a, index_y - b)))
        def _():
            piece = padded.at[target_x, target_y]
            piece[...] = jnp.zeros(piece.shape, piece.dtype)
    for k, (a, b) in enumerate(steps):
        pl.when(inside(index_x + a, index_y + b))(copies[k].wait_send)
        pl.when(inside(index_x - a, index_y - b))(copies[k].wait_recv)
    center.wait()
    for tile_x in range(size_x):
        for tile_y in range(size_y):
            total = x_ref[tile_x, tile_y].astype(jnp.float32)
            for k, (a, b) in enumerate(steps):
                total += jnp.dot(
                    padded[1 + tile_x + a, 1 + tile_y + b],
                    mixing_ref[k],
                    preferred_element_type=jnp.float32,
                )
            o_ref[tile_x, tile_y] = total.astype(o_ref.dtype)


def mix_tiles(rows, row_mask, inducing, first_proj, mixing):
    count_x = lax.axis_size("tx")
    count_y = lax.axis_size("ty")
    tiles = (TLX, TLY) + inducing.shape
    shape = (TLX + 2, TLY + 2) + inducing.shape
    return pl.pallas_call(
        functools.partial(mix_kernel, count_x, count_y),
        out_shape=jax.ShapeDtypeStruct(tiles, jnp.bfloat16),
        in_specs=[pl.BlockSpec(memory_space=pltpu.VMEM)] * 6,
        out_specs=pl.BlockSpec(memory_space=pltpu.VMEM),
        scratch_shapes=[
            pltpu.VMEM(tiles, jnp.bfloat16),
            pltpu.VMEM(shape, jnp.bfloat16),
            pltpu.SemaphoreType.DMA((8,)),
            pltpu.SemaphoreType.DMA((8,)),
            pltpu.SemaphoreType.DMA,
        ],
        compiler_params=pltpu.CompilerParams(collective_id=0, has_side_effects=True),
    )(rows, row_mask.astype(jnp.bfloat16), row_mask.T, inducing, first_proj, mixing)


def unit_heads(projected, head_count):
    pieces = projected.reshape(
        projected.shape[:-1] + (head_count, projected.shape[-1] // head_count)
    )
    magnitude = jnp.sqrt(jnp.sum(pieces * pieces, axis=-1, keepdims=True) + epsilon)
    return (pieces / magnitude).reshape(projected.shape).astype(jnp.bfloat16)


def unit_rows(projected, head_width):
    width = projected.shape[-1]
    lane_head = lax.broadcasted_iota(jnp.int32, (width, width), 0) // head_width
    column_head = lax.broadcasted_iota(jnp.int32, (width, width), 1) // head_width
    same_head = (lane_head == column_head).astype(jnp.float32)
    totals = jnp.dot(
        projected * projected,
        same_head,
        precision=lax.Precision.HIGHEST,
        preferred_element_type=jnp.float32,
    )
    return (projected / jnp.sqrt(totals + epsilon)).astype(jnp.bfloat16)


def summary_body(rows_ref, column_mask_ref, lane_mask_ref, inducing_ref, proj_ref, store):
    width = rows_ref.shape[1]
    head_width = width // HEADS
    tiles = column_mask_ref.shape[1]
    rows = rows_ref[...]
    queries = unit_rows(
        jnp.dot(inducing_ref[...], proj_ref[0], preferred_element_type=jnp.float32), head_width
    )
    keys = unit_rows(jnp.dot(rows, proj_ref[1], preferred_element_type=jnp.float32), head_width)
    values = jnp.dot(rows, proj_ref[2], preferred_element_type=jnp.float32).astype(jnp.bfloat16)
    column_mask = column_mask_ref[...]
    lane_mask = lane_mask_ref[...]
    heads_out = []
    for head_id in range(HEADS):
        lower = head_id * head_width
        upper = lower + head_width
        scores = lax.dot_general(
            queries[:, lower:upper],
            keys[:, lower:upper],
            (((1,), (1,)), ((), ())),
            preferred_element_type=jnp.float32,
        )
        weights = jnp.exp(sharpness * scores)
        rounded = weights.astype(jnp.bfloat16)
        head_values = values[:, lower:upper]
        masked = jnp.concatenate(
            [head_values * column_mask[:, t : t + 1] for t in range(tiles)], axis=1
        )
        numer = jnp.dot(rounded, masked, preferred_element_type=jnp.float32)
        per_tile = []
        for t in range(tiles):
            totals = jnp.sum(weights * lane_mask[t : t + 1, :], axis=1, keepdims=True)
            per_tile.append(numer[:, t * head_width : (t + 1) * head_width] / totals)
        heads_out.append(per_tile)
    inducing = inducing_ref[...].astype(jnp.float32)
    for t in range(tiles):
        attended = jnp.concatenate([heads_out[h][t] for h in range(HEADS)], axis=1)
        attended = attended.astype(jnp.bfloat16)
        store(
            t,
            (inducing + jnp.dot(attended, proj_ref[3], preferred_element_type=jnp.float32)).astype(
                jnp.bfloat16
            ),
        )


def body(
    points,
    embed_weight,
    inner_weights,
    output_weight,
    counts,
    point_order,
    inducing,
    first_proj,
    second_proj,
    mixing,
):
    along_x = lax.axis_size("tx")
    along_y = lax.axis_size("ty")
    devices = along_x * along_y
    index_x = lax.axis_index("tx")
    index_y = lax.axis_index("ty")
    own_index = index_x * along_y + index_y
    point_count = points.shape[0]
    per_device = TLX * TLY
    width = output_weight.shape[1]
    quota = point_count // devices
    band = quota * along_y
    head_width = width // HEADS
    inducing_count = inducing.shape[0]


    source_ids = jnp.arange(devices, dtype=jnp.int32)
    own_row = (source_ids == own_index).astype(jnp.bfloat16)[None, :]
    own_counts = jnp.dot(
        own_row, counts.astype(jnp.bfloat16), preferred_element_type=jnp.float32
    )[0].astype(jnp.int32)
    band_counts = own_counts.reshape(along_x, -1)
    band_offsets = jnp.cumsum(band_counts, axis=1) - band_counts
    grid_counts = own_counts.reshape(along_x, TLX, along_y, TLY)
    grid_offsets = band_offsets.reshape(along_x, TLX, along_y, TLY)
    band_start = (jnp.arange(along_x, dtype=jnp.int32) * band)[:, None]
    first_len = grid_counts[:, 0, :, 0] + grid_counts[:, 0, :, 1]
    first_start = grid_offsets[:, 0, :, 0]
    second_start = grid_offsets[:, 1, :, 0]
    slot_ids = jnp.arange(quota, dtype=jnp.int32)
    local_pos = jnp.where(
        slot_ids[None, None, :] < first_len[:, :, None],
        first_start[:, :, None] + slot_ids[None, None, :],
        second_start[:, :, None] + slot_ids[None, None, :] - first_len[:, :, None],
    ).reshape(along_x, band)
    send_pos = (local_pos + band_start).reshape(-1)
    order = point_order[0]
    outgoing = encode_and_gather(
        send_pos, order, points, embed_weight, inner_weights, output_weight, 2048
    )
    outgoing = outgoing.reshape(devices, quota, width)
    arrived = lax.all_to_all(outgoing, ("tx", "ty"), split_axis=0, concat_axis=0, tiled=True)
    all_rows = arrived.reshape(devices * quota, width)

    inbound = counts.reshape(devices, along_x, TLX, along_y, TLY)
    inbound = lax.dynamic_index_in_dim(inbound, index_x, 1, keepdims=False)
    inbound = lax.dynamic_index_in_dim(inbound, index_y, 2, keepdims=False)
    inbound = inbound.reshape(devices, per_device)
    through = jnp.cumsum(inbound, axis=1)
    row_tile = jnp.sum(
        (slot_ids[None, :, None] >= through[:, None, : per_device - 1]).astype(jnp.int32), axis=2
    ).reshape(-1)
    tile_ids = jnp.arange(per_device, dtype=jnp.int32)
    row_mask = (row_tile[:, None] == tile_ids[None, :]).astype(jnp.float32)

    mixture = mix_tiles(all_rows, row_mask, inducing, first_proj, mixing)
    mixture = mixture.astype(jnp.bfloat16).reshape(per_device * inducing_count, width)

    point_queries = unit_heads(
        jnp.dot(all_rows, second_proj[0], preferred_element_type=jnp.float32), HEADS
    )
    second_keys = unit_heads(
        jnp.dot(mixture, second_proj[1], preferred_element_type=jnp.float32), HEADS
    )
    second_values = jnp.dot(mixture, second_proj[2], preferred_element_type=jnp.float32).astype(
        jnp.bfloat16
    )
    key_mask = jnp.repeat(row_mask, inducing_count, axis=1)
    heads_out = []
    for head_id in range(HEADS):
        lower = head_id * head_width
        upper = lower + head_width
        scores = jnp.dot(
            point_queries[:, lower:upper],
            second_keys[:, lower:upper].T,
            preferred_element_type=jnp.float32,
        )
        weights = jnp.exp(sharpness * scores) * key_mask
        totals = jnp.sum(weights, axis=1, keepdims=True)
        numer = jnp.dot(
            weights.astype(jnp.bfloat16),
            second_values[:, lower:upper],
            preferred_element_type=jnp.float32,
        )
        heads_out.append(numer / totals)
    second_attended = jnp.concatenate(heads_out, axis=1).astype(jnp.bfloat16)
    result = (
        all_rows.astype(jnp.float32)
        + jnp.dot(second_attended, second_proj[3], preferred_element_type=jnp.float32)
    ).astype(jnp.bfloat16)

    coming = lax.all_to_all(
        result.reshape(devices, quota, width), ("tx", "ty"), split_axis=0, concat_axis=0, tiled=True
    )
    returned = move_rows(
        scatter_kernel, send_pos, order, coming.reshape(point_count, width)
    )
    return returned


def solution(mesh):
    placed = (P(("tx", "ty"), None), P(), P(), P(), P(), P(("tx", "ty"), None), P(), P(), P(), P())
    return jax.shard_map(
        body, mesh=mesh, in_specs=placed, out_specs=P(("tx", "ty"), None), check_vma=False
    )
```

```python
import functools

import jax
import jax.numpy as jnp
from jax import lax
from jax.experimental import pallas as pl
from jax.experimental.pallas import tpu as pltpu
from jax.sharding import PartitionSpec as P

HEADS = 2
TLX = 2
TLY = 2


sharpness = 32.0
epsilon = 1e-06
neighbour_steps = ((-1, -1), (-1, 0), (-1, 1), (0, -1), (0, 1), (1, -1), (1, 0), (1, 1))


def mlp_kernel(x_ref, w1_ref, w2_ref, w3_ref, o_ref):
    def silu(v):
        return v / (1.0 + jnp.exp(-v))

    h = silu(jnp.dot(x_ref[...], w1_ref[...], preferred_element_type=jnp.float32))
    h = h.astype(jnp.bfloat16)
    for layer_id in range(w2_ref.shape[0]):
        h = silu(jnp.dot(h, w2_ref[layer_id], preferred_element_type=jnp.float32))
        h = h.astype(jnp.bfloat16)
    o_ref[...] = jnp.dot(h, w3_ref[...], preferred_element_type=jnp.float32).astype(o_ref.dtype)


def point_mlp(x, w1, w2, w3, block):
    rows = x.shape[0]
    full = lambda shape: pl.BlockSpec(shape, lambda i: (0,) * len(shape))
    return pl.pallas_call(
        mlp_kernel,
        out_shape=jax.ShapeDtypeStruct((rows, w3.shape[1]), jnp.bfloat16),
        grid=(rows // block,),
        in_specs=[
            pl.BlockSpec((block, x.shape[1]), lambda i: (i, 0)),
            full(w1.shape),
            full(w2.shape),
            full(w3.shape),
        ],
        out_specs=pl.BlockSpec((block, w3.shape[1]), lambda i: (i, 0)),
    )(x, w1, w2, w3)


def encode_kernel(unroll, block, pos_ref, order_ref, x_ref, w1_ref, w2_ref, w3_ref, o_ref, rows_in, rows_out):
    def silu(v):
        return v * (0.5 + 0.5 * jnp.tanh(0.5 * v))

    for start in range(0, x_ref.shape[0], block):
        part = pl.ds(start, block)
        h = silu(jnp.dot(x_ref[part, :], w1_ref[...], preferred_element_type=jnp.float32))
        h = h.astype(jnp.bfloat16)
        for layer_id in range(w2_ref.shape[0]):
            h = silu(jnp.dot(h, w2_ref[layer_id], preferred_element_type=jnp.float32))
            h = h.astype(jnp.bfloat16)
        features = jnp.dot(h, w3_ref[...], preferred_element_type=jnp.float32)
        rows_in[part, :] = features.astype(jnp.bfloat16).astype(jnp.float32)

    def body(step, carry):
        for lane in range(unroll):
            row = step * unroll + lane
            source = order_ref[pos_ref[row]]
            rows_out[pl.ds(row, 1), :] = rows_in[pl.ds(source, 1), :]
        return carry

    lax.fori_loop(0, o_ref.shape[0] // unroll, body, 0)
    o_ref[...] = rows_out[...].astype(o_ref.dtype)


def encode_and_gather(pos, order, x, w1, w2, w3, block):
    shape = (x.shape[0], w3.shape[1])
    return pl.pallas_call(
        functools.partial(encode_kernel, 64, block),
        out_shape=jax.ShapeDtypeStruct(shape, jnp.bfloat16),
        in_specs=[pl.BlockSpec(memory_space=pltpu.SMEM)] * 2
        + [pl.BlockSpec(memory_space=pltpu.VMEM)] * 4,
        out_specs=pl.BlockSpec(memory_space=pltpu.VMEM),
        scratch_shapes=[pltpu.VMEM(shape, jnp.float32), pltpu.VMEM(shape, jnp.float32)],
    )(pos, order, x, w1, w2, w3)


def gather_kernel(unroll, pos_ref, order_ref, x_ref, o_ref, rows_in, rows_out):
    rows_in[...] = x_ref[...].astype(jnp.float32)

    def body(step, carry):
        for lane in range(unroll):
            row = step * unroll + lane
            source = order_ref[pos_ref[row]]
            rows_out[pl.ds(row, 1), :] = rows_in[pl.ds(source, 1), :]
        return carry

    lax.fori_loop(0, o_ref.shape[0] // unroll, body, 0)
    o_ref[...] = rows_out[...].astype(o_ref.dtype)


def scatter_kernel(unroll, pos_ref, order_ref, x_ref, o_ref, rows_in, rows_out):
    rows_in[...] = x_ref[...].astype(jnp.float32)

    def body(step, carry):
        for lane in range(unroll):
            row = step * unroll + lane
            target = order_ref[pos_ref[row]]
            rows_out[pl.ds(target, 1), :] = rows_in[pl.ds(row, 1), :]
        return carry

    lax.fori_loop(0, x_ref.shape[0] // unroll, body, 0)
    o_ref[...] = rows_out[...].astype(o_ref.dtype)


def move_rows(kernel, pos, order, x):
    return pl.pallas_call(
        functools.partial(kernel, 64),
        out_shape=jax.ShapeDtypeStruct(x.shape, jnp.bfloat16),
        in_specs=[
            pl.BlockSpec(memory_space=pltpu.SMEM),
            pl.BlockSpec(memory_space=pltpu.SMEM),
            pl.BlockSpec(memory_space=pltpu.VMEM),
        ],
        out_specs=pl.BlockSpec(memory_space=pltpu.VMEM),
        scratch_shapes=[pltpu.VMEM(x.shape, jnp.float32), pltpu.VMEM(x.shape, jnp.float32)],
    )(pos, order, x)


def mix_kernel(
    count_x,
    count_y,
    rows_ref,
    column_mask_ref,
    lane_mask_ref,
    inducing_ref,
    proj_ref,
    mixing_ref,
    o_ref,
    x_ref,
    padded,
    send_sem,
    recv_sem,
    local_sem,
):
    index_x = lax.axis_index("tx")
    index_y = lax.axis_index("ty")
    size_x, size_y = x_ref.shape[0], x_ref.shape[1]
    mesh_ids = pl.DeviceIdType.MESH
    steps = [(a, b) for a in (-1, 0, 1) for b in (-1, 0, 1) if (a, b) != (0, 0)]

    def inside(px, py):
        return (px >= 0) & (px < count_x) & (py >= 0) & (py < count_y)

    def ranges(step, size):
        if step == 1:
            return pl.ds(size - 1, 1), pl.ds(0, 1)
        if step == -1:
            return pl.ds(0, 1), pl.ds(size + 1, 1)
        return pl.ds(0, size), pl.ds(1, size)

    barrier = pltpu.get_barrier_semaphore()
    for a, b in steps:
        @pl.when(inside(index_x + a, index_y + b))
        def _():
            pl.semaphore_signal(
                barrier, 1, device_id=(index_x + a, index_y + b), device_id_type=mesh_ids
            )
    def store(t, value):
        x_ref[t // size_y, t % size_y] = value

    summary_body(rows_ref, column_mask_ref, lane_mask_ref, inducing_ref, proj_ref, store)
    peers = sum(inside(index_x + a, index_y + b).astype(jnp.int32) for a, b in steps)
    pl.semaphore_wait(barrier, peers)

    center = pltpu.make_async_copy(
        x_ref, padded.at[pl.ds(1, size_x), pl.ds(1, size_y)], local_sem
    )
    center.start()
    copies = []
    for k, (a, b) in enumerate(steps):
        source_x, target_x = ranges(a, size_x)
        source_y, target_y = ranges(b, size_y)
        copy = pltpu.make_async_remote_copy(
            src_ref=x_ref.at[source_x, source_y],
            dst_ref=padded.at[target_x, target_y],
            send_sem=send_sem.at[k],
            recv_sem=recv_sem.at[k],
            device_id=(index_x + a, index_y + b),
            device_id_type=mesh_ids,
        )
        copies.append(copy)
        pl.when(inside(index_x + a, index_y + b))(copy.start)
    for k, (a, b) in enumerate(steps):
        source_x, target_x = ranges(a, size_x)
        source_y, target_y = ranges(b, size_y)

        @pl.when(jnp.logical_not(inside(index_x - a, index_y - b)))
        def _():
            piece = padded.at[target_x, target_y]
            piece[...] = jnp.zeros(piece.shape, piece.dtype)
    for k, (a, b) in enumerate(steps):
        pl.when(inside(index_x + a, index_y + b))(copies[k].wait_send)
        pl.when(inside(index_x - a, index_y - b))(copies[k].wait_recv)
    center.wait()
    for tile_x in range(size_x):
        for tile_y in range(size_y):
            total = x_ref[tile_x, tile_y].astype(jnp.float32)
            for k, (a, b) in enumerate(steps):
                total += jnp.dot(
                    padded[1 + tile_x + a, 1 + tile_y + b],
                    mixing_ref[k],
                    preferred_element_type=jnp.float32,
                )
            o_ref[tile_x, tile_y] = total.astype(o_ref.dtype)


def mix_tiles(rows, row_mask, inducing, first_proj, mixing):
    count_x = lax.axis_size("tx")
    count_y = lax.axis_size("ty")
    tiles = (TLX, TLY) + inducing.shape
    shape = (TLX + 2, TLY + 2) + inducing.shape
    return pl.pallas_call(
        functools.partial(mix_kernel, count_x, count_y),
        out_shape=jax.ShapeDtypeStruct(tiles, jnp.bfloat16),
        in_specs=[pl.BlockSpec(memory_space=pltpu.VMEM)] * 6,
        out_specs=pl.BlockSpec(memory_space=pltpu.VMEM),
        scratch_shapes=[
            pltpu.VMEM(tiles, jnp.bfloat16),
            pltpu.VMEM(shape, jnp.bfloat16),
            pltpu.SemaphoreType.DMA((8,)),
            pltpu.SemaphoreType.DMA((8,)),
            pltpu.SemaphoreType.DMA,
        ],
        compiler_params=pltpu.CompilerParams(collective_id=0, has_side_effects=True),
    )(rows, row_mask.astype(jnp.bfloat16), row_mask.T, inducing, first_proj, mixing)


def unit_heads(projected, head_count):
    pieces = projected.reshape(
        projected.shape[:-1] + (head_count, projected.shape[-1] // head_count)
    )
    magnitude = jnp.sqrt(jnp.sum(pieces * pieces, axis=-1, keepdims=True) + epsilon)
    return (pieces / magnitude).reshape(projected.shape).astype(jnp.bfloat16)


def unit_rows(projected, head_width):
    width = projected.shape[-1]
    lane_head = lax.broadcasted_iota(jnp.int32, (width, width), 0) // head_width
    column_head = lax.broadcasted_iota(jnp.int32, (width, width), 1) // head_width
    same_head = (lane_head == column_head).astype(jnp.float32)
    totals = jnp.dot(
        projected * projected,
        same_head,
        precision=lax.Precision.HIGHEST,
        preferred_element_type=jnp.float32,
    )
    return (projected / jnp.sqrt(totals + epsilon)).astype(jnp.bfloat16)


def summary_body(rows_ref, column_mask_ref, lane_mask_ref, inducing_ref, proj_ref, store):
    width = rows_ref.shape[1]
    head_width = width // HEADS
    tiles = column_mask_ref.shape[1]
    rows = rows_ref[...]
    queries = unit_rows(
        jnp.dot(inducing_ref[...], proj_ref[0], preferred_element_type=jnp.float32), head_width
    )
    keys = unit_rows(jnp.dot(rows, proj_ref[1], preferred_element_type=jnp.float32), head_width)
    values = jnp.dot(rows, proj_ref[2], preferred_element_type=jnp.float32).astype(jnp.bfloat16)
    column_mask = column_mask_ref[...]
    lane_mask = lane_mask_ref[...]
    heads_out = []
    for head_id in range(HEADS):
        lower = head_id * head_width
        upper = lower + head_width
        scores = lax.dot_general(
            queries[:, lower:upper],
            keys[:, lower:upper],
            (((1,), (1,)), ((), ())),
            preferred_element_type=jnp.float32,
        )
        weights = jnp.exp(sharpness * scores)
        rounded = weights.astype(jnp.bfloat16)
        head_values = values[:, lower:upper]
        masked = jnp.concatenate(
            [head_values * column_mask[:, t : t + 1] for t in range(tiles)], axis=1
        )
        numer = jnp.dot(rounded, masked, preferred_element_type=jnp.float32)
        per_tile = []
        for t in range(tiles):
            totals = jnp.sum(weights * lane_mask[t : t + 1, :], axis=1, keepdims=True)
            per_tile.append(numer[:, t * head_width : (t + 1) * head_width] / totals)
        heads_out.append(per_tile)
    inducing = inducing_ref[...].astype(jnp.float32)
    for t in range(tiles):
        attended = jnp.concatenate([heads_out[h][t] for h in range(HEADS)], axis=1)
        attended = attended.astype(jnp.bfloat16)
        store(
            t,
            (inducing + jnp.dot(attended, proj_ref[3], preferred_element_type=jnp.float32)).astype(
                jnp.bfloat16
            ),
        )


def body(
    points,
    embed_weight,
    inner_weights,
    output_weight,
    counts,
    point_order,
    inducing,
    first_proj,
    second_proj,
    mixing,
):
    along_x = lax.axis_size("tx")
    along_y = lax.axis_size("ty")
    devices = along_x * along_y
    index_x = lax.axis_index("tx")
    index_y = lax.axis_index("ty")
    own_index = index_x * along_y + index_y
    point_count = points.shape[0]
    per_device = TLX * TLY
    width = output_weight.shape[1]
    quota = point_count // devices
    band = quota * along_y
    head_width = width // HEADS
    inducing_count = inducing.shape[0]


    source_ids = jnp.arange(devices, dtype=jnp.int32)
    own_row = (source_ids == own_index).astype(jnp.bfloat16)[None, :]
    own_counts = jnp.dot(
        own_row, counts.astype(jnp.bfloat16), preferred_element_type=jnp.float32
    )[0].astype(jnp.int32)
    band_counts = own_counts.reshape(along_x, -1)
    band_offsets = jnp.cumsum(band_counts, axis=1) - band_counts
    grid_counts = own_counts.reshape(along_x, TLX, along_y, TLY)
    grid_offsets = band_offsets.reshape(along_x, TLX, along_y, TLY)
    band_start = (jnp.arange(along_x, dtype=jnp.int32) * band)[:, None]
    first_len = grid_counts[:, 0, :, 0] + grid_counts[:, 0, :, 1]
    first_start = grid_offsets[:, 0, :, 0]
    second_start = grid_offsets[:, 1, :, 0]
    slot_ids = jnp.arange(quota, dtype=jnp.int32)
    local_pos = jnp.where(
        slot_ids[None, None, :] < first_len[:, :, None],
        first_start[:, :, None] + slot_ids[None, None, :],
        second_start[:, :, None] + slot_ids[None, None, :] - first_len[:, :, None],
    ).reshape(along_x, band)
    send_pos = (local_pos + band_start).reshape(-1)
    order = point_order[0]
    outgoing = encode_and_gather(
        send_pos, order, points, embed_weight, inner_weights, output_weight, 2048
    )
    outgoing = outgoing.reshape(devices, quota, width)
    arrived = lax.all_to_all(outgoing, ("tx", "ty"), split_axis=0, concat_axis=0, tiled=True)
    all_rows = arrived.reshape(devices * quota, width)

    inbound = counts.reshape(devices, along_x, TLX, along_y, TLY)
    inbound = lax.dynamic_index_in_dim(inbound, index_x, 1, keepdims=False)
    inbound = lax.dynamic_index_in_dim(inbound, index_y, 2, keepdims=False)
    inbound = inbound.reshape(devices, per_device)
    through = jnp.cumsum(inbound, axis=1)
    row_tile = jnp.sum(
        (slot_ids[None, :, None] >= through[:, None, : per_device - 1]).astype(jnp.int32), axis=2
    ).reshape(-1)
    tile_ids = jnp.arange(per_device, dtype=jnp.int32)
    row_mask = (row_tile[:, None] == tile_ids[None, :]).astype(jnp.float32)

    mixture = mix_tiles(all_rows, row_mask, inducing, first_proj, mixing)
    mixture = mixture.astype(jnp.bfloat16).reshape(per_device * inducing_count, width)

    point_queries = unit_heads(
        jnp.dot(all_rows, second_proj[0], preferred_element_type=jnp.float32), HEADS
    )
    second_keys = unit_heads(
        jnp.dot(mixture, second_proj[1], preferred_element_type=jnp.float32), HEADS
    )
    second_values = jnp.dot(mixture, second_proj[2], preferred_element_type=jnp.float32).astype(
        jnp.bfloat16
    )
    key_mask = jnp.repeat(row_mask, inducing_count, axis=1)
    heads_out = []
    for head_id in range(HEADS):
        lower = head_id * head_width
        upper = lower + head_width
        scores = jnp.dot(
            point_queries[:, lower:upper],
            second_keys[:, lower:upper].T,
            preferred_element_type=jnp.float32,
        )
        weights = jnp.exp(sharpness * scores) * key_mask
        totals = jnp.sum(weights, axis=1, keepdims=True)
        numer = jnp.dot(
            weights.astype(jnp.bfloat16),
            second_values[:, lower:upper],
            preferred_element_type=jnp.float32,
        )
        heads_out.append(numer / totals)
    second_attended = jnp.concatenate(heads_out, axis=1).astype(jnp.bfloat16)
    result = (
        all_rows.astype(jnp.float32)
        + jnp.dot(second_attended, second_proj[3], preferred_element_type=jnp.float32)
    ).astype(jnp.bfloat16)

    coming = lax.all_to_all(
        result.reshape(devices, quota, width), ("tx", "ty"), split_axis=0, concat_axis=0, tiled=True
    )
    returned = move_rows(
        scatter_kernel, send_pos, order, coming.reshape(point_count, width)
    )
    return returned


def solution(mesh):
    placed = (P(("tx", "ty"), None), P(), P(), P(), P(), P(("tx", "ty"), None), P(), P(), P(), P())
    return jax.shard_map(
        body, mesh=mesh, in_specs=placed, out_specs=P(("tx", "ty"), None), check_vma=False
    )
```

```python
import functools

import jax
import jax.numpy as jnp
from jax import lax
from jax.experimental import pallas as pl
from jax.experimental.pallas import tpu as pltpu
from jax.sharding import PartitionSpec as P

HEADS = 2
TLX = 2
TLY = 2


sharpness = 32.0
epsilon = 1e-06
neighbour_steps = ((-1, -1), (-1, 0), (-1, 1), (0, -1), (0, 1), (1, -1), (1, 0), (1, 1))


def mlp_kernel(x_ref, w1_ref, w2_ref, w3_ref, o_ref):
    def silu(v):
        return v / (1.0 + jnp.exp(-v))

    h = silu(jnp.dot(x_ref[...], w1_ref[...], preferred_element_type=jnp.float32))
    h = h.astype(jnp.bfloat16)
    for layer_id in range(w2_ref.shape[0]):
        h = silu(jnp.dot(h, w2_ref[layer_id], preferred_element_type=jnp.float32))
        h = h.astype(jnp.bfloat16)
    o_ref[...] = jnp.dot(h, w3_ref[...], preferred_element_type=jnp.float32).astype(o_ref.dtype)


def point_mlp(x, w1, w2, w3, block):
    rows = x.shape[0]
    full = lambda shape: pl.BlockSpec(shape, lambda i: (0,) * len(shape))
    return pl.pallas_call(
        mlp_kernel,
        out_shape=jax.ShapeDtypeStruct((rows, w3.shape[1]), jnp.bfloat16),
        grid=(rows // block,),
        in_specs=[
            pl.BlockSpec((block, x.shape[1]), lambda i: (i, 0)),
            full(w1.shape),
            full(w2.shape),
            full(w3.shape),
        ],
        out_specs=pl.BlockSpec((block, w3.shape[1]), lambda i: (i, 0)),
    )(x, w1, w2, w3)


def encode_kernel(
    unroll, block, pos_ref, order_ref, x_ref, w1_ref, w2_ref, w3_ref, o_ref, index_ref, rows_in, rows_out
):
    def silu(v):
        return v / (1.0 + jnp.exp(-v))

    for start in range(0, x_ref.shape[0], block):
        part = pl.ds(start, block)
        h = silu(jnp.dot(x_ref[part, :], w1_ref[...], preferred_element_type=jnp.float32))
        h = h.astype(jnp.bfloat16)
        for layer_id in range(w2_ref.shape[0]):
            h = silu(jnp.dot(h, w2_ref[layer_id], preferred_element_type=jnp.float32))
            h = h.astype(jnp.bfloat16)
        features = jnp.dot(h, w3_ref[...], preferred_element_type=jnp.float32)
        rows_in[part, :] = features.astype(jnp.bfloat16).astype(jnp.float32)

    def body(step, carry):
        for lane in range(unroll):
            row = step * unroll + lane
            source = order_ref[pos_ref[row]]
            index_ref[row] = source
            rows_out[pl.ds(row, 1), :] = rows_in[pl.ds(source, 1), :]
        return carry

    lax.fori_loop(0, o_ref.shape[0] // unroll, body, 0)
    o_ref[...] = rows_out[...].astype(o_ref.dtype)


def encode_and_gather(pos, order, x, w1, w2, w3, block):
    shape = (x.shape[0], w3.shape[1])
    return pl.pallas_call(
        functools.partial(encode_kernel, 64, block),
        out_shape=(
            jax.ShapeDtypeStruct(shape, jnp.bfloat16),
            jax.ShapeDtypeStruct(pos.shape, jnp.int32),
        ),
        in_specs=[pl.BlockSpec(memory_space=pltpu.SMEM)] * 2
        + [pl.BlockSpec(memory_space=pltpu.VMEM)] * 4,
        out_specs=[pl.BlockSpec(memory_space=pltpu.VMEM), pl.BlockSpec(memory_space=pltpu.SMEM)],
        scratch_shapes=[pltpu.VMEM(shape, jnp.float32), pltpu.VMEM(shape, jnp.float32)],
    )(pos, order, x, w1, w2, w3)


def gather_kernel(unroll, pos_ref, order_ref, x_ref, o_ref, rows_in, rows_out):
    rows_in[...] = x_ref[...].astype(jnp.float32)

    def body(step, carry):
        for lane in range(unroll):
            row = step * unroll + lane
            source = order_ref[pos_ref[row]]
            rows_out[pl.ds(row, 1), :] = rows_in[pl.ds(source, 1), :]
        return carry

    lax.fori_loop(0, o_ref.shape[0] // unroll, body, 0)
    o_ref[...] = rows_out[...].astype(o_ref.dtype)


def scatter_kernel(unroll, index_ref, x_ref, o_ref, rows_in, rows_out):
    rows_in[...] = x_ref[...].astype(jnp.float32)

    def body(step, carry):
        for lane in range(unroll):
            row = step * unroll + lane
            target = index_ref[row]
            rows_out[pl.ds(target, 1), :] = rows_in[pl.ds(row, 1), :]
        return carry

    lax.fori_loop(0, x_ref.shape[0] // unroll, body, 0)
    o_ref[...] = rows_out[...].astype(o_ref.dtype)


def place_rows(index, x):
    return pl.pallas_call(
        functools.partial(scatter_kernel, 64),
        out_shape=jax.ShapeDtypeStruct(x.shape, jnp.bfloat16),
        in_specs=[pl.BlockSpec(memory_space=pltpu.SMEM), pl.BlockSpec(memory_space=pltpu.VMEM)],
        out_specs=pl.BlockSpec(memory_space=pltpu.VMEM),
        scratch_shapes=[pltpu.VMEM(x.shape, jnp.float32), pltpu.VMEM(x.shape, jnp.float32)],
    )(index, x)


def move_rows(kernel, pos, order, x):
    return pl.pallas_call(
        functools.partial(kernel, 64),
        out_shape=jax.ShapeDtypeStruct(x.shape, jnp.bfloat16),
        in_specs=[
            pl.BlockSpec(memory_space=pltpu.SMEM),
            pl.BlockSpec(memory_space=pltpu.SMEM),
            pl.BlockSpec(memory_space=pltpu.VMEM),
        ],
        out_specs=pl.BlockSpec(memory_space=pltpu.VMEM),
        scratch_shapes=[pltpu.VMEM(x.shape, jnp.float32), pltpu.VMEM(x.shape, jnp.float32)],
    )(pos, order, x)


def mix_kernel(
    count_x,
    count_y,
    rows_ref,
    column_mask_ref,
    lane_mask_ref,
    inducing_ref,
    proj_ref,
    mixing_ref,
    o_ref,
    x_ref,
    padded,
    send_sem,
    recv_sem,
    local_sem,
):
    index_x = lax.axis_index("tx")
    index_y = lax.axis_index("ty")
    size_x, size_y = x_ref.shape[0], x_ref.shape[1]
    mesh_ids = pl.DeviceIdType.MESH
    steps = [(a, b) for a in (-1, 0, 1) for b in (-1, 0, 1) if (a, b) != (0, 0)]

    def inside(px, py):
        return (px >= 0) & (px < count_x) & (py >= 0) & (py < count_y)

    def ranges(step, size):
        if step == 1:
            return pl.ds(size - 1, 1), pl.ds(0, 1)
        if step == -1:
            return pl.ds(0, 1), pl.ds(size + 1, 1)
        return pl.ds(0, size), pl.ds(1, size)

    barrier = pltpu.get_barrier_semaphore()
    for a, b in steps:
        @pl.when(inside(index_x + a, index_y + b))
        def _():
            pl.semaphore_signal(
                barrier, 1, device_id=(index_x + a, index_y + b), device_id_type=mesh_ids
            )
    def store(t, value):
        x_ref[t // size_y, t % size_y] = value

    summary_body(rows_ref, column_mask_ref, lane_mask_ref, inducing_ref, proj_ref, store)
    peers = sum(inside(index_x + a, index_y + b).astype(jnp.int32) for a, b in steps)
    pl.semaphore_wait(barrier, peers)

    center = pltpu.make_async_copy(
        x_ref, padded.at[pl.ds(1, size_x), pl.ds(1, size_y)], local_sem
    )
    center.start()
    copies = []
    for k, (a, b) in enumerate(steps):
        source_x, target_x = ranges(a, size_x)
        source_y, target_y = ranges(b, size_y)
        copy = pltpu.make_async_remote_copy(
            src_ref=x_ref.at[source_x, source_y],
            dst_ref=padded.at[target_x, target_y],
            send_sem=send_sem.at[k],
            recv_sem=recv_sem.at[k],
            device_id=(index_x + a, index_y + b),
            device_id_type=mesh_ids,
        )
        copies.append(copy)
        pl.when(inside(index_x + a, index_y + b))(copy.start)
    for k, (a, b) in enumerate(steps):
        source_x, target_x = ranges(a, size_x)
        source_y, target_y = ranges(b, size_y)

        @pl.when(jnp.logical_not(inside(index_x - a, index_y - b)))
        def _():
            piece = padded.at[target_x, target_y]
            piece[...] = jnp.zeros(piece.shape, piece.dtype)
    for k, (a, b) in enumerate(steps):
        pl.when(inside(index_x + a, index_y + b))(copies[k].wait_send)
        pl.when(inside(index_x - a, index_y - b))(copies[k].wait_recv)
    center.wait()
    for tile_x in range(size_x):
        for tile_y in range(size_y):
            total = x_ref[tile_x, tile_y].astype(jnp.float32)
            for k, (a, b) in enumerate(steps):
                total += jnp.dot(
                    padded[1 + tile_x + a, 1 + tile_y + b],
                    mixing_ref[k],
                    preferred_element_type=jnp.float32,
                )
            o_ref[tile_x, tile_y] = total.astype(o_ref.dtype)


def mix_tiles(rows, row_mask, inducing, first_proj, mixing):
    count_x = lax.axis_size("tx")
    count_y = lax.axis_size("ty")
    tiles = (TLX, TLY) + inducing.shape
    shape = (TLX + 2, TLY + 2) + inducing.shape
    return pl.pallas_call(
        functools.partial(mix_kernel, count_x, count_y),
        out_shape=jax.ShapeDtypeStruct(tiles, jnp.bfloat16),
        in_specs=[pl.BlockSpec(memory_space=pltpu.VMEM)] * 6,
        out_specs=pl.BlockSpec(memory_space=pltpu.VMEM),
        scratch_shapes=[
            pltpu.VMEM(tiles, jnp.bfloat16),
            pltpu.VMEM(shape, jnp.bfloat16),
            pltpu.SemaphoreType.DMA((8,)),
            pltpu.SemaphoreType.DMA((8,)),
            pltpu.SemaphoreType.DMA,
        ],
        compiler_params=pltpu.CompilerParams(collective_id=0, has_side_effects=True),
    )(rows, row_mask.astype(jnp.bfloat16), row_mask.T, inducing, first_proj, mixing)


def unit_heads(projected, head_count):
    pieces = projected.reshape(
        projected.shape[:-1] + (head_count, projected.shape[-1] // head_count)
    )
    magnitude = jnp.sqrt(jnp.sum(pieces * pieces, axis=-1, keepdims=True) + epsilon)
    return (pieces / magnitude).reshape(projected.shape).astype(jnp.bfloat16)


def unit_rows(projected, head_width):
    width = projected.shape[-1]
    lane_head = lax.broadcasted_iota(jnp.int32, (width, width), 0) // head_width
    column_head = lax.broadcasted_iota(jnp.int32, (width, width), 1) // head_width
    same_head = (lane_head == column_head).astype(jnp.float32)
    totals = jnp.dot(
        projected * projected,
        same_head,
        precision=lax.Precision.HIGHEST,
        preferred_element_type=jnp.float32,
    )
    return (projected / jnp.sqrt(totals + epsilon)).astype(jnp.bfloat16)


def summary_body(rows_ref, column_mask_ref, lane_mask_ref, inducing_ref, proj_ref, store):
    width = rows_ref.shape[1]
    head_width = width // HEADS
    tiles = column_mask_ref.shape[1]
    rows = rows_ref[...]
    queries = unit_rows(
        jnp.dot(inducing_ref[...], proj_ref[0], preferred_element_type=jnp.float32), head_width
    )
    keys = unit_rows(jnp.dot(rows, proj_ref[1], preferred_element_type=jnp.float32), head_width)
    values = jnp.dot(rows, proj_ref[2], preferred_element_type=jnp.float32).astype(jnp.bfloat16)
    column_mask = column_mask_ref[...]
    lane_mask = lane_mask_ref[...]
    heads_out = []
    for head_id in range(HEADS):
        lower = head_id * head_width
        upper = lower + head_width
        scores = lax.dot_general(
            queries[:, lower:upper],
            keys[:, lower:upper],
            (((1,), (1,)), ((), ())),
            preferred_element_type=jnp.float32,
        )
        weights = jnp.exp(sharpness * scores)
        rounded = weights.astype(jnp.bfloat16)
        head_values = values[:, lower:upper]
        masked = jnp.concatenate(
            [head_values * column_mask[:, t : t + 1] for t in range(tiles)], axis=1
        )
        numer = jnp.dot(rounded, masked, preferred_element_type=jnp.float32)
        per_tile = []
        for t in range(tiles):
            totals = jnp.sum(weights * lane_mask[t : t + 1, :], axis=1, keepdims=True)
            per_tile.append(numer[:, t * head_width : (t + 1) * head_width] / totals)
        heads_out.append(per_tile)
    inducing = inducing_ref[...].astype(jnp.float32)
    for t in range(tiles):
        attended = jnp.concatenate([heads_out[h][t] for h in range(HEADS)], axis=1)
        attended = attended.astype(jnp.bfloat16)
        store(
            t,
            (inducing + jnp.dot(attended, proj_ref[3], preferred_element_type=jnp.float32)).astype(
                jnp.bfloat16
            ),
        )


def body(
    points,
    embed_weight,
    inner_weights,
    output_weight,
    counts,
    point_order,
    inducing,
    first_proj,
    second_proj,
    mixing,
):
    along_x = lax.axis_size("tx")
    along_y = lax.axis_size("ty")
    devices = along_x * along_y
    index_x = lax.axis_index("tx")
    index_y = lax.axis_index("ty")
    own_index = index_x * along_y + index_y
    point_count = points.shape[0]
    per_device = TLX * TLY
    width = output_weight.shape[1]
    quota = point_count // devices
    band = quota * along_y
    head_width = width // HEADS
    inducing_count = inducing.shape[0]


    source_ids = jnp.arange(devices, dtype=jnp.int32)
    own_row = (source_ids == own_index).astype(jnp.bfloat16)[None, :]
    own_counts = jnp.dot(
        own_row, counts.astype(jnp.bfloat16), preferred_element_type=jnp.float32
    )[0].astype(jnp.int32)
    band_counts = own_counts.reshape(along_x, -1)
    band_offsets = jnp.cumsum(band_counts, axis=1) - band_counts
    grid_counts = own_counts.reshape(along_x, TLX, along_y, TLY)
    grid_offsets = band_offsets.reshape(along_x, TLX, along_y, TLY)
    band_start = (jnp.arange(along_x, dtype=jnp.int32) * band)[:, None]
    first_len = grid_counts[:, 0, :, 0] + grid_counts[:, 0, :, 1]
    first_start = grid_offsets[:, 0, :, 0]
    second_start = grid_offsets[:, 1, :, 0]
    slot_ids = jnp.arange(quota, dtype=jnp.int32)
    local_pos = jnp.where(
        slot_ids[None, None, :] < first_len[:, :, None],
        first_start[:, :, None] + slot_ids[None, None, :],
        second_start[:, :, None] + slot_ids[None, None, :] - first_len[:, :, None],
    ).reshape(along_x, band)
    send_pos = (local_pos + band_start).reshape(-1)
    order = point_order[0]
    outgoing, send_index = encode_and_gather(
        send_pos, order, points, embed_weight, inner_weights, output_weight, 2048
    )
    outgoing = outgoing.reshape(devices, quota, width)
    arrived = lax.all_to_all(outgoing, ("tx", "ty"), split_axis=0, concat_axis=0, tiled=True)
    all_rows = arrived.reshape(devices * quota, width)

    inbound = counts.reshape(devices, along_x, TLX, along_y, TLY)
    inbound = lax.dynamic_index_in_dim(inbound, index_x, 1, keepdims=False)
    inbound = lax.dynamic_index_in_dim(inbound, index_y, 2, keepdims=False)
    inbound = inbound.reshape(devices, per_device)
    through = jnp.cumsum(inbound, axis=1)
    row_tile = jnp.sum(
        (slot_ids[None, :, None] >= through[:, None, : per_device - 1]).astype(jnp.int32), axis=2
    ).reshape(-1)
    tile_ids = jnp.arange(per_device, dtype=jnp.int32)
    row_mask = (row_tile[:, None] == tile_ids[None, :]).astype(jnp.float32)

    mixture = mix_tiles(all_rows, row_mask, inducing, first_proj, mixing)
    mixture = mixture.astype(jnp.bfloat16).reshape(per_device * inducing_count, width)

    point_queries = unit_heads(
        jnp.dot(all_rows, second_proj[0], preferred_element_type=jnp.float32), HEADS
    )
    second_keys = unit_heads(
        jnp.dot(mixture, second_proj[1], preferred_element_type=jnp.float32), HEADS
    )
    second_values = jnp.dot(mixture, second_proj[2], preferred_element_type=jnp.float32).astype(
        jnp.bfloat16
    )
    key_mask = jnp.repeat(row_mask, inducing_count, axis=1)
    heads_out = []
    for head_id in range(HEADS):
        lower = head_id * head_width
        upper = lower + head_width
        scores = jnp.dot(
            point_queries[:, lower:upper],
            second_keys[:, lower:upper].T,
            preferred_element_type=jnp.float32,
        )
        weights = jnp.exp(sharpness * scores) * key_mask
        totals = jnp.sum(weights, axis=1, keepdims=True)
        numer = jnp.dot(
            weights.astype(jnp.bfloat16),
            second_values[:, lower:upper],
            preferred_element_type=jnp.float32,
        )
        heads_out.append(numer / totals)
    second_attended = jnp.concatenate(heads_out, axis=1).astype(jnp.bfloat16)
    result = (
        all_rows.astype(jnp.float32)
        + jnp.dot(second_attended, second_proj[3], preferred_element_type=jnp.float32)
    ).astype(jnp.bfloat16)

    coming = lax.all_to_all(
        result.reshape(devices, quota, width), ("tx", "ty"), split_axis=0, concat_axis=0, tiled=True
    )
    returned = place_rows(send_index, coming.reshape(point_count, width))
    return returned


def solution(mesh):
    placed = (P(("tx", "ty"), None), P(), P(), P(), P(), P(("tx", "ty"), None), P(), P(), P(), P())
    return jax.shard_map(
        body, mesh=mesh, in_specs=placed, out_specs=P(("tx", "ty"), None), check_vma=False
    )
```
